32 devices in a mesh: grp: 4 (over x, core), gx: 2 (over y), gy: 4 (over z).
Axes of the slice: x: 2, y: 2, z: 4, core: 2. Of those that a mesh axis runs over, the one named last changes fastest.
Arguments:
- sources: float32 [4, 8, 32, 512], P('grp', 'gx', 'gy'), may hold values from -4.5 to 5.5
- diagonal: float32 [8, 32, 512], P('gx', 'gy'), may hold values from 0.02 to 0.3
- coarse_ids: int32 [8, 32, 512], P('gx', 'gy'), may hold values from 0 to 255, as said below
- coarse_inverse: float32 [256, 256], replicated, may hold values from -1 to 3
- omega_rows: float32 [4, 32], replicated, may hold values from -5 to 5
- psi: float32 [32, 8, 32, 512], P(None, 'gx', 'gy', 'grp'), may hold values from -0.015625 to 0.015625
- phi: float32 [64, 8, 32, 512], P(None, 'gx', 'gy', 'grp'), may hold values from -0.015625 to 0.015625
- xi_cols: float32 [64, 4], replicated, may hold values from -5 to 5
- range_sketch: float32 [32, 8, 32, 512], P(None, 'gx', 'gy', 'grp'), may hold values from -3 to 3
- core_sketch: float32 [64, 64], replicated, may hold values from -2 to 2
Outputs:
- range_new: float32 [32, 8, 32, 512], P(None, 'gx', 'gy', 'grp')
- corange_cols: float32 [32, 4], replicated
- core_new: float32 [64, 64], replicated
The draws below stay inside these ranges and needn't reach their ends.
Inputs may be any that keep to these rules, and one draw needn't show every extreme that they name: `coarse_ids`: the grid is cut into 4, 4 and 16 non-empty ranges of consecutive cells along the three dimensions; coarse cell (a * 4 + b) * 16 + c is the box of ranges a, b, c.
All inputs are finite; a program needn't handle non-finite values.
Results may differ from the reference program's by a relative error of at most 0.0003.
Values sent between devices are 32-bit elements; how exact they have to be, the bound alone decides.
No kernel may reach another device: no remote copies, remote signals or barrier semaphores. Data moves between devices by JAX's collectives and lax.ppermute only.
A program may use at most 64 MiB of HBM per device.

```python
import math
import jax
import jax.numpy as jnp
from jax import lax

NZ = 512
OUTER = 2
SWEEPS = 4
XY_CUTS = 4
Z_CUTS = 16
RANGE = 32
CORANGE = 32
CORE = 64
SNAPS = 4
NX = 8
NY = 32
COARSE = 256


def cut_ranks(key, length, pieces):
    chosen = jax.random.permutation(key, length - 1)[:pieces - 1] + 1
    bounds = jnp.sort(chosen)
    places = jnp.arange(length, dtype=jnp.int32)
    return jnp.sum((places[:, None] >= bounds[None, :]).astype(jnp.int32), axis=1)


def draw_coarse_ids(key, part):
    key_first = jax.random.fold_in(key, 11)
    key_second = jax.random.fold_in(key, 12)
    key_third = jax.random.fold_in(key, 13)
    ranks_x = cut_ranks(key_first, NX, XY_CUTS)
    ranks_y = cut_ranks(key_second, NY, XY_CUTS)
    ranks_z = cut_ranks(key_third, NZ, Z_CUTS)
    combined = (ranks_x[:, None, None] * XY_CUTS + ranks_y[None, :, None]) * Z_CUTS + ranks_z[None, None, :]
    return combined.astype(jnp.int32)


def draw_coarse_inverse(key, part):
    key_diag = jax.random.fold_in(key, 21)
    key_off = jax.random.fold_in(key, 22)
    diag_part = jnp.exp(jax.random.uniform(key_diag, (COARSE,), jnp.float32, math.log(0.5), math.log(2.0)))
    off_part = jax.random.truncated_normal(key_off, -4.0, 4.0, (COARSE, COARSE), jnp.float32) * (0.5 / math.sqrt(COARSE))
    return off_part + jnp.diag(diag_part)


def draw_sources(key, part):
    extent = (SNAPS, NX, NY, NZ)
    return jax.random.truncated_normal(key, -5.0, 5.0, extent, jnp.float32) + 0.5


def steps_of(own_key, shape, cuts, smallest, largest):
    factor_of, own = 1.0, jax.random.fold_in(own_key, 6)
    for axis_at, blocks in cuts:
        heights = jnp.exp(jax.random.uniform(jax.random.fold_in(own, axis_at), (blocks,), jnp.float32, smallest / len(cuts), largest / len(cuts)))
        factor_of = factor_of * jnp.repeat(heights, shape[axis_at] // blocks).reshape([-1 if axis == axis_at else 1 for axis in range(len(shape))])
    return factor_of


def gaussian(key, shape, width, most, shards=(), kind=jnp.bfloat16):
    loudness = steps_of(key, shape, shards, -0.22, 0.18) if shards else 1.0
    entries = jax.random.normal(key, shape, jnp.float32) * width * loudness
    return jnp.minimum(jnp.maximum(entries, -most), most).astype(kind)


def setup_inputs(seed: int = 0) -> dict:
    seeds = jax.random.split(jax.random.key(seed), 11)
    sources = draw_sources(jax.random.fold_in(seeds[10], 71), 0)
    diagonal = jnp.clip(jnp.exp(math.log(0.3) - 2.7080503 * jax.random.uniform(seeds[1], (NX, NY, NZ), jnp.float32) ** steps_of(seeds[1], (NX, NY, NZ), ((0, 2), (1, 4)), -0.2, 0.2)), 0.02, 0.3)
    coarse_ids = draw_coarse_ids(jax.random.fold_in(seeds[10], 71), 0)
    coarse_inverse = draw_coarse_inverse(jax.random.fold_in(seeds[10], 71), 0)
    omega_rows = gaussian(seeds[4], (SNAPS, RANGE), 1.0, 5.0, (), jnp.float32)
    psi = gaussian(seeds[5], (CORANGE, NX, NY, NZ), (NX * NY * NZ) ** -0.5, 0.015625, ((1, 2), (2, 4), (3, 4)), jnp.float32)
    phi = gaussian(seeds[6], (CORE, NX, NY, NZ), (NX * NY * NZ) ** -0.5, 0.015625, ((1, 2), (2, 4), (3, 4)), jnp.float32)
    xi_cols = gaussian(seeds[7], (CORE, SNAPS), 1.0, 5.0, (), jnp.float32)
    range_sketch = gaussian(seeds[8], (RANGE, NX, NY, NZ), 0.5, 3.0, ((1, 2), (2, 4), (3, 4)), jnp.float32)
    core_sketch = gaussian(seeds[9], (CORE, CORE), 0.3, 2.0, (), jnp.float32)
    return dict(sources=sources, diagonal=diagonal, coarse_ids=coarse_ids, coarse_inverse=coarse_inverse, omega_rows=omega_rows, psi=psi, phi=phi, xi_cols=xi_cols, range_sketch=range_sketch, core_sketch=core_sketch)


jacobi_weight = 2.0 / 3.0


def apply_operator(values, diagonal):
    padded = jnp.pad(values, 1)
    beside = padded[2:, 1:-1, 1:-1] + padded[:-2, 1:-1, 1:-1]
    beside = beside + padded[1:-1, 2:, 1:-1] + padded[1:-1, :-2, 1:-1]
    beside = beside + padded[1:-1, 1:-1, 2:] + padded[1:-1, 1:-1, :-2]
    return (6.0 + diagonal) * values - beside


def solve_snapshot(source, diagonal, coarse_ids, coarse_inverse):
    cell_count = NX * NY * NZ
    pressure = jnp.zeros_like(source)
    flat_ids = coarse_ids.reshape(-1).astype(jnp.int32)
    for outer_step in range(OUTER):
        residual = source - apply_operator(pressure, diagonal)
        coarse_rhs = jax.ops.segment_sum(residual.reshape(-1), flat_ids, num_segments=COARSE)
        correction = jnp.dot(coarse_inverse, coarse_rhs * (COARSE / cell_count), precision=lax.Precision.HIGHEST)
        pressure = pressure + correction[coarse_ids]
        for sweep_step in range(SWEEPS):
            pressure = pressure + jacobi_weight * (source - apply_operator(pressure, diagonal)) / (6.0 + diagonal)
    return pressure


def reference(sources, diagonal, coarse_ids, coarse_inverse, omega_rows, psi, phi, xi_cols, range_sketch, core_sketch):
    snapshots = jnp.stack([solve_snapshot(sources[index], diagonal, coarse_ids, coarse_inverse) for index in range(SNAPS)])
    range_new = range_sketch + jnp.einsum("tk,txyz->kxyz", omega_rows, snapshots, precision=lax.Precision.HIGHEST)
    corange_cols = jnp.einsum("lxyz,txyz->lt", psi, snapshots, precision=lax.Precision.HIGHEST)
    core_images = jnp.einsum("sxyz,txyz->st", phi, snapshots, precision=lax.Precision.HIGHEST)
    core_new = core_sketch + jnp.dot(core_images, xi_cols.T, precision=lax.Precision.HIGHEST)
    return range_new, corange_cols, core_new
```

```python
import functools

import jax
import jax.numpy as jnp
from jax import lax
from jax.experimental import pallas as pl
from jax.experimental.pallas import tpu as pltpu
from jax.sharding import PartitionSpec as P

OUTER = 2
SWEEPS = 4
XY_CUTS = 4
Z_CUTS = 16
LANES = 128
SUBLANES = 8

jacobi_weight = 2.0 / 3.0
highest = lax.Precision.HIGHEST


def dot_nn(a, b):
    return lax.dot_general(
        a, b, (((1,), (0,)), ((), ())), precision=highest, preferred_element_type=jnp.float32
    )


def dot_nt(a, b):
    return lax.dot_general(
        a, b, (((1,), (1,)), ((), ())), precision=highest, preferred_element_type=jnp.float32
    )


def iota(shape, dim):
    return lax.broadcasted_iota(jnp.int32, shape, dim)


def spread_map(ids_ref, coarse):
    cells_z = ids_ref.shape[2]
    ranks = lax.bitwise_and(ids_ref[0, 0:1, :], Z_CUTS - 1)
    rows = lax.bitwise_and(iota((coarse, cells_z), 0), Z_CUTS - 1)
    return (rows == ranks).astype(jnp.float32)


def column_map(ids_ref):
    rows_x, rows_y, _ = ids_ref.shape
    boxes = XY_CUTS * XY_CUTS
    tile = ids_ref[:, :, :LANES].reshape(rows_x * rows_y, LANES) // Z_CUTS
    turned = tile.astype(jnp.float32).T[:boxes]
    return (turned == iota(turned.shape, 0).astype(jnp.float32)).astype(jnp.float32)


def restrict(values, ids_ref, coarse):
    boxes = XY_CUTS * XY_CUTS
    by_box = dot_nn(column_map(ids_ref), values)
    wide = dot_nt(by_box, spread_map(ids_ref, coarse))
    own = iota((boxes, coarse), 1) // Z_CUTS == iota((boxes, coarse), 0)
    return jnp.sum(jnp.where(own, wide, 0.0), axis=0, keepdims=True)


def store_row(out_ref, row):
    for part in range(row.shape[1] // LANES):
        out_ref[part : part + 1, :] = row[:, part * LANES : (part + 1) * LANES]


def begin_kernel(coarse, source_ref, ids_ref, out_ref):
    rows_x, rows_y, cells_z = source_ref.shape
    row = restrict(source_ref[...].reshape(rows_x * rows_y, cells_z), ids_ref, coarse)
    store_row(out_ref, row)
    lanes = iota((1, LANES), 1)
    tile = ids_ref[:, :, :LANES] // Z_CUTS
    ranks_x = tile[:, 0:1, :] // XY_CUTS
    ranks_y = lax.bitwise_and(tile[0], XY_CUTS - 1)
    below_x = jnp.sum((ranks_x <= lanes[None]).astype(jnp.float32), axis=0)
    below_y = jnp.sum((ranks_y <= lanes - XY_CUTS).astype(jnp.float32), axis=0, keepdims=True)
    last = coarse // LANES
    out_ref[last : last + 1, :] = jnp.where(lanes < XY_CUTS, below_x, below_y)


def coarse_planes(gathered, inverse_ref, ids_ref, scale_factor, cuts, place):
    coarse = inverse_ref.shape[0]
    boxes = XY_CUTS * XY_CUTS
    _, cut_y = cuts
    row = jnp.concatenate(
        [gathered[part : part + 1, :] for part in range(coarse // LANES)], axis=1
    )
    row = jnp.broadcast_to(row * scale_factor, (SUBLANES, coarse))
    solved = dot_nt(row, inverse_ref[...])[0:1]
    own = iota((boxes, coarse), 1) // Z_CUTS == iota((boxes, coarse), 0)
    along_z = dot_nn(jnp.where(own, solved, 0.0), spread_map(ids_ref, coarse))
    place_y, inside = place
    planes = []
    for box_x in range(XY_CUTS):
        first = box_x * XY_CUTS
        plane = jnp.broadcast_to(along_z[first : first + 1], place_y.shape)
        for box_y in range(1, XY_CUTS):
            line = along_z[first + box_y : first + box_y + 1]
            plane = jnp.where(place_y >= cut_y[box_y - 1], line, plane)
        planes.append(jnp.where(inside, plane, 0.0))
    return planes


def correction_of(planes, cuts, place_x):
    cut_x, _ = cuts
    value = planes[0]
    for box_x in range(1, XY_CUTS):
        value = jnp.where(cut_x[box_x - 1] <= place_x, planes[box_x], value)
    return value


def cuts_of(row, count_x, count_y):
    cut_x = [row[:, at : at + 1] * (1.0 / count_y) for at in range(XY_CUTS - 1)]
    cut_y = [row[:, XY_CUTS + at : XY_CUTS + at + 1] * (1.0 / count_x) for at in range(XY_CUTS - 1)]
    return cut_x, cut_y


def beside_z(values):
    cells_z = values.shape[-1]
    lanes = iota(values.shape, values.ndim - 1)
    ahead = pltpu.roll(values, cells_z - 1, values.ndim - 1)
    behind = pltpu.roll(values, 1, values.ndim - 1)
    return jnp.where(lanes == cells_z - 1, 0.0, ahead) + jnp.where(lanes == 0, 0.0, behind)


def beside_y(values):
    rows = values.shape[0]
    return pltpu.roll(values, rows - 1, 0) + pltpu.roll(values, 1, 0)


def neighbours(field_ref, at):
    center = field_ref[at + 1]
    return center, field_ref[at] + field_ref[at + 2] + beside_y(center) + beside_z(center)


def sweep(from_ref, to_ref, weight_ref, drive_ref):
    for at in range(weight_ref.shape[0]):
        center, beside = neighbours(from_ref, at)
        to_ref[at + 1] = (
            center * (1.0 - jacobi_weight) + drive_ref[at] + weight_ref[at] * beside
        )


def window_place(count_y, rows_y, shape):
    place_y = iota(shape, 0) + (lax.axis_index("gy") - 1) * rows_y
    inside = (place_y >= 0) & (place_y < rows_y * count_y)
    return place_y.astype(jnp.float32), inside


def first_kernel(
    counts, scale_factor, own_ref, other_ref, even_ref, even_other_ref, odd_ref, odd_other_ref,
    ids_ref, inverse_ref, gathered_ref,
    field_ref, weight_ref, drive_ref, out_ref, spare_ref,
):
    count_x, count_y = counts
    _, rows_x, rows_y, cells_z = own_ref.shape
    window_x, window_y, _ = weight_ref.shape
    at_x, at_y = lax.axis_index("gx"), lax.axis_index("gy")
    parity = lax.rem(at_y, 2)
    even_row = pl.multiple_of((1 - parity) * 2 * rows_y, SUBLANES)
    odd_row = pl.multiple_of(parity * 2 * rows_y, SUBLANES)
    odd_inside = jnp.where((at_y > 0) & (at_y < count_y - 1), 1.0, 0.0)
    own_x, other_x = at_x * rows_x, (1 - at_x) * rows_x
    for ref, first_x, row, keep in (
        (own_ref, own_x, rows_y, None),
        (other_ref, other_x, rows_y, None),
        (even_ref, own_x, even_row, None),
        (even_other_ref, other_x, even_row, None),
        (odd_ref, own_x, odd_row, odd_inside),
        (odd_other_ref, other_x, odd_row, odd_inside),
    ):
        for at in range(rows_x):
            weight = jacobi_weight / (6.0 + ref[1, at])
            if keep is not None:
                weight = weight * keep
            weight_ref[first_x + at, pl.ds(row, rows_y), :] = weight
            drive_ref[first_x + at, pl.ds(row, rows_y), :] = weight * ref[0, at]

    gathered = jnp.sum(gathered_ref[...], axis=0)
    coarse = inverse_ref.shape[0]
    last = coarse // LANES
    cuts = cuts_of(gathered[last : last + 1], count_x, count_y)
    place = window_place(count_y, rows_y, (window_y, cells_z))
    planes = coarse_planes(gathered, inverse_ref, ids_ref, scale_factor, cuts, place)
    empty = jnp.zeros((window_y, cells_z), jnp.float32)
    for ref in (field_ref, spare_ref):
        ref[0] = empty
        ref[window_x + 1] = empty
    for at in range(window_x):
        field_ref[at + 1] = correction_of(planes, cuts, float(at))
    for step in range(SWEEPS // 2):
        sweep(field_ref, spare_ref, weight_ref, drive_ref)
        sweep(spare_ref, field_ref, weight_ref, drive_ref)

    residual = []
    for at in range(rows_x):
        center, beside = neighbours(field_ref, own_x + at)
        center, beside = center[rows_y : 2 * rows_y], beside[rows_y : 2 * rows_y]
        residual.append(own_ref[0, at] - ((6.0 + own_ref[1, at]) * center - beside))
    row = restrict(jnp.concatenate(residual, axis=0), ids_ref, coarse)
    store_row(out_ref, row)
    out_ref[last : last + 1, :] = gathered[last : last + 1]


def second_kernel(
    counts, scale_factor, pieces,
    field_ref, weight_ref, drive_ref, ids_ref, inverse_ref, gathered_ref, *rest,
):
    out_refs, (one_ref, two_ref) = rest[:pieces], rest[pieces:]
    count_x, count_y = counts
    window_x, window_y, cells_z = weight_ref.shape
    _, rows_y, chunk = out_refs[0].shape
    rows_x = out_refs[0].shape[0]
    own_x = lax.axis_index("gx") * rows_x
    gathered = jnp.sum(gathered_ref[...], axis=0)
    last = inverse_ref.shape[0] // LANES
    cuts = cuts_of(gathered_ref[0, last : last + 1], count_x, count_y)
    place = window_place(count_y, rows_y, (window_y, cells_z))
    planes = coarse_planes(gathered, inverse_ref, ids_ref, scale_factor, cuts, place)
    empty = jnp.zeros((window_y, cells_z), jnp.float32)
    for ref in (one_ref, two_ref):
        ref[0] = empty
        ref[window_x + 1] = empty
    for at in range(window_x):
        one_ref[at + 1] = field_ref[at + 1] + correction_of(planes, cuts, float(at))
    sweep(one_ref, two_ref, weight_ref, drive_ref)
    for step in range(SWEEPS // 2 - 1):
        sweep(two_ref, one_ref, weight_ref, drive_ref)
        sweep(one_ref, two_ref, weight_ref, drive_ref)
    for at in range(rows_x):
        center, beside = neighbours(two_ref, own_x + at)
        value = (
            center * (1.0 - jacobi_weight)
            + drive_ref[own_x + at]
            + weight_ref[own_x + at] * beside
        )
        one_ref[at, pl.ds(0, rows_y), :] = value[rows_y : 2 * rows_y]
    me = lax.axis_index("grp")
    for turn in range(pieces):
        first = pl.multiple_of(lax.bitwise_xor(me, turn) * chunk, LANES)
        for at in range(rows_x):
            out_refs[turn][at] = one_ref[at, pl.ds(0, rows_y), pl.ds(first, chunk)]


def sketch_kernel(pieces, omega_ref, psi_ref, phi_ref, range_ref, *rest):
    snaps, (new_ref, out_ref) = rest[:pieces], rest[pieces:]
    rows_x = psi_ref.shape[1]
    me = lax.axis_index("grp")
    slots = [lax.bitwise_xor(me, turn) for turn in range(pieces)]
    cells = [[snaps[turn][at] for at in range(rows_x)] for turn in range(pieces)]
    corange, core = psi_ref.shape[0], phi_ref.shape[0]
    ones = jnp.ones((SUBLANES, LANES), jnp.float32)
    totals = [[] for _ in range(pieces)]
    for ref, count in ((psi_ref, corange), (phi_ref, core)):
        for at_row in range(count):
            parts = [ref[at_row, at] for at in range(rows_x)]
            for turn in range(pieces):
                total = parts[0] * cells[turn][0]
                for at in range(1, rows_x):
                    total = total + parts[at] * cells[turn][at]
                totals[turn].append(jnp.sum(total, axis=0, keepdims=True))
    out_ref[...] = jnp.zeros_like(out_ref)
    for turn in range(pieces):
        row = dot_nt(ones, jnp.concatenate(totals[turn], axis=0))[0:1]
        out_ref[pl.ds(slots[turn], 1), pl.ds(0, corange + core)] = row
    for at_row in range(range_ref.shape[0]):
        scales = [omega_ref[slots[turn], at_row] for turn in range(pieces)]
        for at in range(rows_x):
            value = range_ref[at_row, at]
            for turn in range(pieces):
                value = value + scales[turn] * cells[turn][at]
            new_ref[at_row, at] = value


def end_kernel(gathered_ref, xi_ref, core_ref, corange_out_ref, core_out_ref):
    snaps = xi_ref.shape[1]
    corange = corange_out_ref.shape[0]
    core = core_ref.shape[0]
    total = jnp.sum(gathered_ref[...], axis=0)
    turned = jnp.concatenate([total, jnp.zeros((SUBLANES - snaps, LANES), jnp.float32)], axis=0).T
    corange_out_ref[...] = turned[:corange, :snaps]
    images = turned[corange : corange + core, :snaps]
    core_out_ref[...] = core_ref[...] + dot_nt(images, xi_ref[...])


vmem = pl.BlockSpec(memory_space=pltpu.VMEM)
smem = pl.BlockSpec(memory_space=pltpu.SMEM)


def call(kernel, outs, inputs, scratch=(), specs=None, name=None):
    many = isinstance(outs, list)
    shapes = [jax.ShapeDtypeStruct(shape, jnp.float32) for shape in (outs if many else [outs])]
    result = pl.pallas_call(
        kernel,
        out_shape=shapes,
        in_specs=specs or [vmem] * len(inputs),
        out_specs=[vmem] * len(shapes),
        scratch_shapes=[pltpu.VMEM(shape, jnp.float32) for shape in scratch],
        name=name,
    )(*inputs)
    return result if many else result[0]


def gather(values, axes, count):
    copies = jnp.broadcast_to(values[None], (count,) + values.shape)
    return lax.all_to_all(copies, axes, 0, 0)


def fast_body(
    sources, diagonal, coarse_ids, coarse_inverse, omega_rows, psi, phi, xi_cols, range_sketch,
    core_sketch,
):
    source = sources[0]
    rows_x, rows_y, cells_z = source.shape
    counts = (lax.axis_size("gx"), lax.axis_size("gy"))
    groups = lax.axis_size("grp")
    count_x, count_y = counts
    coarse = coarse_inverse.shape[0]
    scale_factor = coarse / (rows_x * count_x * rows_y * count_y * cells_z)
    window = (rows_x * count_x, 3 * rows_y, cells_z)
    padded = (window[0] + 2,) + window[1:]
    rows = coarse // LANES + 1

    def partner_y(at, phase):
        found = at ^ 1 if phase == 0 else ((at + 1) ^ 1) - 1
        return found if 0 <= found < count_y else at

    def pairs(cross, phase):
        return [
            (x * count_y + y, (x ^ cross) * count_y + (y if phase is None else partner_y(y, phase)))
            for x in range(count_x)
            for y in range(count_y)
        ]

    mine = jnp.stack([source, diagonal])
    others = [
        lax.ppermute(mine, ("gx", "gy"), pairs(cross, phase))
        for cross, phase in ((1, None), (0, 0), (1, 0), (0, 1), (1, 1))
    ]
    begin = call(
        functools.partial(begin_kernel, coarse), (rows, LANES), (source, coarse_ids), name="begin"
    )
    gathered = gather(begin, ("gx", "gy"), count_x * count_y)
    field, weight, drive, partial = call(
        functools.partial(first_kernel, counts, scale_factor),
        [padded, window, window, (rows, LANES)],
        (mine, *others, coarse_ids, coarse_inverse, gathered),
        scratch=[padded],
        name="first",
    )
    gathered = gather(partial, ("gx", "gy"), count_x * count_y)
    chunk = cells_z // groups
    pieces = call(
        functools.partial(second_kernel, counts, scale_factor, groups),
        [(rows_x, rows_y, chunk)] * groups,
        (field, weight, drive, coarse_ids, coarse_inverse, gathered),
        scratch=[padded, padded],
        name="second",
    )
    snaps = [pieces[0]] + [
        lax.ppermute(pieces[turn], "grp", [(at, at ^ turn) for at in range(groups)])
        for turn in range(1, groups)
    ]
    range_new, products = call(
        functools.partial(sketch_kernel, groups),
        [range_sketch.shape, (groups, LANES)],
        (omega_rows, psi, phi, range_sketch, *snaps),
        specs=[smem] + [vmem] * (3 + groups),
        name="sketch",
    )
    gathered = gather(products, ("grp", "gx", "gy"), groups * count_x * count_y)
    corange_cols, core_new = call(
        end_kernel,
        [(psi.shape[0], groups), core_sketch.shape],
        (gathered, xi_cols, core_sketch),
        name="end",
    )
    return range_new, corange_cols, core_new


def with_halo(cells, sides, width):
    for axis, dim in sides:
        count = lax.axis_size(axis)
        ends = count - 1
        head = lax.slice_in_dim(cells, 0, width, axis=dim)
        tail = lax.slice_in_dim(cells, cells.shape[dim] - width, cells.shape[dim], axis=dim)
        cells = jnp.concatenate(
            [
                lax.ppermute(tail, axis, [(i, (i + 1) % count) for i in range(ends)]),
                cells,
                lax.ppermute(head, axis, [((i + 1) % count, i) for i in range(ends)]),
            ],
            axis=dim,
        )
    return cells


def neighbour_image(widened, diagonal):
    center = widened[1:-1, 1:-1]
    beside = widened[2:, 1:-1] + widened[:-2, 1:-1]
    beside = beside + widened[1:-1, 2:] + widened[1:-1, :-2]
    padded = jnp.pad(center, ((0, 0), (0, 0), (1, 1)))
    beside = beside + padded[:, :, 2:] + padded[:, :, :-2]
    return (center, (6.0 + diagonal) * center - beside)


def smooth_once(widened, source, diagonal):
    center, applied = neighbour_image(widened, diagonal)
    return center + jacobi_weight * (source - applied) / (6.0 + diagonal)


def axis_maps(coarse_ids):
    ranks_x = coarse_ids[:, 0, 0] // (XY_CUTS * Z_CUTS)
    ranks_y = coarse_ids[0, :, 0] // Z_CUTS % XY_CUTS
    ranks_z = coarse_ids[0, 0, :] % Z_CUTS
    cuts_xy = jnp.arange(XY_CUTS, dtype=jnp.int32)
    cuts_z = jnp.arange(Z_CUTS, dtype=jnp.int32)
    map_x = (ranks_x[:, None] == cuts_xy[None, :]).astype(jnp.float32)
    map_y = (ranks_y[:, None] == cuts_xy[None, :]).astype(jnp.float32)
    map_z = (ranks_z[:, None] == cuts_z[None, :]).astype(jnp.float32)
    return (map_x, map_y, map_z)


def restrict_cells(values, maps):
    map_x, map_y, map_z = maps
    rows_x, rows_y, cells_z = values.shape
    along_z = jnp.dot(values.reshape(rows_x * rows_y, cells_z), map_z, precision=highest)
    along_z = along_z.reshape(rows_x, rows_y, Z_CUTS)
    along_y = jnp.einsum("xyc,yb->xbc", along_z, map_y, precision=highest)
    along_x = jnp.einsum("xbc,xa->abc", along_y, map_x, precision=highest)
    return along_x.reshape(-1)


def prolong(correction, maps, extent):
    map_x, map_y, map_z = maps
    boxes = correction.reshape(XY_CUTS, XY_CUTS, Z_CUTS)
    over_x = jnp.einsum("abc,xa->xbc", boxes, map_x, precision=highest)
    over_y = jnp.einsum("xbc,yb->xyc", over_x, map_y, precision=highest)
    spread = jnp.dot(over_y.reshape(extent[0] * extent[1], Z_CUTS), map_z.T, precision=highest)
    return spread.reshape(extent)


def general_body(
    sources, diagonal, coarse_ids, coarse_inverse, omega_rows, psi, phi, xi_cols, range_sketch,
    core_sketch,
):
    source = sources[0]
    rows_x, rows_y, cells_z = source.shape
    coarse = coarse_inverse.shape[0]
    total_cells = rows_x * lax.axis_size("gx") * rows_y * lax.axis_size("gy") * cells_z
    scale_factor = coarse / total_cells
    maps = axis_maps(coarse_ids)
    sides = (("gx", 0), ("gy", 1))
    pressure = jnp.zeros_like(source)
    for outer_step in range(OUTER):
        if outer_step == 0:
            residual = source
        else:
            residual = source - neighbour_image(with_halo(pressure, sides, 1), diagonal)[1]
        coarse_rhs = lax.psum(restrict_cells(residual, maps), ("gx", "gy"))
        correction = jnp.dot(coarse_inverse, coarse_rhs * scale_factor, precision=highest)
        pressure = pressure + prolong(correction, maps, source.shape)
        for sweep_step in range(SWEEPS):
            pressure = smooth_once(with_halo(pressure, sides, 1), source, diagonal)
    snapshot = lax.all_to_all(pressure[None], "grp", split_axis=3, concat_axis=0, tiled=True)
    columns = snapshot.reshape(snapshot.shape[0], -1)
    range_flat = range_sketch.reshape(range_sketch.shape[0], -1)
    range_new = range_flat + jnp.einsum("tk,tc->kc", omega_rows, columns, precision=highest)
    corange_part = jnp.einsum(
        "lc,tc->lt", psi.reshape(psi.shape[0], -1), columns, precision=highest
    )
    core_part = jnp.einsum("sc,tc->st", phi.reshape(phi.shape[0], -1), columns, precision=highest)
    corange_cols, core_images = lax.psum((corange_part, core_part), ("grp", "gx", "gy"))
    core_new = core_sketch + jnp.dot(core_images, xi_cols.T, precision=highest)
    return (range_new.reshape(range_sketch.shape), corange_cols, core_new)


def body(*arrays):
    rows_x, rows_y, cells_z = arrays[1].shape
    coarse, groups = arrays[3].shape[0], lax.axis_size("grp")
    fits = (
        lax.axis_size("gx") == 2
        and lax.axis_size("gy") % 2 == 0
        and rows_y >= OUTER * SWEEPS
        and rows_y % SUBLANES == 0
        and groups & (groups - 1) == 0
        and groups <= SUBLANES
        and cells_z % (groups * LANES) == 0
        and cells_z // groups == LANES
        and coarse % LANES == 0
        and arrays[5].shape[0] + arrays[6].shape[0] <= LANES
    )
    return (fast_body if fits else general_body)(*arrays)


def solution(mesh):
    return jax.shard_map(
        body,
        mesh=mesh,
        in_specs=(
            P("grp", "gx", "gy", None),
            P("gx", "gy", None),
            P("gx", "gy", None),
            P(),
            P(),
            P(None, "gx", "gy", "grp"),
            P(None, "gx", "gy", "grp"),
            P(),
            P(None, "gx", "gy", "grp"),
            P(),
        ),
        out_specs=(P(None, "gx", "gy", "grp"), P(), P()),
        check_vma=False,
    )
```

```python
import functools

import jax
import jax.numpy as jnp
from jax import lax
from jax.experimental import pallas as pl
from jax.experimental.pallas import tpu as pltpu
from jax.sharding import PartitionSpec as P

OUTER = 2
SWEEPS = 4
XY_CUTS = 4
Z_CUTS = 16
LANES = 128
SUBLANES = 8
VMEM_BYTES = 16 * 2**20

jacobi_weight = 2.0 / 3.0
highest = lax.Precision.HIGHEST


def dot_nn(a, b):
    return lax.dot_general(
        a, b, (((1,), (0,)), ((), ())), precision=highest, preferred_element_type=jnp.float32
    )


def dot_nt(a, b):
    return lax.dot_general(
        a, b, (((1,), (1,)), ((), ())), precision=highest, preferred_element_type=jnp.float32
    )


def dot_tn(a, b):
    return lax.dot_general(
        a, b, (((0,), (0,)), ((), ())), precision=highest, preferred_element_type=jnp.float32
    )


def iota(shape, dim):
    return lax.broadcasted_iota(jnp.int32, shape, dim)


def spread_map(ids_ref, coarse):
    cells_z = ids_ref.shape[2]
    ranks = lax.bitwise_and(ids_ref[0, 0:1, :], Z_CUTS - 1)
    rows = lax.bitwise_and(iota((coarse, cells_z), 0), Z_CUTS - 1)
    return (rows == ranks).astype(jnp.float32)


def column_map(ids_ref):
    rows_x, rows_y, _ = ids_ref.shape
    boxes = XY_CUTS * XY_CUTS
    tile = ids_ref[:, :, :LANES].reshape(rows_x * rows_y, LANES) // Z_CUTS
    turned = tile.astype(jnp.float32).T[:boxes]
    return (turned == iota(turned.shape, 0).astype(jnp.float32)).astype(jnp.float32)


def restrict(values, ids_ref, coarse):
    boxes = XY_CUTS * XY_CUTS
    by_box = dot_nn(column_map(ids_ref), values)
    wide = dot_nt(by_box, spread_map(ids_ref, coarse))
    own = iota((boxes, coarse), 1) // Z_CUTS == iota((boxes, coarse), 0)
    return jnp.sum(jnp.where(own, wide, 0.0), axis=0, keepdims=True)


def store_copies(out_ref, rows):
    for copy in range(out_ref.shape[0]):
        for at, row in enumerate(rows):
            out_ref[copy, at : at + 1, :] = row


def lane_rows(row):
    return [row[:, at : at + LANES] for at in range(0, row.shape[1], LANES)]


def begin_kernel(coarse, source_ref, ids_ref, out_ref):
    rows_x, rows_y, cells_z = source_ref.shape
    row = restrict(source_ref[...].reshape(rows_x * rows_y, cells_z), ids_ref, coarse)
    lanes = iota((1, LANES), 1)
    tile = ids_ref[:, :, :LANES] // Z_CUTS
    ranks_x = tile[:, 0:1, :] // XY_CUTS
    ranks_y = lax.bitwise_and(tile[0], XY_CUTS - 1)
    below_x = jnp.sum((ranks_x <= lanes[None]).astype(jnp.float32), axis=0)
    below_y = jnp.sum((ranks_y <= lanes - XY_CUTS).astype(jnp.float32), axis=0, keepdims=True)
    store_copies(out_ref, lane_rows(row) + [jnp.where(lanes < XY_CUTS, below_x, below_y)])


def coarse_planes(gathered, inverse_ref, ids_ref, scale_factor, cuts, place):
    coarse = inverse_ref.shape[0]
    boxes = XY_CUTS * XY_CUTS
    _, cut_y = cuts
    row = jnp.concatenate(
        [gathered[part : part + 1, :] for part in range(coarse // LANES)], axis=1
    )
    row = jnp.broadcast_to(row * scale_factor, (SUBLANES, coarse))
    solved = dot_nt(row, inverse_ref[...])[0:1]
    own = iota((boxes, coarse), 1) // Z_CUTS == iota((boxes, coarse), 0)
    along_z = dot_nn(jnp.where(own, solved, 0.0), spread_map(ids_ref, coarse))
    place_y, inside = place
    planes = []
    for box_x in range(XY_CUTS):
        first = box_x * XY_CUTS
        plane = jnp.broadcast_to(along_z[first : first + 1], place_y.shape)
        for box_y in range(1, XY_CUTS):
            line = along_z[first + box_y : first + box_y + 1]
            plane = jnp.where(place_y >= cut_y[box_y - 1], line, plane)
        planes.append(jnp.where(inside, plane, 0.0))
    return planes


def correction_of(planes, cuts, place_x):
    cut_x, _ = cuts
    value = planes[0]
    for box_x in range(1, XY_CUTS):
        value = jnp.where(cut_x[box_x - 1] <= place_x, planes[box_x], value)
    return value


def cuts_of(row, count_x, count_y):
    cut_x = [row[:, at : at + 1] * (1.0 / count_y) for at in range(XY_CUTS - 1)]
    cut_y = [row[:, XY_CUTS + at : XY_CUTS + at + 1] * (1.0 / count_x) for at in range(XY_CUTS - 1)]
    return cut_x, cut_y


def beside_z(values):
    cells_z = values.shape[-1]
    lanes = iota(values.shape, values.ndim - 1)
    ahead = pltpu.roll(values, cells_z - 1, values.ndim - 1)
    behind = pltpu.roll(values, 1, values.ndim - 1)
    return jnp.where(lanes == cells_z - 1, 0.0, ahead) + jnp.where(lanes == 0, 0.0, behind)


def beside_y(values):
    rows = values.shape[0]
    return pltpu.roll(values, rows - 1, 0) + pltpu.roll(values, 1, 0)


def neighbours(field_ref, at):
    center = field_ref[at + 1]
    return center, field_ref[at] + field_ref[at + 2] + beside_y(center) + beside_z(center)


def sweep(from_ref, to_ref, weight_ref, drive_ref):
    for at in range(weight_ref.shape[0]):
        center, beside = neighbours(from_ref, at)
        to_ref[at + 1] = (
            center * (1.0 - jacobi_weight) + drive_ref[at] + weight_ref[at] * beside
        )


def window_place(count_y, rows_y, shape):
    place_y = iota(shape, 0) + (lax.axis_index("gy") - 1) * rows_y
    inside = (place_y >= 0) & (place_y < rows_y * count_y)
    return place_y.astype(jnp.float32), inside


def first_kernel(
    counts, scale_factor, own_ref, other_ref, even_ref, even_other_ref, odd_ref, odd_other_ref,
    ids_ref, inverse_ref, gathered_ref,
    field_ref, weight_ref, drive_ref, out_ref, spare_ref,
):
    count_x, count_y = counts
    _, rows_x, rows_y, cells_z = own_ref.shape
    window_x, window_y, _ = weight_ref.shape
    at_x, at_y = lax.axis_index("gx"), lax.axis_index("gy")
    parity = lax.rem(at_y, 2)
    even_row = pl.multiple_of((1 - parity) * 2 * rows_y, SUBLANES)
    odd_row = pl.multiple_of(parity * 2 * rows_y, SUBLANES)
    odd_inside = jnp.where((at_y > 0) & (at_y < count_y - 1), 1.0, 0.0)
    own_x, other_x = at_x * rows_x, (1 - at_x) * rows_x
    for ref, first_x, row, keep in (
        (own_ref, own_x, rows_y, None),
        (other_ref, other_x, rows_y, None),
        (even_ref, own_x, even_row, None),
        (even_other_ref, other_x, even_row, None),
        (odd_ref, own_x, odd_row, odd_inside),
        (odd_other_ref, other_x, odd_row, odd_inside),
    ):
        for at in range(rows_x):
            weight = jacobi_weight / (6.0 + ref[1, at])
            if keep is not None:
                weight = weight * keep
            weight_ref[first_x + at, pl.ds(row, rows_y), :] = weight
            drive_ref[first_x + at, pl.ds(row, rows_y), :] = weight * ref[0, at]

    gathered = jnp.sum(gathered_ref[...], axis=0)
    coarse = inverse_ref.shape[0]
    last = coarse // LANES
    cuts = cuts_of(gathered[last : last + 1], count_x, count_y)
    place = window_place(count_y, rows_y, (window_y, cells_z))
    planes = coarse_planes(gathered, inverse_ref, ids_ref, scale_factor, cuts, place)
    empty = jnp.zeros((window_y, cells_z), jnp.float32)
    for ref in (field_ref, spare_ref):
        ref[0] = empty
        ref[window_x + 1] = empty
    for at in range(window_x):
        field_ref[at + 1] = correction_of(planes, cuts, float(at))
    for step in range(SWEEPS // 2):
        sweep(field_ref, spare_ref, weight_ref, drive_ref)
        sweep(spare_ref, field_ref, weight_ref, drive_ref)

    residual = []
    for at in range(rows_x):
        center, beside = neighbours(field_ref, own_x + at)
        center, beside = center[rows_y : 2 * rows_y], beside[rows_y : 2 * rows_y]
        residual.append(own_ref[0, at] - ((6.0 + own_ref[1, at]) * center - beside))
    row = restrict(jnp.concatenate(residual, axis=0), ids_ref, coarse)
    store_copies(out_ref, lane_rows(row) + [gathered[last : last + 1]])


def second_kernel(
    counts, scale_factor, pieces,
    field_ref, weight_ref, drive_ref, ids_ref, inverse_ref, gathered_ref, *rest,
):
    out_refs, (one_ref, two_ref) = rest[:pieces], rest[pieces:]
    count_x, count_y = counts
    window_x, window_y, cells_z = weight_ref.shape
    _, rows_y, chunk = out_refs[0].shape
    rows_x = out_refs[0].shape[0]
    own_x = lax.axis_index("gx") * rows_x
    gathered = jnp.sum(gathered_ref[...], axis=0)
    last = inverse_ref.shape[0] // LANES
    cuts = cuts_of(gathered_ref[0, last : last + 1], count_x, count_y)
    place = window_place(count_y, rows_y, (window_y, cells_z))
    planes = coarse_planes(gathered, inverse_ref, ids_ref, scale_factor, cuts, place)
    empty = jnp.zeros((window_y, cells_z), jnp.float32)
    for ref in (one_ref, two_ref):
        ref[0] = empty
        ref[window_x + 1] = empty
    for at in range(window_x):
        one_ref[at + 1] = field_ref[at + 1] + correction_of(planes, cuts, float(at))
    sweep(one_ref, two_ref, weight_ref, drive_ref)
    for step in range(SWEEPS // 2 - 1):
        sweep(two_ref, one_ref, weight_ref, drive_ref)
        sweep(one_ref, two_ref, weight_ref, drive_ref)
    for at in range(rows_x):
        center, beside = neighbours(two_ref, own_x + at)
        value = (
            center * (1.0 - jacobi_weight)
            + drive_ref[own_x + at]
            + weight_ref[own_x + at] * beside
        )
        one_ref[at, pl.ds(0, rows_y), :] = value[rows_y : 2 * rows_y]
    me = lax.axis_index("grp")
    for turn in range(pieces):
        first = pl.multiple_of(lax.bitwise_xor(me, turn) * chunk, LANES)
        for at in range(rows_x):
            out_refs[turn][at] = one_ref[at, pl.ds(0, rows_y), pl.ds(first, chunk)]


def sketch_kernel(pieces, omega_ref, psi_ref, phi_ref, range_ref, *rest):
    snaps, (new_ref, out_ref) = rest[:pieces], rest[pieces:]
    rows_x = psi_ref.shape[1]
    me = lax.axis_index("grp")
    slots = [lax.bitwise_xor(me, turn) for turn in range(pieces)]
    cells = [[snaps[turn][at] for at in range(rows_x)] for turn in range(pieces)]
    corange, core = psi_ref.shape[0], phi_ref.shape[0]
    ones = jnp.ones((SUBLANES, LANES), jnp.float32)
    totals = [[] for _ in range(pieces)]
    for ref, count in ((psi_ref, corange), (phi_ref, core)):
        for at_row in range(count):
            parts = [ref[at_row, at] for at in range(rows_x)]
            for turn in range(pieces):
                total = parts[0] * cells[turn][0]
                for at in range(1, rows_x):
                    total = total + parts[at] * cells[turn][at]
                totals[turn].append(jnp.sum(total, axis=0, keepdims=True))
    rest = jnp.zeros((LANES - corange - core, LANES), jnp.float32)
    for turn in range(pieces):
        row = dot_nt(ones, jnp.concatenate(totals[turn] + [rest], axis=0))[0:1]
        for copy in range(out_ref.shape[0]):
            out_ref[copy, pl.ds(slots[turn], 1), :] = row
    for at_row in range(range_ref.shape[0]):
        scales = [omega_ref[slots[turn], at_row] for turn in range(pieces)]
        for at in range(rows_x):
            value = range_ref[at_row, at]
            for turn in range(pieces):
                value = value + scales[turn] * cells[turn][at]
            new_ref[at_row, at] = value


def end_kernel(gathered_ref, xi_ref, core_ref, corange_out_ref, core_out_ref):
    corange = corange_out_ref.shape[1]
    core = core_ref.shape[0]
    total = jnp.sum(gathered_ref[...], axis=0)
    corange_out_ref[...] = total[:, :corange]
    images = total[:, corange : corange + core]
    core_out_ref[...] = core_ref[...] + dot_tn(images, xi_ref[...])


vmem = pl.BlockSpec(memory_space=pltpu.VMEM)
smem = pl.BlockSpec(memory_space=pltpu.SMEM)


def call(kernel, outs, inputs, scratch=(), specs=None, name=None):
    many = isinstance(outs, list)
    shapes = [jax.ShapeDtypeStruct(shape, jnp.float32) for shape in (outs if many else [outs])]
    result = pl.pallas_call(
        kernel,
        out_shape=shapes,
        in_specs=specs or [vmem] * len(inputs),
        out_specs=[vmem] * len(shapes),
        scratch_shapes=[pltpu.VMEM(shape, jnp.float32) for shape in scratch],
        compiler_params=pltpu.CompilerParams(vmem_limit_bytes=VMEM_BYTES),
        name=name,
    )(*inputs)
    return result if many else result[0]


def gather(copies, axes):
    return lax.all_to_all(copies, axes, 0, 0)


def fast_body(
    sources, diagonal, coarse_ids, coarse_inverse, omega_rows, psi, phi, xi_cols, range_sketch,
    core_sketch,
):
    source = sources[0]
    rows_x, rows_y, cells_z = source.shape
    counts = (lax.axis_size("gx"), lax.axis_size("gy"))
    groups = lax.axis_size("grp")
    count_x, count_y = counts
    coarse = coarse_inverse.shape[0]
    scale_factor = coarse / (rows_x * count_x * rows_y * count_y * cells_z)
    window = (rows_x * count_x, 3 * rows_y, cells_z)
    padded = (window[0] + 2,) + window[1:]
    copies = (count_x * count_y, coarse // LANES + 1, LANES)

    def partner_y(at, phase):
        found = at ^ 1 if phase == 0 else ((at + 1) ^ 1) - 1
        return found if 0 <= found < count_y else at

    def pairs(cross, phase):
        return [
            (x * count_y + y, (x ^ cross) * count_y + (y if phase is None else partner_y(y, phase)))
            for x in range(count_x)
            for y in range(count_y)
        ]

    mine = jnp.stack([source, diagonal])
    others = [
        lax.ppermute(mine, ("gx", "gy"), pairs(cross, phase))
        for cross, phase in ((1, None), (0, 0), (1, 0), (0, 1), (1, 1))
    ]
    begin = call(
        functools.partial(begin_kernel, coarse), copies, (source, coarse_ids), name="begin"
    )
    gathered = gather(begin, ("gx", "gy"))
    field, weight, drive, partial = call(
        functools.partial(first_kernel, counts, scale_factor),
        [padded, window, window, copies],
        (mine, *others, coarse_ids, coarse_inverse, gathered),
        scratch=[padded],
        name="first",
    )
    gathered = gather(partial, ("gx", "gy"))
    chunk = cells_z // groups
    pieces = call(
        functools.partial(second_kernel, counts, scale_factor, groups),
        [(rows_x, rows_y, chunk)] * groups,
        (field, weight, drive, coarse_ids, coarse_inverse, gathered),
        scratch=[padded, padded],
        name="second",
    )
    snaps = [pieces[0]] + [
        lax.ppermute(pieces[turn], "grp", [(at, at ^ turn) for at in range(groups)])
        for turn in range(1, groups)
    ]
    range_new, products = call(
        functools.partial(sketch_kernel, groups),
        [range_sketch.shape, (groups * count_x * count_y, groups, LANES)],
        (omega_rows, psi, phi, range_sketch, *snaps),
        specs=[smem] + [vmem] * (3 + groups),
        name="sketch",
    )
    gathered = gather(products, ("grp", "gx", "gy"))
    corange_cols, core_new = call(
        end_kernel,
        [(groups, psi.shape[0]), core_sketch.shape],
        (gathered, xi_cols.T, core_sketch),
        name="end",
    )
    return range_new, corange_cols.T, core_new


def with_halo(cells, sides, width):
    for axis, dim in sides:
        count = lax.axis_size(axis)
        ends = count - 1
        head = lax.slice_in_dim(cells, 0, width, axis=dim)
        tail = lax.slice_in_dim(cells, cells.shape[dim] - width, cells.shape[dim], axis=dim)
        cells = jnp.concatenate(
            [
                lax.ppermute(tail, axis, [(i, (i + 1) % count) for i in range(ends)]),
                cells,
                lax.ppermute(head, axis, [((i + 1) % count, i) for i in range(ends)]),
            ],
            axis=dim,
        )
    return cells


def neighbour_image(widened, diagonal):
    center = widened[1:-1, 1:-1]
    beside = widened[2:, 1:-1] + widened[:-2, 1:-1]
    beside = beside + widened[1:-1, 2:] + widened[1:-1, :-2]
    padded = jnp.pad(center, ((0, 0), (0, 0), (1, 1)))
    beside = beside + padded[:, :, 2:] + padded[:, :, :-2]
    return (center, (6.0 + diagonal) * center - beside)


def smooth_once(widened, source, diagonal):
    center, applied = neighbour_image(widened, diagonal)
    return center + jacobi_weight * (source - applied) / (6.0 + diagonal)


def axis_maps(coarse_ids):
    ranks_x = coarse_ids[:, 0, 0] // (XY_CUTS * Z_CUTS)
    ranks_y = coarse_ids[0, :, 0] // Z_CUTS % XY_CUTS
    ranks_z = coarse_ids[0, 0, :] % Z_CUTS
    cuts_xy = jnp.arange(XY_CUTS, dtype=jnp.int32)
    cuts_z = jnp.arange(Z_CUTS, dtype=jnp.int32)
    map_x = (ranks_x[:, None] == cuts_xy[None, :]).astype(jnp.float32)
    map_y = (ranks_y[:, None] == cuts_xy[None, :]).astype(jnp.float32)
    map_z = (ranks_z[:, None] == cuts_z[None, :]).astype(jnp.float32)
    return (map_x, map_y, map_z)


def restrict_cells(values, maps):
    map_x, map_y, map_z = maps
    rows_x, rows_y, cells_z = values.shape
    along_z = jnp.dot(values.reshape(rows_x * rows_y, cells_z), map_z, precision=highest)
    along_z = along_z.reshape(rows_x, rows_y, Z_CUTS)
    along_y = jnp.einsum("xyc,yb->xbc", along_z, map_y, precision=highest)
    along_x = jnp.einsum("xbc,xa->abc", along_y, map_x, precision=highest)
    return along_x.reshape(-1)


def prolong(correction, maps, extent):
    map_x, map_y, map_z = maps
    boxes = correction.reshape(XY_CUTS, XY_CUTS, Z_CUTS)
    over_x = jnp.einsum("abc,xa->xbc", boxes, map_x, precision=highest)
    over_y = jnp.einsum("xbc,yb->xyc", over_x, map_y, precision=highest)
    spread = jnp.dot(over_y.reshape(extent[0] * extent[1], Z_CUTS), map_z.T, precision=highest)
    return spread.reshape(extent)


def general_body(
    sources, diagonal, coarse_ids, coarse_inverse, omega_rows, psi, phi, xi_cols, range_sketch,
    core_sketch,
):
    source = sources[0]
    rows_x, rows_y, cells_z = source.shape
    coarse = coarse_inverse.shape[0]
    total_cells = rows_x * lax.axis_size("gx") * rows_y * lax.axis_size("gy") * cells_z
    scale_factor = coarse / total_cells
    maps = axis_maps(coarse_ids)
    sides = (("gx", 0), ("gy", 1))
    pressure = jnp.zeros_like(source)
    for outer_step in range(OUTER):
        if outer_step == 0:
            residual = source
        else:
            residual = source - neighbour_image(with_halo(pressure, sides, 1), diagonal)[1]
        coarse_rhs = lax.psum(restrict_cells(residual, maps), ("gx", "gy"))
        correction = jnp.dot(coarse_inverse, coarse_rhs * scale_factor, precision=highest)
        pressure = pressure + prolong(correction, maps, source.shape)
        for sweep_step in range(SWEEPS):
            pressure = smooth_once(with_halo(pressure, sides, 1), source, diagonal)
    snapshot = lax.all_to_all(pressure[None], "grp", split_axis=3, concat_axis=0, tiled=True)
    columns = snapshot.reshape(snapshot.shape[0], -1)
    range_flat = range_sketch.reshape(range_sketch.shape[0], -1)
    range_new = range_flat + jnp.einsum("tk,tc->kc", omega_rows, columns, precision=highest)
    corange_part = jnp.einsum(
        "lc,tc->lt", psi.reshape(psi.shape[0], -1), columns, precision=highest
    )
    core_part = jnp.einsum("sc,tc->st", phi.reshape(phi.shape[0], -1), columns, precision=highest)
    corange_cols, core_images = lax.psum((corange_part, core_part), ("grp", "gx", "gy"))
    core_new = core_sketch + jnp.dot(core_images, xi_cols.T, precision=highest)
    return (range_new.reshape(range_sketch.shape), corange_cols, core_new)


def body(*arrays):
    rows_x, rows_y, cells_z = arrays[1].shape
    coarse, groups = arrays[3].shape[0], lax.axis_size("grp")
    fits = (
        lax.axis_size("gx") == 2
        and lax.axis_size("gy") % 2 == 0
        and rows_y >= OUTER * SWEEPS
        and rows_y % SUBLANES == 0
        and groups & (groups - 1) == 0
        and groups <= SUBLANES
        and cells_z % (groups * LANES) == 0
        and cells_z // groups == LANES
        and coarse % LANES == 0
        and arrays[5].shape[0] + arrays[6].shape[0] <= LANES
    )
    return (fast_body if fits else general_body)(*arrays)


def solution(mesh):
    return jax.shard_map(
        body,
        mesh=mesh,
        in_specs=(
            P("grp", "gx", "gy", None),
            P("gx", "gy", None),
            P("gx", "gy", None),
            P(),
            P(),
            P(None, "gx", "gy", "grp"),
            P(None, "gx", "gy", "grp"),
            P(),
            P(None, "gx", "gy", "grp"),
            P(),
        ),
        out_specs=(P(None, "gx", "gy", "grp"), P(), P()),
        check_vma=False,
    )
```

```python
import functools

import jax
import jax.numpy as jnp
from jax import lax
from jax.experimental import pallas as pl
from jax.experimental.pallas import tpu as pltpu
from jax.sharding import PartitionSpec as P


OUTER = 2
SWEEPS = 4
XY_CUTS = 4
Z_CUTS = 16
LANES = 128
SUBLANES = 8
VMEM_BYTES = 16 * 2**20

jacobi_weight = 2.0 / 3.0
highest = lax.Precision.HIGHEST


def dot_nn(a, b):
    return lax.dot_general(
        a, b, (((1,), (0,)), ((), ())), precision=highest, preferred_element_type=jnp.float32
    )


def dot_nt(a, b):
    return lax.dot_general(
        a, b, (((1,), (1,)), ((), ())), precision=highest, preferred_element_type=jnp.float32
    )


def dot_tn(a, b):
    return lax.dot_general(
        a, b, (((0,), (0,)), ((), ())), precision=highest, preferred_element_type=jnp.float32
    )


def iota(shape, dim):
    return lax.broadcasted_iota(jnp.int32, shape, dim)


def spread_map(ids_ref, coarse):
    cells_z = ids_ref.shape[2]
    ranks = lax.bitwise_and(ids_ref[0, 0:1, :], Z_CUTS - 1)
    rows = lax.bitwise_and(iota((coarse, cells_z), 0), Z_CUTS - 1)
    return (rows == ranks).astype(jnp.float32)


def column_map(ids_ref):
    rows_x, rows_y, _ = ids_ref.shape
    boxes = XY_CUTS * XY_CUTS
    tile = ids_ref[:, :, :LANES].reshape(rows_x * rows_y, LANES) // Z_CUTS
    turned = tile.astype(jnp.float32).T[:boxes]
    return (turned == iota(turned.shape, 0).astype(jnp.float32)).astype(jnp.float32)


def restrict(values, ids_ref, coarse):
    boxes = XY_CUTS * XY_CUTS
    by_box = dot_nn(column_map(ids_ref), values)
    wide = dot_nt(by_box, spread_map(ids_ref, coarse))
    own = iota((boxes, coarse), 1) // Z_CUTS == iota((boxes, coarse), 0)
    return jnp.sum(jnp.where(own, wide, 0.0), axis=0, keepdims=True)


def store_copies(out_ref, rows):
    for copy in range(out_ref.shape[0]):
        for at, row in enumerate(rows):
            out_ref[copy, at : at + 1, :] = row


def lane_rows(row):
    return [row[:, at : at + LANES] for at in range(0, row.shape[1], LANES)]


def begin_kernel(
    source_from, diagonal_from, ids_from, inverse_from,
    mine_ref, ids_ref, inverse_ref, out_ref, arrived,
):
    loads = [
        pltpu.make_async_copy(source, target, arrived.at[at])
        for at, (source, target) in enumerate(
            (
                (ids_from, ids_ref),
                (source_from, mine_ref.at[0]),
                (diagonal_from, mine_ref.at[1]),
                (inverse_from, inverse_ref),
            )
        )
    ]
    for load in loads:
        load.start()
    coarse = inverse_ref.shape[0]
    rows_x, rows_y, cells_z = ids_ref.shape
    loads[0].wait()
    loads[1].wait()
    row = restrict(mine_ref[0].reshape(rows_x * rows_y, cells_z), ids_ref, coarse)
    lanes = iota((1, LANES), 1)
    tile = ids_ref[:, :, :LANES] // Z_CUTS
    ranks_x = tile[:, 0:1, :] // XY_CUTS
    ranks_y = lax.bitwise_and(tile[0], XY_CUTS - 1)
    below_x = jnp.sum((ranks_x <= lanes[None]).astype(jnp.float32), axis=0)
    below_y = jnp.sum((ranks_y <= lanes - XY_CUTS).astype(jnp.float32), axis=0, keepdims=True)
    store_copies(out_ref, lane_rows(row) + [jnp.where(lanes < XY_CUTS, below_x, below_y)])
    loads[2].wait()
    loads[3].wait()


def coarse_planes(gathered, inverse_ref, ids_ref, scale_factor, cuts, place):
    coarse = inverse_ref.shape[0]
    boxes = XY_CUTS * XY_CUTS
    _, cut_y = cuts
    row = jnp.concatenate(
        [gathered[part : part + 1, :] for part in range(coarse // LANES)], axis=1
    )
    row = jnp.broadcast_to(row * scale_factor, (SUBLANES, coarse))
    solved = dot_nt(row, inverse_ref[...])[0:1]
    own = iota((boxes, coarse), 1) // Z_CUTS == iota((boxes, coarse), 0)
    along_z = dot_nn(jnp.where(own, solved, 0.0), spread_map(ids_ref, coarse))
    place_y, inside = place
    planes = []
    for box_x in range(XY_CUTS):
        first = box_x * XY_CUTS
        plane = jnp.broadcast_to(along_z[first : first + 1], place_y.shape)
        for box_y in range(1, XY_CUTS):
            line = along_z[first + box_y : first + box_y + 1]
            plane = jnp.where(place_y >= cut_y[box_y - 1], line, plane)
        planes.append(jnp.where(inside, plane, 0.0))
    return planes


def correction_of(planes, cuts, place_x):
    cut_x, _ = cuts
    value = planes[0]
    for box_x in range(1, XY_CUTS):
        value = jnp.where(cut_x[box_x - 1] <= place_x, planes[box_x], value)
    return value


def cuts_of(row, count_x, count_y):
    cut_x = [row[:, at : at + 1] * (1.0 / count_y) for at in range(XY_CUTS - 1)]
    cut_y = [row[:, XY_CUTS + at : XY_CUTS + at + 1] * (1.0 / count_x) for at in range(XY_CUTS - 1)]
    return cut_x, cut_y


def beside_z(values):
    cells_z = values.shape[-1]
    lanes = iota(values.shape, values.ndim - 1)
    ahead = pltpu.roll(values, cells_z - 1, values.ndim - 1)
    behind = pltpu.roll(values, 1, values.ndim - 1)
    return jnp.where(lanes == cells_z - 1, 0.0, ahead) + jnp.where(lanes == 0, 0.0, behind)


def beside_y(values):
    rows = values.shape[0]
    return pltpu.roll(values, rows - 1, 0) + pltpu.roll(values, 1, 0)


def neighbours(field_ref, at):
    center = field_ref[at + 1]
    return center, field_ref[at] + field_ref[at + 2] + beside_y(center) + beside_z(center)


def sweep(from_ref, to_ref, weight_ref, drive_ref):
    for at in range(weight_ref.shape[0]):
        center, beside = neighbours(from_ref, at)
        to_ref[at + 1] = (
            center * (1.0 - jacobi_weight) + drive_ref[at] + weight_ref[at] * beside
        )


def window_place(count_y, rows_y, shape):
    place_y = iota(shape, 0) + (lax.axis_index("gy") - 1) * rows_y
    inside = (place_y >= 0) & (place_y < rows_y * count_y)
    return place_y.astype(jnp.float32), inside


def first_kernel(
    counts, scale_factor, own_ref, other_ref, even_ref, even_other_ref, odd_ref, odd_other_ref,
    ids_ref, inverse_ref, gathered_ref,
    field_ref, weight_ref, drive_ref, out_ref, spare_ref,
):
    count_x, count_y = counts
    _, rows_x, rows_y, cells_z = own_ref.shape
    window_x, window_y, _ = weight_ref.shape
    at_x, at_y = lax.axis_index("gx"), lax.axis_index("gy")
    parity = lax.rem(at_y, 2)
    even_row = pl.multiple_of((1 - parity) * 2 * rows_y, SUBLANES)
    odd_row = pl.multiple_of(parity * 2 * rows_y, SUBLANES)
    odd_inside = jnp.where((at_y > 0) & (at_y < count_y - 1), 1.0, 0.0)
    own_x, other_x = at_x * rows_x, (1 - at_x) * rows_x
    for ref, first_x, row, keep in (
        (own_ref, own_x, rows_y, None),
        (other_ref, other_x, rows_y, None),
        (even_ref, own_x, even_row, None),
        (even_other_ref, other_x, even_row, None),
        (odd_ref, own_x, odd_row, odd_inside),
        (odd_other_ref, other_x, odd_row, odd_inside),
    ):
        for at in range(rows_x):
            weight = jacobi_weight / (6.0 + ref[1, at])
            if keep is not None:
                weight = weight * keep
            weight_ref[first_x + at, pl.ds(row, rows_y), :] = weight
            drive_ref[first_x + at, pl.ds(row, rows_y), :] = weight * ref[0, at]

    gathered = jnp.sum(gathered_ref[...], axis=0)
    coarse = inverse_ref.shape[0]
    last = coarse // LANES
    cuts = cuts_of(gathered[last : last + 1], count_x, count_y)
    place = window_place(count_y, rows_y, (window_y, cells_z))
    planes = coarse_planes(gathered, inverse_ref, ids_ref, scale_factor, cuts, place)
    empty = jnp.zeros((window_y, cells_z), jnp.float32)
    for ref in (field_ref, spare_ref):
        ref[0] = empty
        ref[window_x + 1] = empty
    for at in range(window_x):
        field_ref[at + 1] = correction_of(planes, cuts, float(at))
    for _ in range(SWEEPS // 2):
        sweep(field_ref, spare_ref, weight_ref, drive_ref)
        sweep(spare_ref, field_ref, weight_ref, drive_ref)

    residual = []
    for at in range(rows_x):
        center, beside = neighbours(field_ref, own_x + at)
        center, beside = center[rows_y : 2 * rows_y], beside[rows_y : 2 * rows_y]
        residual.append(own_ref[0, at] - ((6.0 + own_ref[1, at]) * center - beside))
    row = restrict(jnp.concatenate(residual, axis=0), ids_ref, coarse)
    store_copies(out_ref, lane_rows(row) + [gathered[last : last + 1]])


def second_kernel(
    counts, scale_factor, pieces,
    field_ref, weight_ref, drive_ref, ids_ref, inverse_ref, gathered_ref, *rest,
):
    out_refs, (one_ref, two_ref) = rest[:pieces], rest[pieces:]
    count_x, count_y = counts
    window_x, window_y, cells_z = weight_ref.shape
    _, rows_y, chunk = out_refs[0].shape
    rows_x = out_refs[0].shape[0]
    own_x = lax.axis_index("gx") * rows_x
    gathered = jnp.sum(gathered_ref[...], axis=0)
    last = inverse_ref.shape[0] // LANES
    cuts = cuts_of(gathered_ref[0, last : last + 1], count_x, count_y)
    place = window_place(count_y, rows_y, (window_y, cells_z))
    planes = coarse_planes(gathered, inverse_ref, ids_ref, scale_factor, cuts, place)
    empty = jnp.zeros((window_y, cells_z), jnp.float32)
    for ref in (one_ref, two_ref):
        ref[0] = empty
        ref[window_x + 1] = empty
    for at in range(window_x):
        one_ref[at + 1] = field_ref[at + 1] + correction_of(planes, cuts, float(at))
    sweep(one_ref, two_ref, weight_ref, drive_ref)
    for _ in range(SWEEPS // 2 - 1):
        sweep(two_ref, one_ref, weight_ref, drive_ref)
        sweep(one_ref, two_ref, weight_ref, drive_ref)
    for at in range(rows_x):
        center, beside = neighbours(two_ref, own_x + at)
        value = (
            center * (1.0 - jacobi_weight)
            + drive_ref[own_x + at]
            + weight_ref[own_x + at] * beside
        )
        one_ref[at, pl.ds(0, rows_y), :] = value[rows_y : 2 * rows_y]
    me = lax.axis_index("grp")
    for turn in range(pieces):
        first = pl.multiple_of(lax.bitwise_xor(me, turn) * chunk, LANES)
        for at in range(rows_x):
            out_refs[turn][at] = one_ref[at, pl.ds(0, rows_y), pl.ds(first, chunk)]


def range_kernel(pieces, omega_ref, range_ref, *rest):
    snaps, (new_ref,) = rest[:pieces], rest[pieces:]
    rows_x = range_ref.shape[1]
    me = lax.axis_index("grp")
    slots = [lax.bitwise_xor(me, turn) for turn in range(pieces)]
    cells = [[snaps[turn][at] for at in range(rows_x)] for turn in range(pieces)]
    for at_row in range(range_ref.shape[0]):
        scales = [omega_ref[slots[turn], at_row] for turn in range(pieces)]
        for at in range(rows_x):
            value = range_ref[at_row, at]
            for turn in range(pieces):
                value = value + scales[turn] * cells[turn][at]
            new_ref[at_row, at] = value


def sketch_kernel(pieces, psi_ref, phi_ref, *rest):
    snaps, (out_ref,) = rest[:pieces], rest[pieces:]
    rows_x = psi_ref.shape[1]
    me = lax.axis_index("grp")
    slots = [lax.bitwise_xor(me, turn) for turn in range(pieces)]
    cells = [[snaps[turn][at] for at in range(rows_x)] for turn in range(pieces)]
    corange, core = psi_ref.shape[0], phi_ref.shape[0]
    ones = jnp.ones((SUBLANES, LANES), jnp.float32)
    totals = [[] for _ in range(pieces)]
    for ref, count in ((psi_ref, corange), (phi_ref, core)):
        for at_row in range(count):
            parts = [ref[at_row, at] for at in range(rows_x)]
            for turn in range(pieces):
                total = parts[0] * cells[turn][0]
                for at in range(1, rows_x):
                    total = total + parts[at] * cells[turn][at]
                totals[turn].append(jnp.sum(total, axis=0, keepdims=True))
    rest = jnp.zeros((LANES - corange - core, LANES), jnp.float32)
    for turn in range(pieces):
        row = dot_nt(ones, jnp.concatenate(totals[turn] + [rest], axis=0))[0:1]
        for copy in range(out_ref.shape[0]):
            out_ref[copy, pl.ds(slots[turn], 1), :] = row


def end_kernel(gathered_ref, xi_ref, core_ref, corange_out_ref, core_out_ref):
    corange = corange_out_ref.shape[1]
    core = core_ref.shape[0]
    total = jnp.sum(gathered_ref[...], axis=0)
    corange_out_ref[...] = total[:, :corange]
    images = total[:, corange : corange + core]
    core_out_ref[...] = core_ref[...] + dot_tn(images, xi_ref[...])


vmem = pl.BlockSpec(memory_space=pltpu.VMEM)
smem = pl.BlockSpec(memory_space=pltpu.SMEM)


def call(kernel, outs, inputs, scratch=(), specs=None):
    many = isinstance(outs, list)
    shapes = [jax.ShapeDtypeStruct(shape, jnp.float32) for shape in (outs if many else [outs])]
    result = pl.pallas_call(
        kernel,
        out_shape=shapes,
        in_specs=specs or [vmem] * len(inputs),
        out_specs=[vmem] * len(shapes),
        scratch_shapes=[pltpu.VMEM(shape, jnp.float32) for shape in scratch],
        compiler_params=pltpu.CompilerParams(vmem_limit_bytes=VMEM_BYTES),
    )(*inputs)
    return result if many else result[0]


def in_hbm(array):
    return pltpu.with_memory_space_constraint(array, pltpu.HBM)


def gather(copies, axes):
    return lax.all_to_all(copies, axes, 0, 0)


def fast_body(
    sources, diagonal, coarse_ids, coarse_inverse, omega_rows, psi, phi, xi_cols, range_sketch,
    core_sketch,
):
    source = sources[0]
    rows_x, rows_y, cells_z = source.shape
    counts = (lax.axis_size("gx"), lax.axis_size("gy"))
    groups = lax.axis_size("grp")
    count_x, count_y = counts
    coarse = coarse_inverse.shape[0]
    scale_factor = coarse / (rows_x * count_x * rows_y * count_y * cells_z)
    window = (rows_x * count_x, 3 * rows_y, cells_z)
    padded = (window[0] + 2,) + window[1:]
    copies = (count_x * count_y, coarse // LANES + 1, LANES)

    def partner_y(at, phase):
        found = at ^ 1 if phase == 0 else ((at + 1) ^ 1) - 1
        return found if 0 <= found < count_y else at

    def pairs(cross, phase):
        return [
            (x * count_y + y, (x ^ cross) * count_y + (y if phase is None else partner_y(y, phase)))
            for x in range(count_x)
            for y in range(count_y)
        ]

    mine, ids, inverse, begin = pl.pallas_call(
        begin_kernel,
        out_shape=[
            jax.ShapeDtypeStruct((2,) + source.shape, jnp.float32),
            jax.ShapeDtypeStruct(coarse_ids.shape, jnp.int32),
            jax.ShapeDtypeStruct(coarse_inverse.shape, jnp.float32),
            jax.ShapeDtypeStruct(copies, jnp.float32),
        ],
        in_specs=[pl.BlockSpec(memory_space=pltpu.HBM)] * 4,
        out_specs=[vmem] * 4,
        scratch_shapes=[pltpu.SemaphoreType.DMA((4,))],
        compiler_params=pltpu.CompilerParams(vmem_limit_bytes=VMEM_BYTES),
        name="begin",
    )(*map(in_hbm, (source, diagonal, coarse_ids, coarse_inverse)))
    gathered = gather(begin, ("gx", "gy"))
    others = [
        lax.ppermute(mine, ("gx", "gy"), pairs(cross, phase))
        for cross, phase in ((1, None), (0, 0), (1, 0), (0, 1), (1, 1))
    ]
    field, weight, drive, partial = call(
        functools.partial(first_kernel, counts, scale_factor),
        [padded, window, window, copies],
        (mine, *others, ids, inverse, gathered),
        scratch=[padded],
    )
    gathered = gather(partial, ("gx", "gy"))
    chunk = cells_z // groups
    pieces = call(
        functools.partial(second_kernel, counts, scale_factor, groups),
        [(rows_x, rows_y, chunk)] * groups,
        (field, weight, drive, ids, inverse, gathered),
        scratch=[padded, padded],
    )
    snaps = [pieces[0]] + [
        lax.ppermute(pieces[turn], "grp", [(at, at ^ turn) for at in range(groups)])
        for turn in range(1, groups)
    ]
    products = call(
        functools.partial(sketch_kernel, groups),
        (groups * count_x * count_y, groups, LANES),
        (psi, phi, *snaps),
    )
    gathered = gather(products, ("grp", "gx", "gy"))
    range_new = call(
        functools.partial(range_kernel, groups),
        range_sketch.shape,
        (omega_rows, range_sketch, *snaps),
        specs=[smem] + [vmem] * (1 + groups),
    )
    corange_cols, core_new = call(
        end_kernel, [(groups, psi.shape[0]), core_sketch.shape], (gathered, xi_cols.T, core_sketch)
    )
    return range_new, corange_cols.T, core_new


def with_halo(cells, sides, width):
    for axis, dim in sides:
        count = lax.axis_size(axis)
        ends = count - 1
        head = lax.slice_in_dim(cells, 0, width, axis=dim)
        tail = lax.slice_in_dim(cells, cells.shape[dim] - width, cells.shape[dim], axis=dim)
        cells = jnp.concatenate(
            [
                lax.ppermute(tail, axis, [(i, (i + 1) % count) for i in range(ends)]),
                cells,
                lax.ppermute(head, axis, [((i + 1) % count, i) for i in range(ends)]),
            ],
            axis=dim,
        )
    return cells


def neighbour_image(widened, diagonal):
    center = widened[1:-1, 1:-1]
    beside = widened[2:, 1:-1] + widened[:-2, 1:-1]
    beside = beside + widened[1:-1, 2:] + widened[1:-1, :-2]
    padded = jnp.pad(center, ((0, 0), (0, 0), (1, 1)))
    beside = beside + padded[:, :, 2:] + padded[:, :, :-2]
    return (center, (6.0 + diagonal) * center - beside)


def smooth_once(widened, source, diagonal):
    center, applied = neighbour_image(widened, diagonal)
    return center + jacobi_weight * (source - applied) / (6.0 + diagonal)


def axis_maps(coarse_ids):
    ranks_x = coarse_ids[:, 0, 0] // (XY_CUTS * Z_CUTS)
    ranks_y = coarse_ids[0, :, 0] // Z_CUTS % XY_CUTS
    ranks_z = coarse_ids[0, 0, :] % Z_CUTS
    cuts_xy = jnp.arange(XY_CUTS, dtype=jnp.int32)
    cuts_z = jnp.arange(Z_CUTS, dtype=jnp.int32)
    map_x = (ranks_x[:, None] == cuts_xy[None, :]).astype(jnp.float32)
    map_y = (ranks_y[:, None] == cuts_xy[None, :]).astype(jnp.float32)
    map_z = (ranks_z[:, None] == cuts_z[None, :]).astype(jnp.float32)
    return (map_x, map_y, map_z)


def restrict_cells(values, maps):
    map_x, map_y, map_z = maps
    rows_x, rows_y, cells_z = values.shape
    along_z = jnp.dot(values.reshape(rows_x * rows_y, cells_z), map_z, precision=highest)
    along_z = along_z.reshape(rows_x, rows_y, Z_CUTS)
    along_y = jnp.einsum("xyc,yb->xbc", along_z, map_y, precision=highest)
    along_x = jnp.einsum("xbc,xa->abc", along_y, map_x, precision=highest)
    return along_x.reshape(-1)


def prolong(correction, maps, extent):
    map_x, map_y, map_z = maps
    boxes = correction.reshape(XY_CUTS, XY_CUTS, Z_CUTS)
    over_x = jnp.einsum("abc,xa->xbc", boxes, map_x, precision=highest)
    over_y = jnp.einsum("xbc,yb->xyc", over_x, map_y, precision=highest)
    spread = jnp.dot(over_y.reshape(extent[0] * extent[1], Z_CUTS), map_z.T, precision=highest)
    return spread.reshape(extent)


def general_body(
    sources, diagonal, coarse_ids, coarse_inverse, omega_rows, psi, phi, xi_cols, range_sketch,
    core_sketch,
):
    source = sources[0]
    rows_x, rows_y, cells_z = source.shape
    coarse = coarse_inverse.shape[0]
    total_cells = rows_x * lax.axis_size("gx") * rows_y * lax.axis_size("gy") * cells_z
    scale_factor = coarse / total_cells
    maps = axis_maps(coarse_ids)
    sides = (("gx", 0), ("gy", 1))
    pressure = jnp.zeros_like(source)
    for outer_step in range(OUTER):
        if outer_step == 0:
            residual = source
        else:
            residual = source - neighbour_image(with_halo(pressure, sides, 1), diagonal)[1]
        coarse_rhs = lax.psum(restrict_cells(residual, maps), ("gx", "gy"))
        correction = jnp.dot(coarse_inverse, coarse_rhs * scale_factor, precision=highest)
        pressure = pressure + prolong(correction, maps, source.shape)
        for _ in range(SWEEPS):
            pressure = smooth_once(with_halo(pressure, sides, 1), source, diagonal)
    snapshot = lax.all_to_all(pressure[None], "grp", split_axis=3, concat_axis=0, tiled=True)
    columns = snapshot.reshape(snapshot.shape[0], -1)
    range_flat = range_sketch.reshape(range_sketch.shape[0], -1)
    range_new = range_flat + jnp.einsum("tk,tc->kc", omega_rows, columns, precision=highest)
    corange_part = jnp.einsum(
        "lc,tc->lt", psi.reshape(psi.shape[0], -1), columns, precision=highest
    )
    core_part = jnp.einsum("sc,tc->st", phi.reshape(phi.shape[0], -1), columns, precision=highest)
    corange_cols, core_images = lax.psum((corange_part, core_part), ("grp", "gx", "gy"))
    core_new = core_sketch + jnp.dot(core_images, xi_cols.T, precision=highest)
    return (range_new.reshape(range_sketch.shape), corange_cols, core_new)


def body(*arrays):
    _, rows_y, cells_z = arrays[1].shape
    coarse, groups = arrays[3].shape[0], lax.axis_size("grp")
    fits = (
        lax.axis_size("gx") == 2
        and lax.axis_size("gy") % 2 == 0
        and rows_y >= OUTER * SWEEPS
        and rows_y % SUBLANES == 0
        and groups & (groups - 1) == 0
        and groups <= SUBLANES
        and cells_z % (groups * LANES) == 0
        and cells_z // groups == LANES
        and coarse % LANES == 0
        and arrays[5].shape[0] + arrays[6].shape[0] <= LANES
    )
    if not fits:
        return general_body(*arrays)
    return fast_body(*arrays)


def solution(mesh):
    return jax.shard_map(
        body,
        mesh=mesh,
        in_specs=(
            P("grp", "gx", "gy", None),
            P("gx", "gy", None),
            P("gx", "gy", None),
            P(),
            P(),
            P(None, "gx", "gy", "grp"),
            P(None, "gx", "gy", "grp"),
            P(),
            P(None, "gx", "gy", "grp"),
            P(),
        ),
        out_specs=(P(None, "gx", "gy", "grp"), P(), P()),
        check_vma=False,
    )
```

```python
import functools

import jax
import jax.numpy as jnp
from jax import lax
from jax.experimental import pallas as pl
from jax.experimental.pallas import tpu as pltpu
from jax.sharding import PartitionSpec as P


OUTER = 2
SWEEPS = 4
XY_CUTS = 4
Z_CUTS = 16
LANES = 128
SUBLANES = 8
VMEM_BYTES = 16 * 2**20

jacobi_weight = 2.0 / 3.0
highest = lax.Precision.HIGHEST


def dot_nn(a, b):
    return lax.dot_general(
        a, b, (((1,), (0,)), ((), ())), precision=highest, preferred_element_type=jnp.float32
    )


def dot_nt(a, b):
    return lax.dot_general(
        a, b, (((1,), (1,)), ((), ())), precision=highest, preferred_element_type=jnp.float32
    )


def dot_tn(a, b):
    return lax.dot_general(
        a, b, (((0,), (0,)), ((), ())), precision=highest, preferred_element_type=jnp.float32
    )


def iota(shape, dim):
    return lax.broadcasted_iota(jnp.int32, shape, dim)


def spread_map(ids_ref, coarse):
    cells_z = ids_ref.shape[2]
    ranks = lax.bitwise_and(ids_ref[0, 0:1, :], Z_CUTS - 1)
    rows = lax.bitwise_and(iota((coarse, cells_z), 0), Z_CUTS - 1)
    return (rows == ranks).astype(jnp.float32)


def column_map(ids_ref):
    rows_x, rows_y, _ = ids_ref.shape
    boxes = XY_CUTS * XY_CUTS
    tile = ids_ref[:, :, :LANES].reshape(rows_x * rows_y, LANES) // Z_CUTS
    turned = tile.astype(jnp.float32).T[:boxes]
    return (turned == iota(turned.shape, 0).astype(jnp.float32)).astype(jnp.float32)


def restrict(values, ids_ref, coarse):
    boxes = XY_CUTS * XY_CUTS
    by_box = dot_nn(column_map(ids_ref), values)
    wide = dot_nt(by_box, spread_map(ids_ref, coarse))
    own = iota((boxes, coarse), 1) // Z_CUTS == iota((boxes, coarse), 0)
    return jnp.sum(jnp.where(own, wide, 0.0), axis=0, keepdims=True)


def store_copies(out_ref, rows):
    for copy in range(out_ref.shape[0]):
        for at, row in enumerate(rows):
            out_ref[copy, at : at + 1, :] = row


def lane_rows(row):
    return [row[:, at : at + LANES] for at in range(0, row.shape[1], LANES)]


def begin_kernel(
    source_from, diagonal_from, ids_from, inverse_from,
    mine_ref, ids_ref, inverse_ref, out_ref, arrived,
):
    loads = [
        pltpu.make_async_copy(source, target, arrived.at[at])
        for at, (source, target) in enumerate(
            (
                (ids_from, ids_ref),
                (source_from, mine_ref.at[0]),
                (diagonal_from, mine_ref.at[1]),
                (inverse_from, inverse_ref),
            )
        )
    ]
    for load in loads:
        load.start()
    coarse = inverse_ref.shape[0]
    rows_x, rows_y, cells_z = ids_ref.shape
    loads[0].wait()
    loads[1].wait()
    row = restrict(mine_ref[0].reshape(rows_x * rows_y, cells_z), ids_ref, coarse)
    lanes = iota((1, LANES), 1)
    tile = ids_ref[:, :, :LANES] // Z_CUTS
    ranks_x = tile[:, 0:1, :] // XY_CUTS
    ranks_y = lax.bitwise_and(tile[0], XY_CUTS - 1)
    below_x = jnp.sum((ranks_x <= lanes[None]).astype(jnp.float32), axis=0)
    below_y = jnp.sum((ranks_y <= lanes - XY_CUTS).astype(jnp.float32), axis=0, keepdims=True)
    rows = lane_rows(row) + [jnp.where(lanes < XY_CUTS, below_x, below_y)]
    for at, part in enumerate(rows):
        out_ref[at : at + 1, :] = part
    loads[2].wait()
    loads[3].wait()


def coarse_planes(gathered, inverse_ref, ids_ref, scale_factor, cuts, place):
    coarse = inverse_ref.shape[0]
    boxes = XY_CUTS * XY_CUTS
    _, cut_y = cuts
    row = jnp.concatenate(
        [gathered[part : part + 1, :] for part in range(coarse // LANES)], axis=1
    )
    row = jnp.broadcast_to(row * scale_factor, (SUBLANES, coarse))
    solved = dot_nt(row, inverse_ref[...])[0:1]
    own = iota((boxes, coarse), 1) // Z_CUTS == iota((boxes, coarse), 0)
    along_z = dot_nn(jnp.where(own, solved, 0.0), spread_map(ids_ref, coarse))
    place_y, inside = place
    planes = []
    for box_x in range(XY_CUTS):
        first = box_x * XY_CUTS
        plane = jnp.broadcast_to(along_z[first : first + 1], place_y.shape)
        for box_y in range(1, XY_CUTS):
            line = along_z[first + box_y : first + box_y + 1]
            plane = jnp.where(place_y >= cut_y[box_y - 1], line, plane)
        planes.append(jnp.where(inside, plane, 0.0))
    return planes


def correction_of(planes, cuts, place_x):
    cut_x, _ = cuts
    value = planes[0]
    for box_x in range(1, XY_CUTS):
        value = jnp.where(cut_x[box_x - 1] <= place_x, planes[box_x], value)
    return value


def cuts_of(row, count_x, count_y):
    cut_x = [row[:, at : at + 1] * (1.0 / count_y) for at in range(XY_CUTS - 1)]
    cut_y = [row[:, XY_CUTS + at : XY_CUTS + at + 1] * (1.0 / count_x) for at in range(XY_CUTS - 1)]
    return cut_x, cut_y


def beside_z(values):
    cells_z = values.shape[-1]
    lanes = iota(values.shape, values.ndim - 1)
    ahead = pltpu.roll(values, cells_z - 1, values.ndim - 1)
    behind = pltpu.roll(values, 1, values.ndim - 1)
    return jnp.where(lanes == cells_z - 1, 0.0, ahead) + jnp.where(lanes == 0, 0.0, behind)


def beside_y(values):
    rows = values.shape[0]
    return pltpu.roll(values, rows - 1, 0) + pltpu.roll(values, 1, 0)


def neighbours(field_ref, at):
    center = field_ref[at + 1]
    return center, field_ref[at] + field_ref[at + 2] + beside_y(center) + beside_z(center)


def sweep(from_ref, to_ref, weight_ref, drive_ref):
    for at in range(weight_ref.shape[0]):
        center, beside = neighbours(from_ref, at)
        to_ref[at + 1] = (
            center * (1.0 - jacobi_weight) + drive_ref[at] + weight_ref[at] * beside
        )


def window_place(count_y, rows_y, shape):
    place_y = iota(shape, 0) + (lax.axis_index("gy") - 1) * rows_y
    inside = (place_y >= 0) & (place_y < rows_y * count_y)
    return place_y.astype(jnp.float32), inside


def first_kernel(
    counts, scale_factor, own_ref, other_ref, even_ref, even_other_ref, odd_ref, odd_other_ref,
    ids_ref, inverse_ref, gathered_ref,
    field_ref, weight_ref, drive_ref, out_ref, spare_ref,
):
    count_x, count_y = counts
    _, rows_x, rows_y, cells_z = own_ref.shape
    window_x, window_y, _ = weight_ref.shape
    at_x, at_y = lax.axis_index("gx"), lax.axis_index("gy")
    parity = lax.rem(at_y, 2)
    even_row = pl.multiple_of((1 - parity) * 2 * rows_y, SUBLANES)
    odd_row = pl.multiple_of(parity * 2 * rows_y, SUBLANES)
    odd_inside = jnp.where((at_y > 0) & (at_y < count_y - 1), 1.0, 0.0)
    own_x, other_x = at_x * rows_x, (1 - at_x) * rows_x
    for ref, first_x, row, keep in (
        (own_ref, own_x, rows_y, None),
        (other_ref, other_x, rows_y, None),
        (even_ref, own_x, even_row, None),
        (even_other_ref, other_x, even_row, None),
        (odd_ref, own_x, odd_row, odd_inside),
        (odd_other_ref, other_x, odd_row, odd_inside),
    ):
        for at in range(rows_x):
            weight = jacobi_weight / (6.0 + ref[1, at])
            if keep is not None:
                weight = weight * keep
            weight_ref[first_x + at, pl.ds(row, rows_y), :] = weight
            drive_ref[first_x + at, pl.ds(row, rows_y), :] = weight * ref[0, at]

    gathered = gathered_ref[...]
    coarse = inverse_ref.shape[0]
    last = coarse // LANES
    cuts = cuts_of(gathered[last : last + 1], count_x, count_y)
    place = window_place(count_y, rows_y, (window_y, cells_z))
    planes = coarse_planes(gathered, inverse_ref, ids_ref, scale_factor, cuts, place)
    empty = jnp.zeros((window_y, cells_z), jnp.float32)
    for ref in (field_ref, spare_ref):
        ref[0] = empty
        ref[window_x + 1] = empty
    for at in range(window_x):
        field_ref[at + 1] = correction_of(planes, cuts, float(at))
    for _ in range(SWEEPS // 2):
        sweep(field_ref, spare_ref, weight_ref, drive_ref)
        sweep(spare_ref, field_ref, weight_ref, drive_ref)

    residual = []
    for at in range(rows_x):
        center, beside = neighbours(field_ref, own_x + at)
        center, beside = center[rows_y : 2 * rows_y], beside[rows_y : 2 * rows_y]
        residual.append(own_ref[0, at] - ((6.0 + own_ref[1, at]) * center - beside))
    row = restrict(jnp.concatenate(residual, axis=0), ids_ref, coarse)
    store_copies(out_ref, lane_rows(row) + [gathered[last : last + 1]])


def second_kernel(
    counts, scale_factor, pieces,
    field_ref, weight_ref, drive_ref, ids_ref, inverse_ref, gathered_ref, *rest,
):
    out_refs, (one_ref, two_ref) = rest[:pieces], rest[pieces:]
    count_x, count_y = counts
    window_x, window_y, cells_z = weight_ref.shape
    _, rows_y, chunk = out_refs[0].shape
    rows_x = out_refs[0].shape[0]
    own_x = lax.axis_index("gx") * rows_x
    gathered = jnp.sum(gathered_ref[...], axis=0)
    last = inverse_ref.shape[0] // LANES
    cuts = cuts_of(gathered_ref[0, last : last + 1], count_x, count_y)
    place = window_place(count_y, rows_y, (window_y, cells_z))
    planes = coarse_planes(gathered, inverse_ref, ids_ref, scale_factor, cuts, place)
    empty = jnp.zeros((window_y, cells_z), jnp.float32)
    for ref in (one_ref, two_ref):
        ref[0] = empty
        ref[window_x + 1] = empty
    for at in range(window_x):
        one_ref[at + 1] = field_ref[at + 1] + correction_of(planes, cuts, float(at))
    sweep(one_ref, two_ref, weight_ref, drive_ref)
    for _ in range(SWEEPS // 2 - 1):
        sweep(two_ref, one_ref, weight_ref, drive_ref)
        sweep(one_ref, two_ref, weight_ref, drive_ref)
    for at in range(rows_x):
        center, beside = neighbours(two_ref, own_x + at)
        value = (
            center * (1.0 - jacobi_weight)
            + drive_ref[own_x + at]
            + weight_ref[own_x + at] * beside
        )
        one_ref[at, pl.ds(0, rows_y), :] = value[rows_y : 2 * rows_y]
    me = lax.axis_index("grp")
    for turn in range(pieces):
        first = pl.multiple_of(lax.bitwise_xor(me, turn) * chunk, LANES)
        for at in range(rows_x):
            out_refs[turn][at] = one_ref[at, pl.ds(0, rows_y), pl.ds(first, chunk)]


def range_kernel(pieces, omega_ref, range_ref, *rest):
    snaps, (new_ref,) = rest[:pieces], rest[pieces:]
    rows_x = range_ref.shape[1]
    me = lax.axis_index("grp")
    slots = [lax.bitwise_xor(me, turn) for turn in range(pieces)]
    cells = [[snaps[turn][at] for at in range(rows_x)] for turn in range(pieces)]
    for at_row in range(range_ref.shape[0]):
        scales = [omega_ref[slots[turn], at_row] for turn in range(pieces)]
        for at in range(rows_x):
            value = range_ref[at_row, at]
            for turn in range(pieces):
                value = value + scales[turn] * cells[turn][at]
            new_ref[at_row, at] = value


def sketch_kernel(pieces, psi_ref, phi_ref, *rest):
    snaps, (out_ref,) = rest[:pieces], rest[pieces:]
    rows_x = psi_ref.shape[1]
    me = lax.axis_index("grp")
    slots = [lax.bitwise_xor(me, turn) for turn in range(pieces)]
    cells = [[snaps[turn][at] for at in range(rows_x)] for turn in range(pieces)]
    corange, core = psi_ref.shape[0], phi_ref.shape[0]
    ones = jnp.ones((SUBLANES, LANES), jnp.float32)
    totals = [[] for _ in range(pieces)]
    for ref, count in ((psi_ref, corange), (phi_ref, core)):
        for at_row in range(count):
            parts = [ref[at_row, at] for at in range(rows_x)]
            for turn in range(pieces):
                total = parts[0] * cells[turn][0]
                for at in range(1, rows_x):
                    total = total + parts[at] * cells[turn][at]
                totals[turn].append(jnp.sum(total, axis=0, keepdims=True))
    rest = jnp.zeros((LANES - corange - core, LANES), jnp.float32)
    for turn in range(pieces):
        row = dot_nt(ones, jnp.concatenate(totals[turn] + [rest], axis=0))[0:1]
        for copy in range(out_ref.shape[0]):
            out_ref[copy, pl.ds(slots[turn], 1), :] = row


def end_kernel(gathered_ref, xi_ref, core_ref, corange_out_ref, core_out_ref):
    corange = corange_out_ref.shape[1]
    core = core_ref.shape[0]
    total = jnp.sum(gathered_ref[...], axis=0)
    corange_out_ref[...] = total[:, :corange]
    images = total[:, corange : corange + core]
    core_out_ref[...] = core_ref[...] + dot_tn(images, xi_ref[...])


vmem = pl.BlockSpec(memory_space=pltpu.VMEM)
smem = pl.BlockSpec(memory_space=pltpu.SMEM)


def call(kernel, outs, inputs, scratch=(), specs=None):
    many = isinstance(outs, list)
    shapes = [jax.ShapeDtypeStruct(shape, jnp.float32) for shape in (outs if many else [outs])]
    result = pl.pallas_call(
        kernel,
        out_shape=shapes,
        in_specs=specs or [vmem] * len(inputs),
        out_specs=[vmem] * len(shapes),
        scratch_shapes=[pltpu.VMEM(shape, jnp.float32) for shape in scratch],
        compiler_params=pltpu.CompilerParams(vmem_limit_bytes=VMEM_BYTES),
    )(*inputs)
    return result if many else result[0]


def in_hbm(array):
    return pltpu.with_memory_space_constraint(array, pltpu.HBM)


def gather(copies, axes):
    return lax.all_to_all(copies, axes, 0, 0)


def fast_body(
    sources, diagonal, coarse_ids, coarse_inverse, omega_rows, psi, phi, xi_cols, range_sketch,
    core_sketch,
):
    source = sources[0]
    rows_x, rows_y, cells_z = source.shape
    counts = (lax.axis_size("gx"), lax.axis_size("gy"))
    groups = lax.axis_size("grp")
    count_x, count_y = counts
    coarse = coarse_inverse.shape[0]
    scale_factor = coarse / (rows_x * count_x * rows_y * count_y * cells_z)
    window = (rows_x * count_x, 3 * rows_y, cells_z)
    padded = (window[0] + 2,) + window[1:]
    copies = (count_x * count_y, coarse // LANES + 1, LANES)

    def partner_y(at, phase):
        found = at ^ 1 if phase == 0 else ((at + 1) ^ 1) - 1
        return found if 0 <= found < count_y else at

    def pairs(cross, phase):
        return [
            (x * count_y + y, (x ^ cross) * count_y + (y if phase is None else partner_y(y, phase)))
            for x in range(count_x)
            for y in range(count_y)
        ]

    mine, ids, inverse, begin = pl.pallas_call(
        begin_kernel,
        out_shape=[
            jax.ShapeDtypeStruct((2,) + source.shape, jnp.float32),
            jax.ShapeDtypeStruct(coarse_ids.shape, jnp.int32),
            jax.ShapeDtypeStruct(coarse_inverse.shape, jnp.float32),
            jax.ShapeDtypeStruct(copies[1:], jnp.float32),
        ],
        in_specs=[pl.BlockSpec(memory_space=pltpu.HBM)] * 4,
        out_specs=[vmem] * 4,
        scratch_shapes=[pltpu.SemaphoreType.DMA((4,))],
        compiler_params=pltpu.CompilerParams(vmem_limit_bytes=VMEM_BYTES),
        name="begin",
    )(*map(in_hbm, (source, diagonal, coarse_ids, coarse_inverse)))
    others = []
    for at, (cross, phase) in enumerate(((1, None), (0, 0), (0, 0), (0, 1), (0, 1))):
        sent = others[0] if at in (2, 4) else mine
        others.append(lax.ppermute(sent, ("gx", "gy"), pairs(cross, phase)))
    gathered = begin
    turns = [("gx", count_x, 1)] + [("gy", count_y, 1 << bit) for bit in range(count_y.bit_length() - 1)]
    for axis, count, bit in turns:
        gathered = gathered + lax.ppermute(gathered, axis, [(i, i ^ bit) for i in range(count)])
    field, weight, drive, partial = call(
        functools.partial(first_kernel, counts, scale_factor),
        [padded, window, window, copies],
        (mine, *others, ids, inverse, gathered),
        scratch=[padded],
    )
    gathered = gather(partial, ("gx", "gy"))
    chunk = cells_z // groups
    pieces = call(
        functools.partial(second_kernel, counts, scale_factor, groups),
        [(rows_x, rows_y, chunk)] * groups,
        (field, weight, drive, ids, inverse, gathered),
        scratch=[padded, padded],
    )
    snaps = [pieces[0]] + [
        lax.ppermute(pieces[turn], "grp", [(at, at ^ turn) for at in range(groups)])
        for turn in range(1, groups)
    ]
    products = call(
        functools.partial(sketch_kernel, groups),
        (groups * count_x * count_y, groups, LANES),
        (psi, phi, *snaps),
    )
    gathered = gather(products, ("grp", "gx", "gy"))
    range_new = call(
        functools.partial(range_kernel, groups),
        range_sketch.shape,
        (omega_rows, range_sketch, *snaps),
        specs=[smem] + [vmem] * (1 + groups),
    )
    corange_cols, core_new = call(
        end_kernel, [(groups, psi.shape[0]), core_sketch.shape], (gathered, xi_cols.T, core_sketch)
    )
    return range_new, corange_cols.T, core_new


def with_halo(cells, sides, width):
    for axis, dim in sides:
        count = lax.axis_size(axis)
        ends = count - 1
        head = lax.slice_in_dim(cells, 0, width, axis=dim)
        tail = lax.slice_in_dim(cells, cells.shape[dim] - width, cells.shape[dim], axis=dim)
        cells = jnp.concatenate(
            [
                lax.ppermute(tail, axis, [(i, (i + 1) % count) for i in range(ends)]),
                cells,
                lax.ppermute(head, axis, [((i + 1) % count, i) for i in range(ends)]),
            ],
            axis=dim,
        )
    return cells


def neighbour_image(widened, diagonal):
    center = widened[1:-1, 1:-1]
    beside = widened[2:, 1:-1] + widened[:-2, 1:-1]
    beside = beside + widened[1:-1, 2:] + widened[1:-1, :-2]
    padded = jnp.pad(center, ((0, 0), (0, 0), (1, 1)))
    beside = beside + padded[:, :, 2:] + padded[:, :, :-2]
    return (center, (6.0 + diagonal) * center - beside)


def smooth_once(widened, source, diagonal):
    center, applied = neighbour_image(widened, diagonal)
    return center + jacobi_weight * (source - applied) / (6.0 + diagonal)


def axis_maps(coarse_ids):
    ranks_x = coarse_ids[:, 0, 0] // (XY_CUTS * Z_CUTS)
    ranks_y = coarse_ids[0, :, 0] // Z_CUTS % XY_CUTS
    ranks_z = coarse_ids[0, 0, :] % Z_CUTS
    cuts_xy = jnp.arange(XY_CUTS, dtype=jnp.int32)
    cuts_z = jnp.arange(Z_CUTS, dtype=jnp.int32)
    map_x = (ranks_x[:, None] == cuts_xy[None, :]).astype(jnp.float32)
    map_y = (ranks_y[:, None] == cuts_xy[None, :]).astype(jnp.float32)
    map_z = (ranks_z[:, None] == cuts_z[None, :]).astype(jnp.float32)
    return (map_x, map_y, map_z)


def restrict_cells(values, maps):
    map_x, map_y, map_z = maps
    rows_x, rows_y, cells_z = values.shape
    along_z = jnp.dot(values.reshape(rows_x * rows_y, cells_z), map_z, precision=highest)
    along_z = along_z.reshape(rows_x, rows_y, Z_CUTS)
    along_y = jnp.einsum("xyc,yb->xbc", along_z, map_y, precision=highest)
    along_x = jnp.einsum("xbc,xa->abc", along_y, map_x, precision=highest)
    return along_x.reshape(-1)


def prolong(correction, maps, extent):
    map_x, map_y, map_z = maps
    boxes = correction.reshape(XY_CUTS, XY_CUTS, Z_CUTS)
    over_x = jnp.einsum("abc,xa->xbc", boxes, map_x, precision=highest)
    over_y = jnp.einsum("xbc,yb->xyc", over_x, map_y, precision=highest)
    spread = jnp.dot(over_y.reshape(extent[0] * extent[1], Z_CUTS), map_z.T, precision=highest)
    return spread.reshape(extent)


def general_body(
    sources, diagonal, coarse_ids, coarse_inverse, omega_rows, psi, phi, xi_cols, range_sketch,
    core_sketch,
):
    source = sources[0]
    rows_x, rows_y, cells_z = source.shape
    coarse = coarse_inverse.shape[0]
    total_cells = rows_x * lax.axis_size("gx") * rows_y * lax.axis_size("gy") * cells_z
    scale_factor = coarse / total_cells
    maps = axis_maps(coarse_ids)
    sides = (("gx", 0), ("gy", 1))
    pressure = jnp.zeros_like(source)
    for outer_step in range(OUTER):
        if outer_step == 0:
            residual = source
        else:
            residual = source - neighbour_image(with_halo(pressure, sides, 1), diagonal)[1]
        coarse_rhs = lax.psum(restrict_cells(residual, maps), ("gx", "gy"))
        correction = jnp.dot(coarse_inverse, coarse_rhs * scale_factor, precision=highest)
        pressure = pressure + prolong(correction, maps, source.shape)
        for _ in range(SWEEPS):
            pressure = smooth_once(with_halo(pressure, sides, 1), source, diagonal)
    snapshot = lax.all_to_all(pressure[None], "grp", split_axis=3, concat_axis=0, tiled=True)
    columns = snapshot.reshape(snapshot.shape[0], -1)
    range_flat = range_sketch.reshape(range_sketch.shape[0], -1)
    range_new = range_flat + jnp.einsum("tk,tc->kc", omega_rows, columns, precision=highest)
    corange_part = jnp.einsum(
        "lc,tc->lt", psi.reshape(psi.shape[0], -1), columns, precision=highest
    )
    core_part = jnp.einsum("sc,tc->st", phi.reshape(phi.shape[0], -1), columns, precision=highest)
    corange_cols, core_images = lax.psum((corange_part, core_part), ("grp", "gx", "gy"))
    core_new = core_sketch + jnp.dot(core_images, xi_cols.T, precision=highest)
    return (range_new.reshape(range_sketch.shape), corange_cols, core_new)


def body(*arrays):
    _, rows_y, cells_z = arrays[1].shape
    coarse, groups = arrays[3].shape[0], lax.axis_size("grp")
    fits = (
        lax.axis_size("gx") == 2
        and lax.axis_size("gy") & (lax.axis_size("gy") - 1) == 0
        and lax.axis_size("gy") > 1
        and rows_y >= OUTER * SWEEPS
        and rows_y % SUBLANES == 0
        and groups & (groups - 1) == 0
        and groups <= SUBLANES
        and cells_z % (groups * LANES) == 0
        and cells_z // groups == LANES
        and coarse % LANES == 0
        and arrays[5].shape[0] + arrays[6].shape[0] <= LANES
    )
    if not fits:
        return general_body(*arrays)
    return fast_body(*arrays)


def solution(mesh):
    return jax.shard_map(
        body,
        mesh=mesh,
        in_specs=(
            P("grp", "gx", "gy", None),
            P("gx", "gy", None),
            P("gx", "gy", None),
            P(),
            P(),
            P(None, "gx", "gy", "grp"),
            P(None, "gx", "gy", "grp"),
            P(),
            P(None, "gx", "gy", "grp"),
            P(),
        ),
        out_specs=(P(None, "gx", "gy", "grp"), P(), P()),
        check_vma=False,
    )
```

```python
import functools

import jax
import jax.numpy as jnp
from jax import lax
from jax.experimental import pallas as pl
from jax.experimental.pallas import tpu as pltpu
from jax.sharding import PartitionSpec as P


OUTER = 2
SWEEPS = 4
XY_CUTS = 4
Z_CUTS = 16
XY_BITS = XY_CUTS.bit_length() - 1
Z_BITS = Z_CUTS.bit_length() - 1
LANES = 128
SUBLANES = 8
VMEM_BYTES = 16 * 2**20

jacobi_weight = 2.0 / 3.0
highest = lax.Precision.HIGHEST


def dot_nt(a, b):
    return lax.dot_general(
        a, b, (((1,), (1,)), ((), ())), precision=highest, preferred_element_type=jnp.float32
    )


def dot_tn(a, b):
    return lax.dot_general(
        a, b, (((0,), (0,)), ((), ())), precision=highest, preferred_element_type=jnp.float32
    )


def iota(shape, dim):
    return lax.broadcasted_iota(jnp.int32, shape, dim)


def store_copies(out_ref, rows):
    for copy in range(out_ref.shape[0]):
        for at, row in enumerate(rows):
            out_ref[copy, at : at + 1, :] = row


def box_of(ids_ref, at):
    return lax.shift_right_logical(ids_ref[at, :, :LANES], Z_BITS)


def restrict(values, ids_ref, planes, coarse):
    cells_z = values.shape[1]
    rows_y = ids_ref.shape[1]
    ranks = lax.bitwise_and(ids_ref[0, 0:1, :], Z_CUTS - 1)
    members = lax.bitwise_and(iota((LANES, cells_z), 0), Z_CUTS - 1) == ranks
    sums = dot_nt(values, members.astype(jnp.float32))
    lane_box = lax.shift_right_logical(iota((rows_y, LANES), 1), Z_BITS)
    rows = []
    for part in range(coarse // LANES):
        total = None
        for at, plane in enumerate(planes):
            own = box_of(ids_ref, plane) == lane_box + part * (LANES // Z_CUTS)
            kept = jnp.where(own, sums[at * rows_y : (at + 1) * rows_y], 0.0)
            total = kept if total is None else total + kept
        rows.append(jnp.sum(total, axis=0, keepdims=True))
    return rows


def begin_kernel(
    source_from, diagonal_from, ids_from, inverse_from,
    mine_ref, ids_ref, inverse_ref, out_ref, arrived,
):
    loads = [
        pltpu.make_async_copy(source, target, arrived.at[at])
        for at, (source, target) in enumerate(
            (
                (ids_from, ids_ref),
                (source_from, mine_ref.at[0]),
                (diagonal_from, mine_ref.at[1]),
                (inverse_from, inverse_ref),
            )
        )
    ]
    for load in loads:
        load.start()
    coarse = inverse_ref.shape[0]
    rows_x, rows_y, cells_z = ids_ref.shape
    loads[0].wait()
    lanes = iota((1, LANES), 1)
    boxes = [box_of(ids_ref, at) for at in range(rows_x)]
    below_x = jnp.zeros((1, LANES), jnp.float32)
    for box in boxes:
        below_x = below_x + (lax.shift_right_logical(box[0:1], XY_BITS) <= lanes).astype(jnp.float32)
    ranks_y = lax.bitwise_and(boxes[0], XY_CUTS - 1)
    below_y = jnp.sum((ranks_y <= lanes - XY_CUTS).astype(jnp.float32), axis=0, keepdims=True)
    loads[1].wait()
    rows = restrict(
        mine_ref[0].reshape(rows_x * rows_y, cells_z), ids_ref, range(rows_x), coarse
    ) + [jnp.where(lanes < XY_CUTS, below_x, below_y)]
    for at, part in enumerate(rows):
        out_ref[at : at + 1, :] = part
    loads[2].wait()
    loads[3].wait()


def coarse_planes(rows, inverse_ref, ids_ref, scale_factor, cut_y, place):
    coarse = inverse_ref.shape[0]
    cells_z = ids_ref.shape[2]
    per_part = LANES // Z_CUTS
    row = jnp.broadcast_to(jnp.concatenate(rows, axis=1) * scale_factor, (SUBLANES, coarse))
    solved = dot_nt(row, inverse_ref[...])
    shape = (per_part, LANES)
    own = lax.shift_right_logical(iota(shape, 1), Z_BITS) == iota(shape, 0)
    lines = []
    for part in range(coarse // LANES):
        values = jnp.where(own, solved[:per_part, part * LANES : (part + 1) * LANES], 0.0)
        shift = LANES // 2
        while shift >= Z_CUTS:
            values = values + pltpu.roll(values, shift, 1)
            shift //= 2
        along_z = jnp.concatenate(
            [
                jnp.take_along_axis(
                    values,
                    lax.bitwise_and(ids_ref[0, :per_part, at : at + LANES], Z_CUTS - 1),
                    axis=1,
                )
                for at in range(0, cells_z, LANES)
            ],
            axis=1,
        )
        lines.extend(along_z[at : at + 1] for at in range(per_part))
    place_y, inside = place
    planes = []
    for box_x in range(XY_CUTS):
        first = box_x * XY_CUTS
        plane = jnp.broadcast_to(lines[first], place_y.shape)
        for box_y in range(1, XY_CUTS):
            plane = jnp.where(place_y >= cut_y[box_y - 1], lines[first + box_y], plane)
        planes.append(jnp.where(inside, plane, 0.0))
    return planes


def correction_of(planes, cut_x, place_x):
    value = planes[0]
    for box_x in range(1, XY_CUTS):
        value = jnp.where(cut_x[box_x - 1] <= place_x, planes[box_x], value)
    return value


def cuts_of(row, count_x, count_y):
    cut_x = [row[:, at : at + 1] * (1.0 / count_y) for at in range(XY_CUTS - 1)]
    cut_y = [row[:, XY_CUTS + at : XY_CUTS + at + 1] * (1.0 / count_x) for at in range(XY_CUTS - 1)]
    return cut_x, cut_y


def beside_z(values):
    lanes = iota((values.shape[0], LANES), 1)
    tiles = [values[:, at : at + LANES] for at in range(0, values.shape[1], LANES)]
    empty = jnp.zeros_like(tiles[0])
    ahead = [pltpu.roll(tile, LANES - 1, 1) for tile in tiles] + [empty]
    behind = [empty] + [pltpu.roll(tile, 1, 1) for tile in tiles]
    return jnp.concatenate(
        [
            jnp.where(lanes == LANES - 1, ahead[at + 1], ahead[at])
            + jnp.where(lanes == 0, behind[at], behind[at + 1])
            for at in range(len(tiles))
        ],
        axis=1,
    )


def beside_y(values):
    rows = values.shape[0]
    return pltpu.roll(values, rows - 1, 0) + pltpu.roll(values, 1, 0)


def neighbours(field_ref, at, rows=None):
    center = field_ref[at + 1]
    along_y = beside_y(center)
    if rows is None:
        rows = slice(0, center.shape[0])
    center = center[rows]
    across = field_ref[at, rows, :] + field_ref[at + 2, rows, :]
    return center, across + along_y[rows] + beside_z(center)


def smooth(field_ref, weight_ref, drive_ref, at, rows=None):
    center, beside = neighbours(field_ref, at, rows)
    rows = slice(None) if rows is None else rows
    kept = center * (1.0 - jacobi_weight) + drive_ref[at, rows, :]
    return kept + weight_ref[at, rows, :] * beside


def sweep(from_ref, to_ref, weight_ref, drive_ref, rows_x, reach):
    window_x, window_y, _ = weight_ref.shape
    own_rows = slice(window_y // 3, 2 * window_y // 3)
    for at in range(window_x):
        away = max(0, at - rows_x + 1)
        if away > reach:
            continue
        if away == reach:
            to_ref[at + 1, own_rows, :] = smooth(from_ref, weight_ref, drive_ref, at, own_rows)
        else:
            to_ref[at + 1] = smooth(from_ref, weight_ref, drive_ref, at)


def window_place(count_y, rows_y, shape):
    place_y = iota(shape, 0) + (lax.axis_index("gy") - 1) * rows_y
    inside = (place_y >= 0) & (place_y < rows_y * count_y)
    return place_y.astype(jnp.float32), inside


def mirrored(at, last):
    return jnp.where(lax.axis_index("gx") == 0, at, last - at)


def add_correction(planes, cut_x, window_x, planes_used, from_ref, to_ref):
    for at in range(planes_used):
        place_x = mirrored(at, window_x - 1).astype(jnp.float32)
        value = correction_of(planes, cut_x, place_x)
        to_ref[at + 1] = value if from_ref is None else from_ref[at + 1] + value


def clear_ends(field_ref, window_x):
    empty = jnp.zeros(field_ref.shape[1:], jnp.float32)
    field_ref[0] = empty
    field_ref[window_x + 1] = empty


def first_kernel(
    counts, scale_factor, own_ref, other_ref, even_ref, even_other_ref, odd_ref, odd_other_ref,
    ids_ref, inverse_ref, gathered_ref,
    field_ref, weight_ref, drive_ref, out_ref, spare_ref,
):
    count_x, count_y = counts
    _, rows_x, rows_y, cells_z = own_ref.shape
    window_x, window_y, _ = weight_ref.shape
    at_y = lax.axis_index("gy")
    parity = lax.rem(at_y, 2)
    even_row = pl.multiple_of((1 - parity) * 2 * rows_y, SUBLANES)
    odd_row = pl.multiple_of(parity * 2 * rows_y, SUBLANES)
    odd_inside = jnp.where((at_y > 0) & (at_y < count_y - 1), jacobi_weight, 0.0)
    for ref, first, row, scale in (
        (own_ref, 0, rows_y, jacobi_weight),
        (other_ref, rows_x, rows_y, jacobi_weight),
        (even_ref, 0, even_row, jacobi_weight),
        (even_other_ref, rows_x, even_row, jacobi_weight),
        (odd_ref, 0, odd_row, odd_inside),
        (odd_other_ref, rows_x, odd_row, odd_inside),
    ):
        for at in range(rows_x):
            plane = mirrored(at, rows_x - 1)
            weight = scale / (6.0 + ref[1, plane])
            weight_ref[first + at, pl.ds(row, rows_y), :] = weight
            drive_ref[first + at, pl.ds(row, rows_y), :] = weight * ref[0, plane]

    parts = inverse_ref.shape[0] // LANES
    rows = [gathered_ref[at : at + 1] for at in range(parts + 1)]
    cut_x, cut_y = cuts_of(rows[parts], count_x, count_y)
    place = window_place(count_y, rows_y, (window_y, cells_z))
    planes = coarse_planes(rows[:parts], inverse_ref, ids_ref, scale_factor, cut_y, place)
    clear_ends(field_ref, window_x)
    clear_ends(spare_ref, window_x)
    add_correction(planes, cut_x, window_x, window_x, None, field_ref)
    for step in range(SWEEPS):
        refs = (field_ref, spare_ref) if step % 2 == 0 else (spare_ref, field_ref)
        sweep(*refs, weight_ref, drive_ref, rows_x, 2 * SWEEPS - 1 - step)

    residual, used = [], []
    own_rows = slice(rows_y, 2 * rows_y)
    for at in range(rows_x):
        plane = mirrored(at, rows_x - 1)
        center, beside = neighbours(field_ref, at, own_rows)
        residual.append(own_ref[0, plane] - ((6.0 + own_ref[1, plane]) * center - beside))
        used.append(plane)
    partial = restrict(jnp.concatenate(residual, axis=0), ids_ref, used, inverse_ref.shape[0])
    store_copies(out_ref, partial + rows[parts:])


def second_kernel(
    counts, scale_factor, pieces,
    field_ref, weight_ref, drive_ref, ids_ref, inverse_ref, gathered_ref, *rest,
):
    out_refs, (one_ref, two_ref) = rest[:pieces], rest[pieces:]
    count_x, count_y = counts
    window_x, window_y, cells_z = weight_ref.shape
    rows_x, rows_y, chunk = out_refs[0].shape
    parts = inverse_ref.shape[0] // LANES
    gathered = jnp.sum(gathered_ref[...], axis=0)
    rows = [gathered[at : at + 1] for at in range(parts)]
    cut_x, cut_y = cuts_of(gathered_ref[0, parts : parts + 1], count_x, count_y)
    place = window_place(count_y, rows_y, (window_y, cells_z))
    planes = coarse_planes(rows, inverse_ref, ids_ref, scale_factor, cut_y, place)
    clear_ends(one_ref, window_x)
    clear_ends(two_ref, window_x)
    used = min(window_x, rows_x + SWEEPS)
    add_correction(planes, cut_x, window_x, used, field_ref, one_ref)
    fields = [one_ref, two_ref]
    for step in range(SWEEPS - 1):
        sweep(*fields, weight_ref, drive_ref, rows_x, SWEEPS - 1 - step)
        fields.reverse()
    last_ref, own_ref = fields
    own_rows = slice(rows_y, 2 * rows_y)
    for at in range(rows_x):
        value = smooth(last_ref, weight_ref, drive_ref, at, own_rows)
        own_ref[mirrored(at, rows_x - 1), pl.ds(0, rows_y), :] = value
    me = lax.axis_index("grp")
    for turn in range(pieces):
        first = pl.multiple_of(lax.bitwise_xor(me, turn) * chunk, LANES)
        for at in range(rows_x):
            out_refs[turn][at] = own_ref[at, pl.ds(0, rows_y), pl.ds(first, chunk)]


def range_kernel(pieces, omega_ref, range_ref, *rest):
    snaps, (new_ref,) = rest[:pieces], rest[pieces:]
    rows_x = range_ref.shape[1]
    me = lax.axis_index("grp")
    slots = [lax.bitwise_xor(me, turn) for turn in range(pieces)]
    cells = [[snaps[turn][at] for at in range(rows_x)] for turn in range(pieces)]
    for at_row in range(range_ref.shape[0]):
        scales = [omega_ref[slots[turn], at_row] for turn in range(pieces)]
        for at in range(rows_x):
            value = range_ref[at_row, at]
            for turn in range(pieces):
                value = value + scales[turn] * cells[turn][at]
            new_ref[at_row, at] = value


def sum_rows(values):
    sublanes = iota(values[0].shape, 0)
    shift = SUBLANES // 2
    while shift:
        low = lax.bitwise_and(sublanes, shift) == 0
        half = len(values) // 2
        values = [
            jnp.where(
                low,
                values[at] + pltpu.roll(values[at], SUBLANES - shift, 0),
                values[at + half] + pltpu.roll(values[at + half], shift, 0),
            )
            for at in range(half)
        ]
        shift //= 2
    return values[0]


def products(psi_ref, phi_ref, snaps):
    rows_x = psi_ref.shape[1]
    cells = [[snap[at] for at in range(rows_x)] for snap in snaps]
    kept = [[] for _ in snaps]
    for ref in (psi_ref, phi_ref):
        for first in range(0, ref.shape[0], SUBLANES):
            totals = [[] for _ in snaps]
            for at_row in range(first, first + SUBLANES):
                parts = [ref[at_row, at] for at in range(rows_x)]
                for turn in range(len(snaps)):
                    total = parts[0] * cells[turn][0]
                    for at in range(1, rows_x):
                        total = total + parts[at] * cells[turn][at]
                    totals[turn].append(total)
            for turn in range(len(snaps)):
                kept[turn].append(sum_rows(totals[turn]))
    count = psi_ref.shape[0] + phi_ref.shape[0]
    rest = [jnp.zeros((LANES - count, LANES), jnp.float32)] if count < LANES else []
    ones = jnp.ones((SUBLANES, LANES), jnp.float32)
    return [dot_nt(ones, jnp.concatenate(rows + rest, axis=0))[0:1] for rows in kept]


def early_kernel(pieces, psi_ref, phi_ref, *rest):
    snaps, (out_ref,) = rest[:pieces], rest[pieces:]
    for at, row in enumerate(products(psi_ref, phi_ref, snaps)):
        out_ref[at : at + 1, :] = row


def late_kernel(pieces, psi_ref, phi_ref, early_ref, *rest):
    snaps, (out_ref,) = rest[:pieces], rest[pieces:]
    me = lax.axis_index("grp")
    early = early_ref.shape[0]
    rows = [early_ref[at : at + 1, :] for at in range(early)]
    rows += products(psi_ref, phi_ref, snaps)
    for turn, row in enumerate(rows):
        slot = lax.bitwise_xor(me, turn)
        for copy in range(out_ref.shape[0]):
            out_ref[copy, pl.ds(slot, 1), :] = row


def end_kernel(gathered_ref, xi_ref, core_ref, corange_out_ref, core_out_ref):
    corange = corange_out_ref.shape[1]
    core = core_ref.shape[0]
    total = jnp.sum(gathered_ref[...], axis=0)
    corange_out_ref[...] = total[:, :corange]
    images = total[:, corange : corange + core]
    core_out_ref[...] = core_ref[...] + dot_tn(images, xi_ref[...])


vmem = pl.BlockSpec(memory_space=pltpu.VMEM)
smem = pl.BlockSpec(memory_space=pltpu.SMEM)


def call(kernel, outs, inputs, scratch=(), specs=None):
    many = isinstance(outs, list)
    shapes = [jax.ShapeDtypeStruct(shape, jnp.float32) for shape in (outs if many else [outs])]
    result = pl.pallas_call(
        kernel,
        out_shape=shapes,
        in_specs=specs or [vmem] * len(inputs),
        out_specs=[vmem] * len(shapes),
        scratch_shapes=[pltpu.VMEM(shape, jnp.float32) for shape in scratch],
        compiler_params=pltpu.CompilerParams(vmem_limit_bytes=VMEM_BYTES),
    )(*inputs)
    return result if many else result[0]


def in_hbm(array):
    return pltpu.with_memory_space_constraint(array, pltpu.HBM)


def gather(copies, axes):
    return lax.all_to_all(copies, axes, 0, 0)


def fast_body(
    sources, diagonal, coarse_ids, coarse_inverse, omega_rows, psi, phi, xi_cols, range_sketch,
    core_sketch,
):
    source = sources[0]
    rows_x, rows_y, cells_z = source.shape
    counts = (lax.axis_size("gx"), lax.axis_size("gy"))
    groups = lax.axis_size("grp")
    count_x, count_y = counts
    coarse = coarse_inverse.shape[0]
    scale_factor = coarse / (rows_x * count_x * rows_y * count_y * cells_z)
    window = (rows_x * count_x, 3 * rows_y, cells_z)
    padded = (window[0] + 2,) + window[1:]
    copies = (count_x * count_y, coarse // LANES + 1, LANES)

    def partner_y(at, phase):
        found = at ^ 1 if phase == 0 else ((at + 1) ^ 1) - 1
        return found if 0 <= found < count_y else at

    def pairs(cross, phase):
        return [
            (x * count_y + y, (x ^ cross) * count_y + (y if phase is None else partner_y(y, phase)))
            for x in range(count_x)
            for y in range(count_y)
        ]

    mine, ids, inverse, begin = pl.pallas_call(
        begin_kernel,
        out_shape=[
            jax.ShapeDtypeStruct((2,) + source.shape, jnp.float32),
            jax.ShapeDtypeStruct(coarse_ids.shape, jnp.int32),
            jax.ShapeDtypeStruct(coarse_inverse.shape, jnp.float32),
            jax.ShapeDtypeStruct(copies[1:], jnp.float32),
        ],
        in_specs=[pl.BlockSpec(memory_space=pltpu.HBM)] * 4,
        out_specs=[vmem] * 4,
        scratch_shapes=[pltpu.SemaphoreType.DMA((4,))],
        compiler_params=pltpu.CompilerParams(vmem_limit_bytes=VMEM_BYTES),
        name="begin",
    )(*map(in_hbm, (source, diagonal, coarse_ids, coarse_inverse)))
    others = []
    for at, (cross, phase) in enumerate(((1, None), (0, 0), (0, 0), (0, 1), (0, 1))):
        sent = others[0] if at in (2, 4) else mine
        others.append(lax.ppermute(sent, ("gx", "gy"), pairs(cross, phase)))
    gathered = begin
    bits = [1 << bit for bit in reversed(range(count_y.bit_length() - 1))]
    turns = [("gy", count_y, bit) for bit in bits]
    turns.insert(1, ("gx", count_x, 1))
    for axis, count, bit in turns:
        gathered = gathered + lax.ppermute(gathered, axis, [(i, i ^ bit) for i in range(count)])
    field, weight, drive, partial = call(
        functools.partial(first_kernel, counts, scale_factor),
        [padded, window, window, copies],
        (mine, *others, ids, inverse, gathered),
        scratch=[padded],
    )
    gathered = gather(partial, ("gx", "gy"))
    chunk = cells_z // groups
    pieces = call(
        functools.partial(second_kernel, counts, scale_factor, groups),
        [(rows_x, rows_y, chunk)] * groups,
        (field, weight, drive, ids, inverse, gathered),
        scratch=[padded, padded],
    )
    snaps = [pieces[0]] + [
        lax.ppermute(pieces[turn], "grp", [(at, at ^ turn) for at in range(groups)])
        for turn in range(1, groups)
    ]
    early = max(1, groups // 2)
    kept = call(functools.partial(early_kernel, early), (early, LANES), (psi, phi, *snaps[:early]))
    sketched = call(
        functools.partial(late_kernel, groups - early),
        (groups * count_x * count_y, groups, LANES),
        (psi, phi, kept, *snaps[early:]),
    )
    gathered = gather(sketched, ("grp", "gx", "gy"))
    range_new = call(
        functools.partial(range_kernel, groups),
        range_sketch.shape,
        (omega_rows, range_sketch, *snaps),
        specs=[smem] + [vmem] * (1 + groups),
    )
    corange_cols, core_new = call(
        end_kernel, [(groups, psi.shape[0]), core_sketch.shape], (gathered, xi_cols.T, core_sketch)
    )
    return range_new, corange_cols.T, core_new


def with_halo(cells, sides, width):
    for axis, dim in sides:
        count = lax.axis_size(axis)
        ends = count - 1
        head = lax.slice_in_dim(cells, 0, width, axis=dim)
        tail = lax.slice_in_dim(cells, cells.shape[dim] - width, cells.shape[dim], axis=dim)
        cells = jnp.concatenate(
            [
                lax.ppermute(tail, axis, [(i, (i + 1) % count) for i in range(ends)]),
                cells,
                lax.ppermute(head, axis, [((i + 1) % count, i) for i in range(ends)]),
            ],
            axis=dim,
        )
    return cells


def neighbour_image(widened, diagonal):
    center = widened[1:-1, 1:-1]
    beside = widened[2:, 1:-1] + widened[:-2, 1:-1]
    beside = beside + widened[1:-1, 2:] + widened[1:-1, :-2]
    padded = jnp.pad(center, ((0, 0), (0, 0), (1, 1)))
    beside = beside + padded[:, :, 2:] + padded[:, :, :-2]
    return (center, (6.0 + diagonal) * center - beside)


def smooth_once(widened, source, diagonal):
    center, applied = neighbour_image(widened, diagonal)
    return center + jacobi_weight * (source - applied) / (6.0 + diagonal)


def axis_maps(coarse_ids):
    ranks_x = coarse_ids[:, 0, 0] // (XY_CUTS * Z_CUTS)
    ranks_y = coarse_ids[0, :, 0] // Z_CUTS % XY_CUTS
    ranks_z = coarse_ids[0, 0, :] % Z_CUTS
    cuts_xy = jnp.arange(XY_CUTS, dtype=jnp.int32)
    cuts_z = jnp.arange(Z_CUTS, dtype=jnp.int32)
    map_x = (ranks_x[:, None] == cuts_xy[None, :]).astype(jnp.float32)
    map_y = (ranks_y[:, None] == cuts_xy[None, :]).astype(jnp.float32)
    map_z = (ranks_z[:, None] == cuts_z[None, :]).astype(jnp.float32)
    return (map_x, map_y, map_z)


def restrict_cells(values, maps):
    map_x, map_y, map_z = maps
    rows_x, rows_y, cells_z = values.shape
    along_z = jnp.dot(values.reshape(rows_x * rows_y, cells_z), map_z, precision=highest)
    along_z = along_z.reshape(rows_x, rows_y, Z_CUTS)
    along_y = jnp.einsum("xyc,yb->xbc", along_z, map_y, precision=highest)
    along_x = jnp.einsum("xbc,xa->abc", along_y, map_x, precision=highest)
    return along_x.reshape(-1)


def prolong(correction, maps, extent):
    map_x, map_y, map_z = maps
    boxes = correction.reshape(XY_CUTS, XY_CUTS, Z_CUTS)
    over_x = jnp.einsum("abc,xa->xbc", boxes, map_x, precision=highest)
    over_y = jnp.einsum("xbc,yb->xyc", over_x, map_y, precision=highest)
    spread = jnp.dot(over_y.reshape(extent[0] * extent[1], Z_CUTS), map_z.T, precision=highest)
    return spread.reshape(extent)


def general_body(
    sources, diagonal, coarse_ids, coarse_inverse, omega_rows, psi, phi, xi_cols, range_sketch,
    core_sketch,
):
    source = sources[0]
    rows_x, rows_y, cells_z = source.shape
    coarse = coarse_inverse.shape[0]
    total_cells = rows_x * lax.axis_size("gx") * rows_y * lax.axis_size("gy") * cells_z
    scale_factor = coarse / total_cells
    maps = axis_maps(coarse_ids)
    sides = (("gx", 0), ("gy", 1))
    pressure = jnp.zeros_like(source)
    for outer_step in range(OUTER):
        if outer_step == 0:
            residual = source
        else:
            residual = source - neighbour_image(with_halo(pressure, sides, 1), diagonal)[1]
        coarse_rhs = lax.psum(restrict_cells(residual, maps), ("gx", "gy"))
        correction = jnp.dot(coarse_inverse, coarse_rhs * scale_factor, precision=highest)
        pressure = pressure + prolong(correction, maps, source.shape)
        for _ in range(SWEEPS):
            pressure = smooth_once(with_halo(pressure, sides, 1), source, diagonal)
    snapshot = lax.all_to_all(pressure[None], "grp", split_axis=3, concat_axis=0, tiled=True)
    columns = snapshot.reshape(snapshot.shape[0], -1)
    range_flat = range_sketch.reshape(range_sketch.shape[0], -1)
    range_new = range_flat + jnp.einsum("tk,tc->kc", omega_rows, columns, precision=highest)
    corange_part = jnp.einsum(
        "lc,tc->lt", psi.reshape(psi.shape[0], -1), columns, precision=highest
    )
    core_part = jnp.einsum("sc,tc->st", phi.reshape(phi.shape[0], -1), columns, precision=highest)
    corange_cols, core_images = lax.psum((corange_part, core_part), ("grp", "gx", "gy"))
    core_new = core_sketch + jnp.dot(core_images, xi_cols.T, precision=highest)
    return (range_new.reshape(range_sketch.shape), corange_cols, core_new)


def body(*arrays):
    _, rows_y, cells_z = arrays[1].shape
    coarse, groups = arrays[3].shape[0], lax.axis_size("grp")
    fits = (
        lax.axis_size("gx") == 2
        and lax.axis_size("gy") & (lax.axis_size("gy") - 1) == 0
        and lax.axis_size("gy") > 1
        and rows_y >= OUTER * SWEEPS
        and OUTER == 2
        and rows_y == SUBLANES
        and coarse == XY_CUTS * XY_CUTS * Z_CUTS
        and groups & (groups - 1) == 0
        and 1 < groups <= SUBLANES
        and cells_z % (groups * LANES) == 0
        and cells_z // groups == LANES
        and coarse % LANES == 0
        and arrays[5].shape[0] % SUBLANES == 0
        and arrays[6].shape[0] % SUBLANES == 0
        and arrays[5].shape[0] + arrays[6].shape[0] <= LANES
    )
    if not fits:
        return general_body(*arrays)
    return fast_body(*arrays)


def solution(mesh):
    return jax.shard_map(
        body,
        mesh=mesh,
        in_specs=(
            P("grp", "gx", "gy", None),
            P("gx", "gy", None),
            P("gx", "gy", None),
            P(),
            P(),
            P(None, "gx", "gy", "grp"),
            P(None, "gx", "gy", "grp"),
            P(),
            P(None, "gx", "gy", "grp"),
            P(),
        ),
        out_specs=(P(None, "gx", "gy", "grp"), P(), P()),
        check_vma=False,
    )
```

```python
import functools

import jax
import jax.numpy as jnp
from jax import lax
from jax.experimental import pallas as pl
from jax.experimental.pallas import tpu as pltpu
from jax.sharding import PartitionSpec as P


OUTER = 2
SWEEPS = 4
XY_CUTS = 4
Z_CUTS = 16
XY_BITS = XY_CUTS.bit_length() - 1
Z_BITS = Z_CUTS.bit_length() - 1
LANES = 128
SUBLANES = 8
VMEM_BYTES = 16 * 2**20

jacobi_weight = 2.0 / 3.0
highest = lax.Precision.HIGHEST


def dot_nt(a, b):
    return lax.dot_general(
        a, b, (((1,), (1,)), ((), ())), precision=highest, preferred_element_type=jnp.float32
    )


def dot_tn(a, b):
    return lax.dot_general(
        a, b, (((0,), (0,)), ((), ())), precision=highest, preferred_element_type=jnp.float32
    )


def iota(shape, dim):
    return lax.broadcasted_iota(jnp.int32, shape, dim)


def store_copies(out_ref, rows):
    for copy in range(out_ref.shape[0]):
        for at, row in enumerate(rows):
            out_ref[copy, at : at + 1, :] = row


def box_of(ids_ref, at):
    return lax.shift_right_logical(ids_ref[at, :, :LANES], Z_BITS)


def restrict(values, ids_ref, planes, coarse):
    cells_z = values.shape[1]
    rows_y = ids_ref.shape[1]
    ranks = lax.bitwise_and(ids_ref[0, 0:1, :], Z_CUTS - 1)
    members = lax.bitwise_and(iota((LANES, cells_z), 0), Z_CUTS - 1) == ranks
    sums = dot_nt(values, members.astype(jnp.float32))
    lane_box = lax.shift_right_logical(iota((rows_y, LANES), 1), Z_BITS)
    rows = []
    for part in range(coarse // LANES):
        total = None
        for at, plane in enumerate(planes):
            own = box_of(ids_ref, plane) == lane_box + part * (LANES // Z_CUTS)
            kept = jnp.where(own, sums[at * rows_y : (at + 1) * rows_y], 0.0)
            total = kept if total is None else total + kept
        rows.append(jnp.sum(total, axis=0, keepdims=True))
    return rows


def begin_kernel(
    source_from, diagonal_from, ids_from, inverse_from,
    mine_ref, ids_ref, inverse_ref, out_ref, arrived,
):
    loads = [
        pltpu.make_async_copy(source, target, arrived.at[at])
        for at, (source, target) in enumerate(
            (
                (ids_from, ids_ref),
                (source_from, mine_ref.at[0]),
                (diagonal_from, mine_ref.at[1]),
                (inverse_from, inverse_ref),
            )
        )
    ]
    for load in loads:
        load.start()
    coarse = inverse_ref.shape[0]
    rows_x, rows_y, cells_z = ids_ref.shape
    loads[0].wait()
    lanes = iota((1, LANES), 1)
    boxes = [box_of(ids_ref, at) for at in range(rows_x)]
    below_x = jnp.zeros((1, LANES), jnp.float32)
    for box in boxes:
        below_x = below_x + (lax.shift_right_logical(box[0:1], XY_BITS) <= lanes).astype(jnp.float32)
    ranks_y = lax.bitwise_and(boxes[0], XY_CUTS - 1)
    below_y = jnp.sum((ranks_y <= lanes - XY_CUTS).astype(jnp.float32), axis=0, keepdims=True)
    loads[1].wait()
    rows = restrict(
        mine_ref[0].reshape(rows_x * rows_y, cells_z), ids_ref, range(rows_x), coarse
    ) + [jnp.where(lanes < XY_CUTS, below_x, below_y)]
    for at, part in enumerate(rows):
        out_ref[at : at + 1, :] = part
    loads[2].wait()
    loads[3].wait()


def coarse_planes(rows, inverse_ref, ids_ref, scale_factor, cut_y, place):
    coarse = inverse_ref.shape[0]
    cells_z = ids_ref.shape[2]
    per_part = LANES // Z_CUTS
    row = jnp.broadcast_to(jnp.concatenate(rows, axis=1) * scale_factor, (SUBLANES, coarse))
    solved = dot_nt(row, inverse_ref[...])
    shape = (per_part, LANES)
    own = lax.shift_right_logical(iota(shape, 1), Z_BITS) == iota(shape, 0)
    lines = []
    for part in range(coarse // LANES):
        values = jnp.where(own, solved[:per_part, part * LANES : (part + 1) * LANES], 0.0)
        shift = LANES // 2
        while shift >= Z_CUTS:
            values = values + pltpu.roll(values, shift, 1)
            shift //= 2
        along_z = jnp.concatenate(
            [
                jnp.take_along_axis(
                    values,
                    lax.bitwise_and(ids_ref[0, :per_part, at : at + LANES], Z_CUTS - 1),
                    axis=1,
                )
                for at in range(0, cells_z, LANES)
            ],
            axis=1,
        )
        lines.extend(along_z[at : at + 1] for at in range(per_part))
    place_y, inside = place
    planes = []
    for box_x in range(XY_CUTS):
        first = box_x * XY_CUTS
        plane = jnp.broadcast_to(lines[first], place_y.shape)
        for box_y in range(1, XY_CUTS):
            plane = jnp.where(place_y >= cut_y[box_y - 1], lines[first + box_y], plane)
        planes.append(jnp.where(inside, plane, 0.0))
    return planes


def correction_of(planes, cut_x, place_x):
    value = planes[0]
    for box_x in range(1, XY_CUTS):
        value = jnp.where(cut_x[box_x - 1] <= place_x, planes[box_x], value)
    return value


def cuts_of(row, count_x, count_y):
    cut_x = [row[:, at : at + 1] * (1.0 / count_y) for at in range(XY_CUTS - 1)]
    cut_y = [row[:, XY_CUTS + at : XY_CUTS + at + 1] * (1.0 / count_x) for at in range(XY_CUTS - 1)]
    return cut_x, cut_y


def beside_z(values):
    lanes = iota((values.shape[0], LANES), 1)
    tiles = [values[:, at : at + LANES] for at in range(0, values.shape[1], LANES)]
    empty = jnp.zeros_like(tiles[0])
    ahead = [pltpu.roll(tile, LANES - 1, 1) for tile in tiles] + [empty]
    behind = [empty] + [pltpu.roll(tile, 1, 1) for tile in tiles]
    return jnp.concatenate(
        [
            jnp.where(lanes == LANES - 1, ahead[at + 1], ahead[at])
            + jnp.where(lanes == 0, behind[at], behind[at + 1])
            for at in range(len(tiles))
        ],
        axis=1,
    )


def beside_y(values):
    rows = values.shape[0]
    return pltpu.roll(values, rows - 1, 0) + pltpu.roll(values, 1, 0)


def neighbours(field_ref, at, rows=None):
    center = field_ref[at + 1]
    along_y = beside_y(center)
    if rows is None:
        rows = slice(0, center.shape[0])
    center = center[rows]
    across = field_ref[at, rows, :] + field_ref[at + 2, rows, :]
    return center, across + along_y[rows] + beside_z(center)


def smooth(field_ref, weight_ref, drive_ref, at, rows=None):
    center, beside = neighbours(field_ref, at, rows)
    rows = slice(None) if rows is None else rows
    kept = center * (1.0 - jacobi_weight) + drive_ref[at, rows, :]
    return kept + weight_ref[at, rows, :] * beside


def sweep(from_ref, to_ref, weight_ref, drive_ref, rows_x, reach):
    window_x, window_y, _ = weight_ref.shape
    own_rows = slice(window_y // 3, 2 * window_y // 3)
    for at in range(window_x):
        away = max(0, at - rows_x + 1)
        if away > reach:
            continue
        if away == reach:
            to_ref[at + 1, own_rows, :] = smooth(from_ref, weight_ref, drive_ref, at, own_rows)
        else:
            to_ref[at + 1] = smooth(from_ref, weight_ref, drive_ref, at)


def window_place(count_y, rows_y, shape):
    place_y = iota(shape, 0) + (lax.axis_index("gy") - 1) * rows_y
    inside = (place_y >= 0) & (place_y < rows_y * count_y)
    return place_y.astype(jnp.float32), inside


def mirrored(at, last):
    return jnp.where(lax.axis_index("gx") == 0, at, last - at)


def add_correction(planes, cut_x, window_x, planes_used, from_ref, to_ref):
    for at in range(planes_used):
        place_x = mirrored(at, window_x - 1).astype(jnp.float32)
        value = correction_of(planes, cut_x, place_x)
        to_ref[at + 1] = value if from_ref is None else from_ref[at + 1] + value


def clear_ends(field_ref, window_x):
    empty = jnp.zeros(field_ref.shape[1:], jnp.float32)
    field_ref[0] = empty
    field_ref[window_x + 1] = empty


def first_kernel(
    counts, scale_factor, own_ref, other_ref, even_ref, even_other_ref, odd_ref, odd_other_ref,
    ids_ref, inverse_ref, gathered_ref,
    field_ref, weight_ref, drive_ref, out_ref, spare_ref,
):
    count_x, count_y = counts
    _, rows_x, rows_y, cells_z = own_ref.shape
    window_x, window_y, _ = weight_ref.shape
    at_y = lax.axis_index("gy")
    parity = lax.rem(at_y, 2)
    even_row = pl.multiple_of((1 - parity) * 2 * rows_y, SUBLANES)
    odd_row = pl.multiple_of(parity * 2 * rows_y, SUBLANES)
    odd_inside = jnp.where((at_y > 0) & (at_y < count_y - 1), jacobi_weight, 0.0)
    for ref, first, row, scale in (
        (own_ref, 0, rows_y, jacobi_weight),
        (other_ref, rows_x, rows_y, jacobi_weight),
        (even_ref, 0, even_row, jacobi_weight),
        (even_other_ref, rows_x, even_row, jacobi_weight),
        (odd_ref, 0, odd_row, odd_inside),
        (odd_other_ref, rows_x, odd_row, odd_inside),
    ):
        for at in range(rows_x):
            plane = mirrored(at, rows_x - 1)
            weight = scale / (6.0 + ref[1, plane])
            weight_ref[first + at, pl.ds(row, rows_y), :] = weight
            drive_ref[first + at, pl.ds(row, rows_y), :] = weight * ref[0, plane]

    parts = inverse_ref.shape[0] // LANES
    rows = [gathered_ref[at : at + 1] for at in range(parts + 1)]
    cut_x, cut_y = cuts_of(rows[parts], count_x, count_y)
    place = window_place(count_y, rows_y, (window_y, cells_z))
    planes = coarse_planes(rows[:parts], inverse_ref, ids_ref, scale_factor, cut_y, place)
    clear_ends(field_ref, window_x)
    clear_ends(spare_ref, window_x)
    add_correction(planes, cut_x, window_x, window_x, None, field_ref)
    for step in range(SWEEPS):
        refs = (field_ref, spare_ref) if step % 2 == 0 else (spare_ref, field_ref)
        sweep(*refs, weight_ref, drive_ref, rows_x, 2 * SWEEPS - 1 - step)

    residual, used = [], []
    own_rows = slice(rows_y, 2 * rows_y)
    for at in range(rows_x):
        plane = mirrored(at, rows_x - 1)
        center, beside = neighbours(field_ref, at, own_rows)
        residual.append(own_ref[0, plane] - ((6.0 + own_ref[1, plane]) * center - beside))
        used.append(plane)
    partial = restrict(jnp.concatenate(residual, axis=0), ids_ref, used, inverse_ref.shape[0])
    store_copies(out_ref, partial + rows[parts:])


def second_kernel(
    counts, scale_factor, pieces,
    field_ref, weight_ref, drive_ref, ids_ref, inverse_ref, gathered_ref, *rest,
):
    out_refs, (one_ref, two_ref) = rest[:pieces], rest[pieces:]
    count_x, count_y = counts
    window_x, window_y, cells_z = weight_ref.shape
    rows_x, rows_y, chunk = out_refs[0].shape
    parts = inverse_ref.shape[0] // LANES
    gathered = jnp.sum(gathered_ref[...], axis=0)
    rows = [gathered[at : at + 1] for at in range(parts)]
    cut_x, cut_y = cuts_of(gathered_ref[0, parts : parts + 1], count_x, count_y)
    place = window_place(count_y, rows_y, (window_y, cells_z))
    planes = coarse_planes(rows, inverse_ref, ids_ref, scale_factor, cut_y, place)
    clear_ends(one_ref, window_x)
    clear_ends(two_ref, window_x)
    used = min(window_x, rows_x + SWEEPS)
    add_correction(planes, cut_x, window_x, used, field_ref, one_ref)
    fields = [one_ref, two_ref]
    for step in range(SWEEPS - 1):
        sweep(*fields, weight_ref, drive_ref, rows_x, SWEEPS - 1 - step)
        fields.reverse()
    last_ref, own_ref = fields
    own_rows = slice(rows_y, 2 * rows_y)
    for at in range(rows_x):
        value = smooth(last_ref, weight_ref, drive_ref, at, own_rows)
        own_ref[mirrored(at, rows_x - 1), pl.ds(0, rows_y), :] = value
    me = lax.axis_index("grp")
    for turn in range(pieces):
        first = pl.multiple_of(lax.bitwise_xor(me, turn) * chunk, LANES)
        for at in range(rows_x):
            out_refs[turn][at] = own_ref[at, pl.ds(0, rows_y), pl.ds(first, chunk)]


def range_kernel(pieces, omega_ref, range_ref, *rest):
    snaps, (new_ref,) = rest[:pieces], rest[pieces:]
    rows_x = range_ref.shape[1]
    me = lax.axis_index("grp")
    slots = [lax.bitwise_xor(me, turn) for turn in range(pieces)]
    cells = [[snaps[turn][at] for at in range(rows_x)] for turn in range(pieces)]
    for at_row in range(range_ref.shape[0]):
        scales = [omega_ref[slots[turn], at_row] for turn in range(pieces)]
        for at in range(rows_x):
            value = range_ref[at_row, at]
            for turn in range(pieces):
                value = value + scales[turn] * cells[turn][at]
            new_ref[at_row, at] = value


def sum_rows(values):
    sublanes = iota(values[0].shape, 0)
    shift = SUBLANES // 2
    while shift:
        low = lax.bitwise_and(sublanes, shift) == 0
        half = len(values) // 2
        values = [
            jnp.where(
                low,
                values[at] + pltpu.roll(values[at], SUBLANES - shift, 0),
                values[at + half] + pltpu.roll(values[at + half], shift, 0),
            )
            for at in range(half)
        ]
        shift //= 2
    return values[0]


def products(psi_ref, phi_ref, snaps):
    rows_x = psi_ref.shape[1]
    cells = [[snap[at] for at in range(rows_x)] for snap in snaps]
    kept = [[] for _ in snaps]
    for ref in (psi_ref, phi_ref):
        for first in range(0, ref.shape[0], SUBLANES):
            totals = [[] for _ in snaps]
            for at_row in range(first, first + SUBLANES):
                parts = [ref[at_row, at] for at in range(rows_x)]
                for turn in range(len(snaps)):
                    total = parts[0] * cells[turn][0]
                    for at in range(1, rows_x):
                        total = total + parts[at] * cells[turn][at]
                    totals[turn].append(total)
            for turn in range(len(snaps)):
                kept[turn].append(sum_rows(totals[turn]))
    count = psi_ref.shape[0] + phi_ref.shape[0]
    rest = [jnp.zeros((LANES - count, LANES), jnp.float32)] if count < LANES else []
    ones = jnp.ones((SUBLANES, LANES), jnp.float32)
    return [dot_nt(ones, jnp.concatenate(rows + rest, axis=0))[0:1] for rows in kept]


def early_kernel(pieces, psi_ref, phi_ref, *rest):
    snaps, (out_ref,) = rest[:pieces], rest[pieces:]
    for at, row in enumerate(products(psi_ref, phi_ref, snaps)):
        out_ref[at : at + 1, :] = row


def late_kernel(pieces, psi_ref, phi_ref, early_ref, *rest):
    snaps, (out_ref,) = rest[:pieces], rest[pieces:]
    me = lax.axis_index("grp")
    early = early_ref.shape[0]
    rows = [early_ref[at : at + 1, :] for at in range(early)]
    rows += products(psi_ref, phi_ref, snaps)
    for turn, row in enumerate(rows):
        slot = lax.bitwise_xor(me, turn)
        for copy in range(out_ref.shape[0]):
            out_ref[copy, pl.ds(slot, 1), :] = row


def end_kernel(gathered_ref, xi_ref, core_ref, corange_out_ref, core_out_ref):
    corange = corange_out_ref.shape[1]
    core = core_ref.shape[0]
    total = jnp.sum(gathered_ref[...], axis=0)
    corange_out_ref[...] = total[:, :corange]
    images = total[:, corange : corange + core]
    core_out_ref[...] = core_ref[...] + dot_tn(images, xi_ref[...])


vmem = pl.BlockSpec(memory_space=pltpu.VMEM)
smem = pl.BlockSpec(memory_space=pltpu.SMEM)


def call(kernel, outs, inputs, scratch=(), specs=None):
    many = isinstance(outs, list)
    shapes = [jax.ShapeDtypeStruct(shape, jnp.float32) for shape in (outs if many else [outs])]
    result = pl.pallas_call(
        kernel,
        out_shape=shapes,
        in_specs=specs or [vmem] * len(inputs),
        out_specs=[vmem] * len(shapes),
        scratch_shapes=[pltpu.VMEM(shape, jnp.float32) for shape in scratch],
        compiler_params=pltpu.CompilerParams(vmem_limit_bytes=VMEM_BYTES),
    )(*inputs)
    return result if many else result[0]


def in_hbm(array):
    return pltpu.with_memory_space_constraint(array, pltpu.HBM)


def gather(copies, axes):
    return lax.all_to_all(copies, axes, 0, 0)


def fast_body(
    sources, diagonal, coarse_ids, coarse_inverse, omega_rows, psi, phi, xi_cols, range_sketch,
    core_sketch,
):
    source = sources[0]
    rows_x, rows_y, cells_z = source.shape
    counts = (lax.axis_size("gx"), lax.axis_size("gy"))
    groups = lax.axis_size("grp")
    count_x, count_y = counts
    coarse = coarse_inverse.shape[0]
    scale_factor = coarse / (rows_x * count_x * rows_y * count_y * cells_z)
    window = (rows_x * count_x, 3 * rows_y, cells_z)
    padded = (window[0] + 2,) + window[1:]
    copies = (count_x * count_y, coarse // LANES + 1, LANES)

    def place(group, x, y):
        return (group * count_x + x) * count_y + y

    def partner(group, x, y, phase):
        if phase is None:
            return place(group, x ^ 1, y)
        beyond = y ^ 1 if phase == 0 else ((y + 1) ^ 1) - 1
        return place(group, x, beyond) if 0 <= beyond < count_y else place(group ^ 1, x, y)

    def pairs(phase):
        return [
            (place(group, x, y), partner(group, x, y, phase))
            for group in range(groups)
            for x in range(count_x)
            for y in range(count_y)
        ]

    mine, ids, inverse, begin = pl.pallas_call(
        begin_kernel,
        out_shape=[
            jax.ShapeDtypeStruct((2,) + source.shape, jnp.float32),
            jax.ShapeDtypeStruct(coarse_ids.shape, jnp.int32),
            jax.ShapeDtypeStruct(coarse_inverse.shape, jnp.float32),
            jax.ShapeDtypeStruct(copies[1:], jnp.float32),
        ],
        in_specs=[pl.BlockSpec(memory_space=pltpu.HBM)] * 4,
        out_specs=[vmem] * 4,
        scratch_shapes=[pltpu.SemaphoreType.DMA((4,))],
        compiler_params=pltpu.CompilerParams(vmem_limit_bytes=VMEM_BYTES),
        name="begin",
    )(*map(in_hbm, (source, diagonal, coarse_ids, coarse_inverse)))
    others = []
    for at, phase in enumerate((None, 0, 0, 1, 1)):
        sent = others[0] if at in (2, 4) else mine
        others.append(lax.ppermute(sent, ("grp", "gx", "gy"), pairs(phase)))
    gathered = begin
    bits = [1 << bit for bit in reversed(range(count_y.bit_length() - 1))]
    turns = [("gy", count_y, bit) for bit in bits]
    turns.insert(1, ("gx", count_x, 1))
    for axis, count, bit in turns:
        gathered = gathered + lax.ppermute(gathered, axis, [(i, i ^ bit) for i in range(count)])
    field, weight, drive, partial = call(
        functools.partial(first_kernel, counts, scale_factor),
        [padded, window, window, copies],
        (mine, *others, ids, inverse, gathered),
        scratch=[padded],
    )
    gathered = gather(partial, ("gx", "gy"))
    chunk = cells_z // groups
    pieces = call(
        functools.partial(second_kernel, counts, scale_factor, groups),
        [(rows_x, rows_y, chunk)] * groups,
        (field, weight, drive, ids, inverse, gathered),
        scratch=[padded, padded],
    )
    snaps = [pieces[0]] + [
        lax.ppermute(pieces[turn], "grp", [(at, at ^ turn) for at in range(groups)])
        for turn in range(1, groups)
    ]
    early = max(1, groups // 2)
    kept = call(functools.partial(early_kernel, early), (early, LANES), (psi, phi, *snaps[:early]))
    sketched = call(
        functools.partial(late_kernel, groups - early),
        (groups * count_x * count_y, groups, LANES),
        (psi, phi, kept, *snaps[early:]),
    )
    gathered = gather(sketched, ("grp", "gx", "gy"))
    range_new = call(
        functools.partial(range_kernel, groups),
        range_sketch.shape,
        (omega_rows, range_sketch, *snaps),
        specs=[smem] + [vmem] * (1 + groups),
    )
    corange_cols, core_new = call(
        end_kernel, [(groups, psi.shape[0]), core_sketch.shape], (gathered, xi_cols.T, core_sketch)
    )
    return range_new, corange_cols.T, core_new


def with_halo(cells, sides, width):
    for axis, dim in sides:
        count = lax.axis_size(axis)
        ends = count - 1
        head = lax.slice_in_dim(cells, 0, width, axis=dim)
        tail = lax.slice_in_dim(cells, cells.shape[dim] - width, cells.shape[dim], axis=dim)
        cells = jnp.concatenate(
            [
                lax.ppermute(tail, axis, [(i, (i + 1) % count) for i in range(ends)]),
                cells,
                lax.ppermute(head, axis, [((i + 1) % count, i) for i in range(ends)]),
            ],
            axis=dim,
        )
    return cells


def neighbour_image(widened, diagonal):
    center = widened[1:-1, 1:-1]
    beside = widened[2:, 1:-1] + widened[:-2, 1:-1]
    beside = beside + widened[1:-1, 2:] + widened[1:-1, :-2]
    padded = jnp.pad(center, ((0, 0), (0, 0), (1, 1)))
    beside = beside + padded[:, :, 2:] + padded[:, :, :-2]
    return (center, (6.0 + diagonal) * center - beside)


def smooth_once(widened, source, diagonal):
    center, applied = neighbour_image(widened, diagonal)
    return center + jacobi_weight * (source - applied) / (6.0 + diagonal)


def axis_maps(coarse_ids):
    ranks_x = coarse_ids[:, 0, 0] // (XY_CUTS * Z_CUTS)
    ranks_y = coarse_ids[0, :, 0] // Z_CUTS % XY_CUTS
    ranks_z = coarse_ids[0, 0, :] % Z_CUTS
    cuts_xy = jnp.arange(XY_CUTS, dtype=jnp.int32)
    cuts_z = jnp.arange(Z_CUTS, dtype=jnp.int32)
    map_x = (ranks_x[:, None] == cuts_xy[None, :]).astype(jnp.float32)
    map_y = (ranks_y[:, None] == cuts_xy[None, :]).astype(jnp.float32)
    map_z = (ranks_z[:, None] == cuts_z[None, :]).astype(jnp.float32)
    return (map_x, map_y, map_z)


def restrict_cells(values, maps):
    map_x, map_y, map_z = maps
    rows_x, rows_y, cells_z = values.shape
    along_z = jnp.dot(values.reshape(rows_x * rows_y, cells_z), map_z, precision=highest)
    along_z = along_z.reshape(rows_x, rows_y, Z_CUTS)
    along_y = jnp.einsum("xyc,yb->xbc", along_z, map_y, precision=highest)
    along_x = jnp.einsum("xbc,xa->abc", along_y, map_x, precision=highest)
    return along_x.reshape(-1)


def prolong(correction, maps, extent):
    map_x, map_y, map_z = maps
    boxes = correction.reshape(XY_CUTS, XY_CUTS, Z_CUTS)
    over_x = jnp.einsum("abc,xa->xbc", boxes, map_x, precision=highest)
    over_y = jnp.einsum("xbc,yb->xyc", over_x, map_y, precision=highest)
    spread = jnp.dot(over_y.reshape(extent[0] * extent[1], Z_CUTS), map_z.T, precision=highest)
    return spread.reshape(extent)


def general_body(
    sources, diagonal, coarse_ids, coarse_inverse, omega_rows, psi, phi, xi_cols, range_sketch,
    core_sketch,
):
    source = sources[0]
    rows_x, rows_y, cells_z = source.shape
    coarse = coarse_inverse.shape[0]
    total_cells = rows_x * lax.axis_size("gx") * rows_y * lax.axis_size("gy") * cells_z
    scale_factor = coarse / total_cells
    maps = axis_maps(coarse_ids)
    sides = (("gx", 0), ("gy", 1))
    pressure = jnp.zeros_like(source)
    for outer_step in range(OUTER):
        if outer_step == 0:
            residual = source
        else:
            residual = source - neighbour_image(with_halo(pressure, sides, 1), diagonal)[1]
        coarse_rhs = lax.psum(restrict_cells(residual, maps), ("gx", "gy"))
        correction = jnp.dot(coarse_inverse, coarse_rhs * scale_factor, precision=highest)
        pressure = pressure + prolong(correction, maps, source.shape)
        for _ in range(SWEEPS):
            pressure = smooth_once(with_halo(pressure, sides, 1), source, diagonal)
    snapshot = lax.all_to_all(pressure[None], "grp", split_axis=3, concat_axis=0, tiled=True)
    columns = snapshot.reshape(snapshot.shape[0], -1)
    range_flat = range_sketch.reshape(range_sketch.shape[0], -1)
    range_new = range_flat + jnp.einsum("tk,tc->kc", omega_rows, columns, precision=highest)
    corange_part = jnp.einsum(
        "lc,tc->lt", psi.reshape(psi.shape[0], -1), columns, precision=highest
    )
    core_part = jnp.einsum("sc,tc->st", phi.reshape(phi.shape[0], -1), columns, precision=highest)
    corange_cols, core_images = lax.psum((corange_part, core_part), ("grp", "gx", "gy"))
    core_new = core_sketch + jnp.dot(core_images, xi_cols.T, precision=highest)
    return (range_new.reshape(range_sketch.shape), corange_cols, core_new)


def body(*arrays):
    _, rows_y, cells_z = arrays[1].shape
    coarse, groups = arrays[3].shape[0], lax.axis_size("grp")
    fits = (
        lax.axis_size("gx") == 2
        and lax.axis_size("gy") & (lax.axis_size("gy") - 1) == 0
        and lax.axis_size("gy") > 1
        and rows_y >= OUTER * SWEEPS
        and OUTER == 2
        and rows_y == SUBLANES
        and coarse == XY_CUTS * XY_CUTS * Z_CUTS
        and groups & (groups - 1) == 0
        and 1 < groups <= SUBLANES
        and cells_z % (groups * LANES) == 0
        and cells_z // groups == LANES
        and coarse % LANES == 0
        and arrays[5].shape[0] % SUBLANES == 0
        and arrays[6].shape[0] % SUBLANES == 0
        and arrays[5].shape[0] + arrays[6].shape[0] <= LANES
    )
    if not fits:
        return general_body(*arrays)
    return fast_body(*arrays)


def solution(mesh):
    return jax.shard_map(
        body,
        mesh=mesh,
        in_specs=(
            P("grp", "gx", "gy", None),
            P("gx", "gy", None),
            P("gx", "gy", None),
            P(),
            P(),
            P(None, "gx", "gy", "grp"),
            P(None, "gx", "gy", "grp"),
            P(),
            P(None, "gx", "gy", "grp"),
            P(),
        ),
        out_specs=(P(None, "gx", "gy", "grp"), P(), P()),
        check_vma=False,
    )
```

```python
import functools

import jax
import jax.numpy as jnp
from jax import lax
from jax.experimental import pallas as pl
from jax.experimental.pallas import tpu as pltpu
from jax.sharding import PartitionSpec as P


OUTER = 2
SWEEPS = 4
XY_CUTS = 4
Z_CUTS = 16
XY_BITS = XY_CUTS.bit_length() - 1
Z_BITS = Z_CUTS.bit_length() - 1
LANES = 128
SUBLANES = 8
VMEM_BYTES = 16 * 2**20

jacobi_weight = 2.0 / 3.0
highest = lax.Precision.HIGHEST


def dot_nt(a, b):
    return lax.dot_general(
        a, b, (((1,), (1,)), ((), ())), precision=highest, preferred_element_type=jnp.float32
    )


def dot_tn(a, b):
    return lax.dot_general(
        a, b, (((0,), (0,)), ((), ())), precision=highest, preferred_element_type=jnp.float32
    )


def iota(shape, dim):
    return lax.broadcasted_iota(jnp.int32, shape, dim)


def store_copies(out_ref, rows):
    for copy in range(out_ref.shape[0]):
        for at, row in enumerate(rows):
            out_ref[copy, at : at + 1, :] = row


def box_of(ids_ref, at):
    return lax.shift_right_logical(ids_ref[at, :, :LANES], Z_BITS)


def restrict(values, ids_ref, planes, coarse):
    cells_z = values.shape[1]
    rows_y = ids_ref.shape[1]
    ranks = lax.bitwise_and(ids_ref[0, 0:1, :], Z_CUTS - 1)
    members = lax.bitwise_and(iota((LANES, cells_z), 0), Z_CUTS - 1) == ranks
    sums = dot_nt(values, members.astype(jnp.float32))
    lane_box = lax.shift_right_logical(iota((rows_y, LANES), 1), Z_BITS)
    rows = []
    for part in range(coarse // LANES):
        total = None
        for at, plane in enumerate(planes):
            own = box_of(ids_ref, plane) == lane_box + part * (LANES // Z_CUTS)
            kept = jnp.where(own, sums[at * rows_y : (at + 1) * rows_y], 0.0)
            total = kept if total is None else total + kept
        rows.append(jnp.sum(total, axis=0, keepdims=True))
    return rows


def begin_kernel(
    source_from, diagonal_from, ids_from, inverse_from,
    mine_ref, ids_ref, inverse_ref, out_ref, arrived,
):
    loads = [
        pltpu.make_async_copy(source, target, arrived.at[at])
        for at, (source, target) in enumerate(
            (
                (ids_from, ids_ref),
                (source_from, mine_ref.at[0]),
                (diagonal_from, mine_ref.at[1]),
                (inverse_from, inverse_ref),
            )
        )
    ]
    for load in loads:
        load.start()
    coarse = inverse_ref.shape[0]
    rows_x, rows_y, cells_z = ids_ref.shape
    loads[0].wait()
    lanes = iota((1, LANES), 1)
    boxes = [box_of(ids_ref, at) for at in range(rows_x)]
    below_x = jnp.zeros((1, LANES), jnp.float32)
    for box in boxes:
        below_x = below_x + (lax.shift_right_logical(box[0:1], XY_BITS) <= lanes).astype(jnp.float32)
    ranks_y = lax.bitwise_and(boxes[0], XY_CUTS - 1)
    below_y = jnp.sum((ranks_y <= lanes - XY_CUTS).astype(jnp.float32), axis=0, keepdims=True)
    loads[1].wait()
    rows = restrict(
        mine_ref[0].reshape(rows_x * rows_y, cells_z), ids_ref, range(rows_x), coarse
    ) + [jnp.where(lanes < XY_CUTS, below_x, below_y)]
    for at, part in enumerate(rows):
        out_ref[at : at + 1, :] = part
    loads[2].wait()
    loads[3].wait()


def coarse_planes(rows, inverse_ref, ids_ref, scale_factor, cut_y, place):
    coarse = inverse_ref.shape[0]
    cells_z = ids_ref.shape[2]
    per_part = LANES // Z_CUTS
    row = jnp.broadcast_to(jnp.concatenate(rows, axis=1) * scale_factor, (SUBLANES, coarse))
    solved = dot_nt(row, inverse_ref[...])
    shape = (per_part, LANES)
    own = lax.shift_right_logical(iota(shape, 1), Z_BITS) == iota(shape, 0)
    lines = []
    for part in range(coarse // LANES):
        values = jnp.where(own, solved[:per_part, part * LANES : (part + 1) * LANES], 0.0)
        shift = LANES // 2
        while shift >= Z_CUTS:
            values = values + pltpu.roll(values, shift, 1)
            shift //= 2
        along_z = jnp.concatenate(
            [
                jnp.take_along_axis(
                    values,
                    lax.bitwise_and(ids_ref[0, :per_part, at : at + LANES], Z_CUTS - 1),
                    axis=1,
                )
                for at in range(0, cells_z, LANES)
            ],
            axis=1,
        )
        lines.extend(along_z[at : at + 1] for at in range(per_part))
    place_y, inside = place
    planes = []
    for box_x in range(XY_CUTS):
        first = box_x * XY_CUTS
        plane = jnp.broadcast_to(lines[first], place_y.shape)
        for box_y in range(1, XY_CUTS):
            plane = jnp.where(place_y >= cut_y[box_y - 1], lines[first + box_y], plane)
        planes.append(jnp.where(inside, plane, 0.0))
    return planes


def correction_of(planes, cut_x, place_x):
    value = planes[0]
    for box_x in range(1, XY_CUTS):
        value = jnp.where(cut_x[box_x - 1] <= place_x, planes[box_x], value)
    return value


def cuts_of(row, count_x, count_y):
    cut_x = [row[:, at : at + 1] * (1.0 / count_y) for at in range(XY_CUTS - 1)]
    cut_y = [row[:, XY_CUTS + at : XY_CUTS + at + 1] * (1.0 / count_x) for at in range(XY_CUTS - 1)]
    return cut_x, cut_y


def beside_z(values):
    lanes = iota((values.shape[0], LANES), 1)
    tiles = [values[:, at : at + LANES] for at in range(0, values.shape[1], LANES)]
    empty = jnp.zeros_like(tiles[0])
    ahead = [pltpu.roll(tile, LANES - 1, 1) for tile in tiles] + [empty]
    behind = [empty] + [pltpu.roll(tile, 1, 1) for tile in tiles]
    return jnp.concatenate(
        [
            jnp.where(lanes == LANES - 1, ahead[at + 1], ahead[at])
            + jnp.where(lanes == 0, behind[at], behind[at + 1])
            for at in range(len(tiles))
        ],
        axis=1,
    )


def beside_y(values):
    rows = values.shape[0]
    return pltpu.roll(values, rows - 1, 0) + pltpu.roll(values, 1, 0)


def neighbours(field_ref, at, rows=None):
    center = field_ref[at + 1]
    along_y = beside_y(center)
    if rows is None:
        rows = slice(0, center.shape[0])
    center = center[rows]
    across = field_ref[at, rows, :] + field_ref[at + 2, rows, :]
    return center, across + along_y[rows] + beside_z(center)


def smooth(field_ref, weight_ref, drive_ref, at, rows=None):
    center, beside = neighbours(field_ref, at, rows)
    rows = slice(None) if rows is None else rows
    kept = center * (1.0 - jacobi_weight) + drive_ref[at, rows, :]
    return kept + weight_ref[at, rows, :] * beside


def sweep(from_ref, to_ref, weight_ref, drive_ref, rows_x, reach):
    window_x, window_y, _ = weight_ref.shape
    own_rows = slice(window_y // 3, 2 * window_y // 3)
    for at in range(window_x):
        away = max(0, at - rows_x + 1)
        if away > reach:
            continue
        if away == reach:
            to_ref[at + 1, own_rows, :] = smooth(from_ref, weight_ref, drive_ref, at, own_rows)
        else:
            to_ref[at + 1] = smooth(from_ref, weight_ref, drive_ref, at)


def window_place(count_y, rows_y, shape):
    place_y = iota(shape, 0) + (lax.axis_index("gy") - 1) * rows_y
    inside = (place_y >= 0) & (place_y < rows_y * count_y)
    return place_y.astype(jnp.float32), inside


def mirrored(at, last):
    return jnp.where(lax.axis_index("gx") == 0, at, last - at)


def add_correction(planes, cut_x, window_x, planes_used, from_ref, to_ref):
    for at in range(planes_used):
        place_x = mirrored(at, window_x - 1).astype(jnp.float32)
        value = correction_of(planes, cut_x, place_x)
        to_ref[at + 1] = value if from_ref is None else from_ref[at + 1] + value


def clear_ends(field_ref, window_x):
    empty = jnp.zeros(field_ref.shape[1:], jnp.float32)
    field_ref[0] = empty
    field_ref[window_x + 1] = empty


def first_kernel(
    counts, scale_factor, own_ref, other_ref, even_ref, even_other_ref, odd_ref, odd_other_ref,
    ids_ref, inverse_ref, gathered_ref,
    field_ref, weight_ref, drive_ref, out_ref, spare_ref,
):
    count_x, count_y = counts
    _, rows_x, rows_y, cells_z = own_ref.shape
    window_x, window_y, _ = weight_ref.shape
    at_y = lax.axis_index("gy")
    parity = lax.rem(at_y, 2)
    even_row = pl.multiple_of((1 - parity) * 2 * rows_y, SUBLANES)
    odd_row = pl.multiple_of(parity * 2 * rows_y, SUBLANES)
    odd_inside = jnp.where((at_y > 0) & (at_y < count_y - 1), jacobi_weight, 0.0)
    for ref, first, row, scale in (
        (own_ref, 0, rows_y, jacobi_weight),
        (other_ref, rows_x, rows_y, jacobi_weight),
        (even_ref, 0, even_row, jacobi_weight),
        (even_other_ref, rows_x, even_row, jacobi_weight),
        (odd_ref, 0, odd_row, odd_inside),
        (odd_other_ref, rows_x, odd_row, odd_inside),
    ):
        for at in range(rows_x):
            plane = mirrored(at, rows_x - 1)
            weight = scale / (6.0 + ref[1, plane])
            weight_ref[first + at, pl.ds(row, rows_y), :] = weight
            drive_ref[first + at, pl.ds(row, rows_y), :] = weight * ref[0, plane]

    parts = inverse_ref.shape[0] // LANES
    rows = [gathered_ref[at : at + 1] for at in range(parts + 1)]
    cut_x, cut_y = cuts_of(rows[parts], count_x, count_y)
    place = window_place(count_y, rows_y, (window_y, cells_z))
    planes = coarse_planes(rows[:parts], inverse_ref, ids_ref, scale_factor, cut_y, place)
    clear_ends(field_ref, window_x)
    clear_ends(spare_ref, window_x)
    add_correction(planes, cut_x, window_x, window_x, None, field_ref)
    for step in range(SWEEPS):
        refs = (field_ref, spare_ref) if step % 2 == 0 else (spare_ref, field_ref)
        sweep(*refs, weight_ref, drive_ref, rows_x, 2 * SWEEPS - 1 - step)

    residual, used = [], []
    own_rows = slice(rows_y, 2 * rows_y)
    for at in range(rows_x):
        plane = mirrored(at, rows_x - 1)
        center, beside = neighbours(field_ref, at, own_rows)
        residual.append(own_ref[0, plane] - ((6.0 + own_ref[1, plane]) * center - beside))
        used.append(plane)
    partial = restrict(jnp.concatenate(residual, axis=0), ids_ref, used, inverse_ref.shape[0])
    store_copies(out_ref, partial + rows[parts:])


def second_kernel(
    counts, scale_factor, pieces,
    field_ref, weight_ref, drive_ref, ids_ref, inverse_ref, gathered_ref, *rest,
):
    out_refs, (one_ref, two_ref) = rest[:pieces], rest[pieces:]
    count_x, count_y = counts
    window_x, window_y, cells_z = weight_ref.shape
    rows_x, rows_y, chunk = out_refs[0].shape
    parts = inverse_ref.shape[0] // LANES
    gathered = jnp.sum(gathered_ref[...], axis=0)
    rows = [gathered[at : at + 1] for at in range(parts)]
    cut_x, cut_y = cuts_of(gathered_ref[0, parts : parts + 1], count_x, count_y)
    place = window_place(count_y, rows_y, (window_y, cells_z))
    planes = coarse_planes(rows, inverse_ref, ids_ref, scale_factor, cut_y, place)
    clear_ends(one_ref, window_x)
    clear_ends(two_ref, window_x)
    used = min(window_x, rows_x + SWEEPS)
    add_correction(planes, cut_x, window_x, used, field_ref, one_ref)
    fields = [one_ref, two_ref]
    for step in range(SWEEPS - 1):
        sweep(*fields, weight_ref, drive_ref, rows_x, SWEEPS - 1 - step)
        fields.reverse()
    last_ref, own_ref = fields
    own_rows = slice(rows_y, 2 * rows_y)
    for at in range(rows_x):
        value = smooth(last_ref, weight_ref, drive_ref, at, own_rows)
        own_ref[mirrored(at, rows_x - 1), pl.ds(0, rows_y), :] = value
    me = lax.axis_index("grp")
    for turn in range(pieces):
        first = pl.multiple_of(lax.bitwise_xor(me, turn) * chunk, LANES)
        for at in range(rows_x):
            out_refs[turn][at] = own_ref[at, pl.ds(0, rows_y), pl.ds(first, chunk)]


def range_kernel(pieces, omega_ref, range_ref, *rest):
    snaps, (new_ref,) = rest[:pieces], rest[pieces:]
    rows_x = range_ref.shape[1]
    me = lax.axis_index("grp")
    slots = [lax.bitwise_xor(me, turn) for turn in range(pieces)]
    cells = [[snaps[turn][at] for at in range(rows_x)] for turn in range(pieces)]
    for at_row in range(range_ref.shape[0]):
        scales = [omega_ref[slots[turn], at_row] for turn in range(pieces)]
        for at in range(rows_x):
            value = range_ref[at_row, at]
            for turn in range(pieces):
                value = value + scales[turn] * cells[turn][at]
            new_ref[at_row, at] = value


def sum_rows(values):
    sublanes = iota(values[0].shape, 0)
    shift = SUBLANES // 2
    while shift:
        low = lax.bitwise_and(sublanes, shift) == 0
        half = len(values) // 2
        values = [
            jnp.where(
                low,
                values[at] + pltpu.roll(values[at], SUBLANES - shift, 0),
                values[at + half] + pltpu.roll(values[at + half], shift, 0),
            )
            for at in range(half)
        ]
        shift //= 2
    return values[0]


def products(psi_ref, phi_ref, snaps):
    rows_x = psi_ref.shape[1]
    cells = [[snap[at] for at in range(rows_x)] for snap in snaps]
    kept = [[] for _ in snaps]
    for ref in (psi_ref, phi_ref):
        for first in range(0, ref.shape[0], SUBLANES):
            totals = [[] for _ in snaps]
            for at_row in range(first, first + SUBLANES):
                parts = [ref[at_row, at] for at in range(rows_x)]
                for turn in range(len(snaps)):
                    total = parts[0] * cells[turn][0]
                    for at in range(1, rows_x):
                        total = total + parts[at] * cells[turn][at]
                    totals[turn].append(total)
            for turn in range(len(snaps)):
                kept[turn].append(sum_rows(totals[turn]))
    count = psi_ref.shape[0] + phi_ref.shape[0]
    rest = [jnp.zeros((LANES - count, LANES), jnp.float32)] if count < LANES else []
    ones = jnp.ones((SUBLANES, LANES), jnp.float32)
    return [dot_nt(ones, jnp.concatenate(rows + rest, axis=0))[0:1] for rows in kept]


def early_kernel(pieces, psi_ref, phi_ref, *rest):
    snaps, (out_ref,) = rest[:pieces], rest[pieces:]
    for at, row in enumerate(products(psi_ref, phi_ref, snaps)):
        out_ref[at : at + 1, :] = row


def late_kernel(pieces, psi_ref, phi_ref, early_ref, *rest):
    snaps, (out_ref,) = rest[:pieces], rest[pieces:]
    me = lax.axis_index("grp")
    early = early_ref.shape[0]
    rows = [early_ref[at : at + 1, :] for at in range(early)]
    rows += products(psi_ref, phi_ref, snaps)
    for turn, row in enumerate(rows):
        slot = lax.bitwise_xor(me, turn)
        for copy in range(out_ref.shape[0]):
            out_ref[copy, pl.ds(slot, 1), :] = row


def end_kernel(gathered_ref, xi_ref, core_ref, corange_out_ref, core_out_ref):
    corange = corange_out_ref.shape[1]
    core = core_ref.shape[0]
    total = jnp.sum(gathered_ref[...], axis=0)
    corange_out_ref[...] = total[:, :corange]
    images = total[:, corange : corange + core]
    core_out_ref[...] = core_ref[...] + dot_tn(images, xi_ref[...])


vmem = pl.BlockSpec(memory_space=pltpu.VMEM)
smem = pl.BlockSpec(memory_space=pltpu.SMEM)


def call(kernel, outs, inputs, scratch=(), specs=None):
    many = isinstance(outs, list)
    shapes = [jax.ShapeDtypeStruct(shape, jnp.float32) for shape in (outs if many else [outs])]
    result = pl.pallas_call(
        kernel,
        out_shape=shapes,
        in_specs=specs or [vmem] * len(inputs),
        out_specs=[vmem] * len(shapes),
        scratch_shapes=[pltpu.VMEM(shape, jnp.float32) for shape in scratch],
        compiler_params=pltpu.CompilerParams(vmem_limit_bytes=VMEM_BYTES),
    )(*inputs)
    return result if many else result[0]


def in_hbm(array):
    return pltpu.with_memory_space_constraint(array, pltpu.HBM)


def gather(copies, axes):
    return lax.all_to_all(copies, axes, 0, 0)


def fast_body(
    sources, diagonal, coarse_ids, coarse_inverse, omega_rows, psi, phi, xi_cols, range_sketch,
    core_sketch,
):
    source = sources[0]
    rows_x, rows_y, cells_z = source.shape
    counts = (lax.axis_size("gx"), lax.axis_size("gy"))
    groups = lax.axis_size("grp")
    count_x, count_y = counts
    coarse = coarse_inverse.shape[0]
    scale_factor = coarse / (rows_x * count_x * rows_y * count_y * cells_z)
    window = (rows_x * count_x, 3 * rows_y, cells_z)
    padded = (window[0] + 2,) + window[1:]
    copies = (count_x * count_y, coarse // LANES + 1, LANES)

    def place(group, x, y):
        return (group * count_x + x) * count_y + y

    def partner(group, x, y, phase):
        if phase is None:
            return place(group, x ^ 1, y)
        beyond = y ^ 1 if phase == 0 else ((y + 1) ^ 1) - 1
        return place(group, x, beyond) if 0 <= beyond < count_y else place(group ^ 1, x, y)

    def pairs(phase):
        return [
            (place(group, x, y), partner(group, x, y, phase))
            for group in range(groups)
            for x in range(count_x)
            for y in range(count_y)
        ]

    mine, ids, inverse, begin = pl.pallas_call(
        begin_kernel,
        out_shape=[
            jax.ShapeDtypeStruct((2,) + source.shape, jnp.float32),
            jax.ShapeDtypeStruct(coarse_ids.shape, jnp.int32),
            jax.ShapeDtypeStruct(coarse_inverse.shape, jnp.float32),
            jax.ShapeDtypeStruct(copies[1:], jnp.float32),
        ],
        in_specs=[pl.BlockSpec(memory_space=pltpu.HBM)] * 4,
        out_specs=[vmem] * 4,
        scratch_shapes=[pltpu.SemaphoreType.DMA((4,))],
        compiler_params=pltpu.CompilerParams(vmem_limit_bytes=VMEM_BYTES),
        name="begin",
    )(*map(in_hbm, (source, diagonal, coarse_ids, coarse_inverse)))
    others = []
    for at, phase in enumerate((None, 0, 0, 1, 1)):
        sent = others[0] if at in (2, 4) else mine
        others.append(lax.ppermute(sent, ("grp", "gx", "gy"), pairs(phase)))
    gathered = begin
    bits = [1 << bit for bit in reversed(range(count_y.bit_length() - 1))]
    turns = [("gy", count_y, bit) for bit in bits]
    turns.append(("gx", count_x, 1))
    for axis, count, bit in turns:
        gathered = gathered + lax.ppermute(gathered, axis, [(i, i ^ bit) for i in range(count)])
    field, weight, drive, partial = call(
        functools.partial(first_kernel, counts, scale_factor),
        [padded, window, window, copies],
        (mine, *others, ids, inverse, gathered),
        scratch=[padded],
    )
    gathered = gather(partial, ("gx", "gy"))
    chunk = cells_z // groups
    pieces = call(
        functools.partial(second_kernel, counts, scale_factor, groups),
        [(rows_x, rows_y, chunk)] * groups,
        (field, weight, drive, ids, inverse, gathered),
        scratch=[padded, padded],
    )
    snaps = [pieces[0]] + [
        lax.ppermute(pieces[turn], "grp", [(at, at ^ turn) for at in range(groups)])
        for turn in range(1, groups)
    ]
    early = max(1, groups // 2)
    kept = call(functools.partial(early_kernel, early), (early, LANES), (psi, phi, *snaps[:early]))
    sketched = call(
        functools.partial(late_kernel, groups - early),
        (groups * count_x * count_y, groups, LANES),
        (psi, phi, kept, *snaps[early:]),
    )
    gathered = gather(sketched, ("grp", "gx", "gy"))
    range_new = call(
        functools.partial(range_kernel, groups),
        range_sketch.shape,
        (omega_rows, range_sketch, *snaps),
        specs=[smem] + [vmem] * (1 + groups),
    )
    corange_cols, core_new = call(
        end_kernel, [(groups, psi.shape[0]), core_sketch.shape], (gathered, xi_cols.T, core_sketch)
    )
    return range_new, corange_cols.T, core_new


def with_halo(cells, sides, width):
    for axis, dim in sides:
        count = lax.axis_size(axis)
        ends = count - 1
        head = lax.slice_in_dim(cells, 0, width, axis=dim)
        tail = lax.slice_in_dim(cells, cells.shape[dim] - width, cells.shape[dim], axis=dim)
        cells = jnp.concatenate(
            [
                lax.ppermute(tail, axis, [(i, (i + 1) % count) for i in range(ends)]),
                cells,
                lax.ppermute(head, axis, [((i + 1) % count, i) for i in range(ends)]),
            ],
            axis=dim,
        )
    return cells


def neighbour_image(widened, diagonal):
    center = widened[1:-1, 1:-1]
    beside = widened[2:, 1:-1] + widened[:-2, 1:-1]
    beside = beside + widened[1:-1, 2:] + widened[1:-1, :-2]
    padded = jnp.pad(center, ((0, 0), (0, 0), (1, 1)))
    beside = beside + padded[:, :, 2:] + padded[:, :, :-2]
    return (center, (6.0 + diagonal) * center - beside)


def smooth_once(widened, source, diagonal):
    center, applied = neighbour_image(widened, diagonal)
    return center + jacobi_weight * (source - applied) / (6.0 + diagonal)


def widen_faces(values):
    return with_halo(values, (("gx", 0), ("gy", 1)), 1)


def axis_maps(coarse_ids):
    ranks_x = coarse_ids[:, 0, 0] // (XY_CUTS * Z_CUTS)
    ranks_y = coarse_ids[0, :, 0] // Z_CUTS % XY_CUTS
    ranks_z = coarse_ids[0, 0, :] % Z_CUTS
    cuts_xy = jnp.arange(XY_CUTS, dtype=jnp.int32)
    cuts_z = jnp.arange(Z_CUTS, dtype=jnp.int32)
    map_x = (ranks_x[:, None] == cuts_xy[None, :]).astype(jnp.float32)
    map_y = (ranks_y[:, None] == cuts_xy[None, :]).astype(jnp.float32)
    map_z = (ranks_z[:, None] == cuts_z[None, :]).astype(jnp.float32)
    return (map_x, map_y, map_z)


def restrict_cells(values, maps):
    map_x, map_y, map_z = maps
    rows_x, rows_y, cells_z = values.shape
    along_z = jnp.dot(values.reshape(rows_x * rows_y, cells_z), map_z, precision=highest)
    along_z = along_z.reshape(rows_x, rows_y, Z_CUTS)
    along_y = jnp.einsum("xyc,yb->xbc", along_z, map_y, precision=highest)
    along_x = jnp.einsum("xbc,xa->abc", along_y, map_x, precision=highest)
    return along_x.reshape(-1)


def prolong(correction, maps, extent):
    map_x, map_y, map_z = maps
    boxes = correction.reshape(XY_CUTS, XY_CUTS, Z_CUTS)
    over_x = jnp.einsum("abc,xa->xbc", boxes, map_x, precision=highest)
    over_y = jnp.einsum("xbc,yb->xyc", over_x, map_y, precision=highest)
    spread = jnp.dot(over_y.reshape(extent[0] * extent[1], Z_CUTS), map_z.T, precision=highest)
    return spread.reshape(extent)


def general_body(
    sources,
    diagonal,
    coarse_ids,
    coarse_inverse,
    omega_rows,
    psi,
    phi,
    xi_cols,
    range_sketch,
    core_sketch,
):
    source = sources[0]
    rows_x, rows_y, cells_z = source.shape
    coarse = coarse_inverse.shape[0]
    total_cells = rows_x * lax.axis_size("gx") * rows_y * lax.axis_size("gy") * cells_z
    scale_factor = coarse / total_cells
    maps = axis_maps(coarse_ids)
    stacked = jnp.stack([source, diagonal])
    margin = with_halo(stacked, (("gx", 1), ("gy", 2)), 2)
    place_x = lax.axis_index("gx") * rows_x + jnp.arange(rows_x + 4) - 2
    place_y = lax.axis_index("gy") * rows_y + jnp.arange(rows_y + 4) - 2
    inside_x = ((place_x >= 0) & (place_x < rows_x * lax.axis_size("gx"))).astype(jnp.float32)
    inside_y = ((place_y >= 0) & (place_y < rows_y * lax.axis_size("gy"))).astype(jnp.float32)
    inside = inside_x[:, None, None] * inside_y[None, :, None]
    pressure = jnp.zeros_like(source)
    for outer_step in range(OUTER):
        if outer_step == 0:
            residual = source
        else:
            residual = source - neighbour_image(widen_faces(pressure), diagonal)[1]
        coarse_rhs = lax.psum(restrict_cells(residual, maps), ("gx", "gy"))
        correction = jnp.dot(coarse_inverse, coarse_rhs * scale_factor, precision=highest)
        pressure = pressure + prolong(correction, maps, source.shape)
        for _ in range(SWEEPS // 2):
            widened = with_halo(pressure, (("gx", 0), ("gy", 1)), 2)
            halfway = (
                smooth_once(widened, margin[0, 1:-1, 1:-1], margin[1, 1:-1, 1:-1])
                * inside[1:-1, 1:-1]
            )
            pressure = smooth_once(halfway, source, diagonal)
    snapshot = lax.all_to_all(pressure[None], "grp", split_axis=3, concat_axis=0, tiled=True)
    columns = snapshot.reshape(snapshot.shape[0], -1)
    range_flat = range_sketch.reshape(range_sketch.shape[0], -1)
    range_new = range_flat + jnp.einsum("tk,tc->kc", omega_rows, columns, precision=highest)
    corange_part = jnp.einsum(
        "lc,tc->lt", psi.reshape(psi.shape[0], -1), columns, precision=highest
    )
    core_part = jnp.einsum("sc,tc->st", phi.reshape(phi.shape[0], -1), columns, precision=highest)
    corange_cols, core_images = lax.psum((corange_part, core_part), ("grp", "gx", "gy"))
    core_new = core_sketch + jnp.dot(core_images, xi_cols.T, precision=highest)
    return (range_new.reshape(range_sketch.shape), corange_cols, core_new)


def body(*arrays):
    _, rows_y, cells_z = arrays[1].shape
    coarse, groups = arrays[3].shape[0], lax.axis_size("grp")
    fits = (
        lax.axis_size("gx") == 2
        and lax.axis_size("gy") & (lax.axis_size("gy") - 1) == 0
        and lax.axis_size("gy") > 1
        and rows_y >= OUTER * SWEEPS
        and OUTER == 2
        and rows_y == SUBLANES
        and coarse == XY_CUTS * XY_CUTS * Z_CUTS
        and groups & (groups - 1) == 0
        and 1 < groups <= SUBLANES
        and cells_z % (groups * LANES) == 0
        and cells_z // groups == LANES
        and coarse % LANES == 0
        and arrays[5].shape[0] % SUBLANES == 0
        and arrays[6].shape[0] % SUBLANES == 0
        and arrays[5].shape[0] + arrays[6].shape[0] <= LANES
    )
    if not fits:
        return general_body(*arrays)
    return fast_body(*arrays)


def solution(mesh):
    return jax.shard_map(
        body,
        mesh=mesh,
        in_specs=(
            P("grp", "gx", "gy", None),
            P("gx", "gy", None),
            P("gx", "gy", None),
            P(),
            P(),
            P(None, "gx", "gy", "grp"),
            P(None, "gx", "gy", "grp"),
            P(),
            P(None, "gx", "gy", "grp"),
            P(),
        ),
        out_specs=(P(None, "gx", "gy", "grp"), P(), P()),
        check_vma=False,
    )
```

```python
import functools

import jax
import jax.numpy as jnp
from jax import lax
from jax.experimental import pallas as pl
from jax.experimental.pallas import tpu as pltpu
from jax.sharding import PartitionSpec as P


OUTER = 2
SWEEPS = 4
XY_CUTS = 4
Z_CUTS = 16
XY_BITS = XY_CUTS.bit_length() - 1
Z_BITS = Z_CUTS.bit_length() - 1
LANES = 128
SUBLANES = 8
VMEM_BYTES = 16 * 2**20

jacobi_weight = 2.0 / 3.0
highest = lax.Precision.HIGHEST


def dot_nt(a, b):
    return lax.dot_general(
        a, b, (((1,), (1,)), ((), ())), precision=highest, preferred_element_type=jnp.float32
    )


def dot_tn(a, b):
    return lax.dot_general(
        a, b, (((0,), (0,)), ((), ())), precision=highest, preferred_element_type=jnp.float32
    )


def iota(shape, dim):
    return lax.broadcasted_iota(jnp.int32, shape, dim)


def store_copies(out_ref, rows):
    for copy in range(out_ref.shape[0]):
        for at, row in enumerate(rows):
            out_ref[copy, at : at + 1, :] = row


def box_of(ids_ref, at):
    return lax.shift_right_logical(ids_ref[at, :, :LANES], Z_BITS)


def restrict(values, ids_ref, planes, coarse):
    cells_z = values.shape[1]
    rows_y = ids_ref.shape[1]
    ranks = lax.bitwise_and(ids_ref[0, 0:1, :], Z_CUTS - 1)
    members = lax.bitwise_and(iota((LANES, cells_z), 0), Z_CUTS - 1) == ranks
    sums = dot_nt(values, members.astype(jnp.float32))
    lane_box = lax.shift_right_logical(iota((rows_y, LANES), 1), Z_BITS)
    rows = []
    for part in range(coarse // LANES):
        total = None
        for at, plane in enumerate(planes):
            own = box_of(ids_ref, plane) == lane_box + part * (LANES // Z_CUTS)
            kept = jnp.where(own, sums[at * rows_y : (at + 1) * rows_y], 0.0)
            total = kept if total is None else total + kept
        rows.append(jnp.sum(total, axis=0, keepdims=True))
    return rows


def begin_kernel(
    source_from, diagonal_from, ids_from, inverse_from,
    mine_ref, ids_ref, inverse_ref, out_ref, arrived,
):
    loads = [
        pltpu.make_async_copy(source, target, arrived.at[at])
        for at, (source, target) in enumerate(
            (
                (ids_from, ids_ref),
                (source_from, mine_ref.at[0]),
                (diagonal_from, mine_ref.at[1]),
                (inverse_from, inverse_ref),
            )
        )
    ]
    for load in loads:
        load.start()
    coarse = inverse_ref.shape[0]
    rows_x, rows_y, cells_z = ids_ref.shape
    loads[0].wait()
    lanes = iota((1, LANES), 1)
    boxes = [box_of(ids_ref, at) for at in range(rows_x)]
    below_x = jnp.zeros((1, LANES), jnp.float32)
    for box in boxes:
        below_x = below_x + (lax.shift_right_logical(box[0:1], XY_BITS) <= lanes).astype(jnp.float32)
    ranks_y = lax.bitwise_and(boxes[0], XY_CUTS - 1)
    below_y = jnp.sum((ranks_y <= lanes - XY_CUTS).astype(jnp.float32), axis=0, keepdims=True)
    loads[1].wait()
    rows = restrict(
        mine_ref[0].reshape(rows_x * rows_y, cells_z), ids_ref, range(rows_x), coarse
    ) + [jnp.where(lanes < XY_CUTS, below_x, below_y)]
    for at, part in enumerate(rows):
        out_ref[at : at + 1, :] = part
    loads[2].wait()
    loads[3].wait()


def coarse_planes(rows, inverse_ref, ids_ref, scale_factor, cut_y, place):
    coarse = inverse_ref.shape[0]
    cells_z = ids_ref.shape[2]
    per_part = LANES // Z_CUTS
    row = jnp.broadcast_to(jnp.concatenate(rows, axis=1) * scale_factor, (SUBLANES, coarse))
    solved = dot_nt(row, inverse_ref[...])
    shape = (per_part, LANES)
    own = lax.shift_right_logical(iota(shape, 1), Z_BITS) == iota(shape, 0)
    lines = []
    for part in range(coarse // LANES):
        values = jnp.where(own, solved[:per_part, part * LANES : (part + 1) * LANES], 0.0)
        shift = LANES // 2
        while shift >= Z_CUTS:
            values = values + pltpu.roll(values, shift, 1)
            shift //= 2
        along_z = jnp.concatenate(
            [
                jnp.take_along_axis(
                    values,
                    lax.bitwise_and(ids_ref[0, :per_part, at : at + LANES], Z_CUTS - 1),
                    axis=1,
                )
                for at in range(0, cells_z, LANES)
            ],
            axis=1,
        )
        lines.extend(along_z[at : at + 1] for at in range(per_part))
    place_y, inside = place
    planes = []
    for box_x in range(XY_CUTS):
        first = box_x * XY_CUTS
        plane = jnp.broadcast_to(lines[first], place_y.shape)
        for box_y in range(1, XY_CUTS):
            plane = jnp.where(place_y >= cut_y[box_y - 1], lines[first + box_y], plane)
        planes.append(jnp.where(inside, plane, 0.0))
    return planes


def correction_of(planes, cut_x, place_x):
    value = planes[0]
    for box_x in range(1, XY_CUTS):
        value = jnp.where(cut_x[box_x - 1] <= place_x, planes[box_x], value)
    return value


def cuts_of(row, count_x, count_y):
    cut_x = [row[:, at : at + 1] * (1.0 / count_y) for at in range(XY_CUTS - 1)]
    cut_y = [row[:, XY_CUTS + at : XY_CUTS + at + 1] * (1.0 / count_x) for at in range(XY_CUTS - 1)]
    return cut_x, cut_y


def beside_z(values):
    lanes = iota((values.shape[0], LANES), 1)
    tiles = [values[:, at : at + LANES] for at in range(0, values.shape[1], LANES)]
    empty = jnp.zeros_like(tiles[0])
    ahead = [pltpu.roll(tile, LANES - 1, 1) for tile in tiles] + [empty]
    behind = [empty] + [pltpu.roll(tile, 1, 1) for tile in tiles]
    return jnp.concatenate(
        [
            jnp.where(lanes == LANES - 1, ahead[at + 1], ahead[at])
            + jnp.where(lanes == 0, behind[at], behind[at + 1])
            for at in range(len(tiles))
        ],
        axis=1,
    )


def beside_y(values):
    rows = values.shape[0]
    return pltpu.roll(values, rows - 1, 0) + pltpu.roll(values, 1, 0)


def neighbours(field_ref, at, rows=None):
    center = field_ref[at + 1]
    along_y = beside_y(center)
    if rows is None:
        rows = slice(0, center.shape[0])
    center = center[rows]
    across = field_ref[at, rows, :] + field_ref[at + 2, rows, :]
    return center, across + along_y[rows] + beside_z(center)


def smooth(field_ref, weight_ref, drive_ref, at, rows=None):
    center, beside = neighbours(field_ref, at, rows)
    rows = slice(None) if rows is None else rows
    kept = center * (1.0 - jacobi_weight) + drive_ref[at, rows, :]
    return kept + weight_ref[at, rows, :] * beside


def sweep(from_ref, to_ref, weight_ref, drive_ref, rows_x, reach):
    window_x, window_y, _ = weight_ref.shape
    own_rows = slice(window_y // 3, 2 * window_y // 3)
    for at in range(window_x):
        away = max(0, at - rows_x + 1)
        if away > reach:
            continue
        if away == reach:
            to_ref[at + 1, own_rows, :] = smooth(from_ref, weight_ref, drive_ref, at, own_rows)
        else:
            to_ref[at + 1] = smooth(from_ref, weight_ref, drive_ref, at)


def window_place(count_y, rows_y, shape):
    place_y = iota(shape, 0) + (lax.axis_index("gy") - 1) * rows_y
    inside = (place_y >= 0) & (place_y < rows_y * count_y)
    return place_y.astype(jnp.float32), inside


def mirrored(at, last):
    return jnp.where(lax.axis_index("gx") == 0, at, last - at)


def add_correction(planes, cut_x, window_x, planes_used, from_ref, to_ref):
    for at in range(planes_used):
        place_x = mirrored(at, window_x - 1).astype(jnp.float32)
        value = correction_of(planes, cut_x, place_x)
        to_ref[at + 1] = value if from_ref is None else from_ref[at + 1] + value


def clear_ends(field_ref, window_x):
    empty = jnp.zeros(field_ref.shape[1:], jnp.float32)
    field_ref[0] = empty
    field_ref[window_x + 1] = empty


def fill(blocks, weight_ref, drive_ref):
    for ref, first, row, scale in blocks:
        _, rows_x, rows_y, _ = ref.shape
        for at in range(rows_x):
            plane = mirrored(at, rows_x - 1)
            weight = scale / (6.0 + ref[1, plane])
            weight_ref[first + at, pl.ds(row, rows_y), :] = weight
            drive_ref[first + at, pl.ds(row, rows_y), :] = weight * ref[0, plane]


def pair_places(count_y, rows_y):
    at_y = lax.axis_index("gy")
    parity = lax.rem(at_y, 2)
    even_row = pl.multiple_of((1 - parity) * 2 * rows_y, SUBLANES)
    odd_row = pl.multiple_of(parity * 2 * rows_y, SUBLANES)
    odd_inside = jnp.where((at_y > 0) & (at_y < count_y - 1), jacobi_weight, 0.0)
    return even_row, odd_row, odd_inside


def prepare_kernel(count_y, own_ref, other_ref, even_ref, odd_ref, weight_ref, drive_ref):
    _, rows_x, rows_y, _ = own_ref.shape
    even_row, odd_row, odd_inside = pair_places(count_y, rows_y)
    blocks = (
        (own_ref, 0, rows_y, jacobi_weight),
        (other_ref, rows_x, rows_y, jacobi_weight),
        (even_ref, 0, even_row, jacobi_weight),
        (odd_ref, 0, odd_row, odd_inside),
    )
    fill(blocks, weight_ref, drive_ref)


def first_kernel(
    counts, scale_factor, own_ref, even_other_ref, odd_other_ref, ids_ref, inverse_ref,
    gathered_ref, weight_from, drive_from,
    field_ref, weight_ref, drive_ref, out_ref, spare_ref,
):
    count_x, count_y = counts
    _, rows_x, rows_y, cells_z = own_ref.shape
    window_x, window_y, _ = weight_ref.shape
    even_row, odd_row, odd_inside = pair_places(count_y, rows_y)
    blocks = (
        (even_other_ref, rows_x, even_row, jacobi_weight),
        (odd_other_ref, rows_x, odd_row, odd_inside),
    )
    fill(blocks, weight_ref, drive_ref)

    parts = inverse_ref.shape[0] // LANES
    rows = [gathered_ref[at : at + 1] for at in range(parts + 1)]
    cut_x, cut_y = cuts_of(rows[parts], count_x, count_y)
    place = window_place(count_y, rows_y, (window_y, cells_z))
    planes = coarse_planes(rows[:parts], inverse_ref, ids_ref, scale_factor, cut_y, place)
    clear_ends(field_ref, window_x)
    clear_ends(spare_ref, window_x)
    add_correction(planes, cut_x, window_x, window_x, None, field_ref)
    for step in range(SWEEPS):
        refs = (field_ref, spare_ref) if step % 2 == 0 else (spare_ref, field_ref)
        sweep(*refs, weight_ref, drive_ref, rows_x, 2 * SWEEPS - 1 - step)

    residual, used = [], []
    own_rows = slice(rows_y, 2 * rows_y)
    for at in range(rows_x):
        plane = mirrored(at, rows_x - 1)
        center, beside = neighbours(field_ref, at, own_rows)
        residual.append(own_ref[0, plane] - ((6.0 + own_ref[1, plane]) * center - beside))
        used.append(plane)
    partial = restrict(jnp.concatenate(residual, axis=0), ids_ref, used, inverse_ref.shape[0])
    store_copies(out_ref, partial + rows[parts:])


def second_kernel(
    counts, scale_factor, pieces,
    field_ref, weight_ref, drive_ref, ids_ref, inverse_ref, gathered_ref, *rest,
):
    out_refs, (one_ref, two_ref) = rest[:pieces], rest[pieces:]
    count_x, count_y = counts
    window_x, window_y, cells_z = weight_ref.shape
    rows_x, rows_y, chunk = out_refs[0].shape
    parts = inverse_ref.shape[0] // LANES
    gathered = jnp.sum(gathered_ref[...], axis=0)
    rows = [gathered[at : at + 1] for at in range(parts)]
    cut_x, cut_y = cuts_of(gathered_ref[0, parts : parts + 1], count_x, count_y)
    place = window_place(count_y, rows_y, (window_y, cells_z))
    planes = coarse_planes(rows, inverse_ref, ids_ref, scale_factor, cut_y, place)
    clear_ends(one_ref, window_x)
    clear_ends(two_ref, window_x)
    used = min(window_x, rows_x + SWEEPS)
    add_correction(planes, cut_x, window_x, used, field_ref, one_ref)
    fields = [one_ref, two_ref]
    for step in range(SWEEPS - 1):
        sweep(*fields, weight_ref, drive_ref, rows_x, SWEEPS - 1 - step)
        fields.reverse()
    last_ref, own_ref = fields
    own_rows = slice(rows_y, 2 * rows_y)
    for at in range(rows_x):
        value = smooth(last_ref, weight_ref, drive_ref, at, own_rows)
        own_ref[mirrored(at, rows_x - 1), pl.ds(0, rows_y), :] = value
    me = lax.axis_index("grp")
    for turn in range(pieces):
        first = pl.multiple_of(lax.bitwise_xor(me, turn) * chunk, LANES)
        for at in range(rows_x):
            out_refs[turn][at] = own_ref[at, pl.ds(0, rows_y), pl.ds(first, chunk)]


def range_kernel(pieces, omega_ref, range_ref, *rest):
    snaps, (new_ref,) = rest[:pieces], rest[pieces:]
    rows_x = range_ref.shape[1]
    me = lax.axis_index("grp")
    slots = [lax.bitwise_xor(me, turn) for turn in range(pieces)]
    cells = [[snaps[turn][at] for at in range(rows_x)] for turn in range(pieces)]
    for at_row in range(range_ref.shape[0]):
        scales = [omega_ref[slots[turn], at_row] for turn in range(pieces)]
        for at in range(rows_x):
            value = range_ref[at_row, at]
            for turn in range(pieces):
                value = value + scales[turn] * cells[turn][at]
            new_ref[at_row, at] = value


def sum_rows(values):
    sublanes = iota(values[0].shape, 0)
    shift = SUBLANES // 2
    while shift:
        low = lax.bitwise_and(sublanes, shift) == 0
        half = len(values) // 2
        values = [
            jnp.where(
                low,
                values[at] + pltpu.roll(values[at], SUBLANES - shift, 0),
                values[at + half] + pltpu.roll(values[at + half], shift, 0),
            )
            for at in range(half)
        ]
        shift //= 2
    return values[0]


def products(psi_ref, phi_ref, snaps):
    rows_x = psi_ref.shape[1]
    cells = [[snap[at] for at in range(rows_x)] for snap in snaps]
    kept = [[] for _ in snaps]
    for ref in (psi_ref, phi_ref):
        for first in range(0, ref.shape[0], SUBLANES):
            totals = [[] for _ in snaps]
            for at_row in range(first, first + SUBLANES):
                parts = [ref[at_row, at] for at in range(rows_x)]
                for turn in range(len(snaps)):
                    total = parts[0] * cells[turn][0]
                    for at in range(1, rows_x):
                        total = total + parts[at] * cells[turn][at]
                    totals[turn].append(total)
            for turn in range(len(snaps)):
                kept[turn].append(sum_rows(totals[turn]))
    count = psi_ref.shape[0] + phi_ref.shape[0]
    rest = [jnp.zeros((LANES - count, LANES), jnp.float32)] if count < LANES else []
    ones = jnp.ones((SUBLANES, LANES), jnp.float32)
    return [dot_nt(ones, jnp.concatenate(rows + rest, axis=0))[0:1] for rows in kept]


def early_kernel(pieces, psi_ref, phi_ref, *rest):
    snaps, (out_ref,) = rest[:pieces], rest[pieces:]
    for at, row in enumerate(products(psi_ref, phi_ref, snaps)):
        out_ref[at : at + 1, :] = row


def late_kernel(pieces, psi_ref, phi_ref, early_ref, *rest):
    snaps, (out_ref,) = rest[:pieces], rest[pieces:]
    me = lax.axis_index("grp")
    early = early_ref.shape[0]
    rows = [early_ref[at : at + 1, :] for at in range(early)]
    rows += products(psi_ref, phi_ref, snaps)
    for turn, row in enumerate(rows):
        slot = lax.bitwise_xor(me, turn)
        for copy in range(out_ref.shape[0]):
            out_ref[copy, pl.ds(slot, 1), :] = row


def end_kernel(gathered_ref, xi_ref, core_ref, corange_out_ref, core_out_ref):
    corange = corange_out_ref.shape[1]
    core = core_ref.shape[0]
    total = jnp.sum(gathered_ref[...], axis=0)
    corange_out_ref[...] = total[:, :corange]
    images = total[:, corange : corange + core]
    core_out_ref[...] = core_ref[...] + dot_tn(images, xi_ref[...])


vmem = pl.BlockSpec(memory_space=pltpu.VMEM)
smem = pl.BlockSpec(memory_space=pltpu.SMEM)


def call(kernel, outs, inputs, scratch=(), specs=None, aliases=None):
    many = isinstance(outs, list)
    shapes = [jax.ShapeDtypeStruct(shape, jnp.float32) for shape in (outs if many else [outs])]
    result = pl.pallas_call(
        kernel,
        out_shape=shapes,
        in_specs=specs or [vmem] * len(inputs),
        out_specs=[vmem] * len(shapes),
        scratch_shapes=[pltpu.VMEM(shape, jnp.float32) for shape in scratch],
        compiler_params=pltpu.CompilerParams(vmem_limit_bytes=VMEM_BYTES),
        input_output_aliases=aliases or {},
    )(*inputs)
    return result if many else result[0]


def in_hbm(array):
    return pltpu.with_memory_space_constraint(array, pltpu.HBM)


def gather(copies, axes):
    return lax.all_to_all(copies, axes, 0, 0)


def fast_body(
    sources, diagonal, coarse_ids, coarse_inverse, omega_rows, psi, phi, xi_cols, range_sketch,
    core_sketch,
):
    source = sources[0]
    rows_x, rows_y, cells_z = source.shape
    counts = (lax.axis_size("gx"), lax.axis_size("gy"))
    groups = lax.axis_size("grp")
    count_x, count_y = counts
    coarse = coarse_inverse.shape[0]
    scale_factor = coarse / (rows_x * count_x * rows_y * count_y * cells_z)
    window = (rows_x * count_x, 3 * rows_y, cells_z)
    padded = (window[0] + 2,) + window[1:]
    copies = (count_x * count_y, coarse // LANES + 1, LANES)

    def place(group, x, y):
        return (group * count_x + x) * count_y + y

    def partner(group, x, y, phase):
        if phase is None:
            return place(group, x ^ 1, y)
        beyond = y ^ 1 if phase == 0 else ((y + 1) ^ 1) - 1
        return place(group, x, beyond) if 0 <= beyond < count_y else place(group ^ 1, x, y)

    def pairs(phase):
        return [
            (place(group, x, y), partner(group, x, y, phase))
            for group in range(groups)
            for x in range(count_x)
            for y in range(count_y)
        ]

    mine, ids, inverse, begin = pl.pallas_call(
        begin_kernel,
        out_shape=[
            jax.ShapeDtypeStruct((2,) + source.shape, jnp.float32),
            jax.ShapeDtypeStruct(coarse_ids.shape, jnp.int32),
            jax.ShapeDtypeStruct(coarse_inverse.shape, jnp.float32),
            jax.ShapeDtypeStruct(copies[1:], jnp.float32),
        ],
        in_specs=[pl.BlockSpec(memory_space=pltpu.HBM)] * 4,
        out_specs=[vmem] * 4,
        scratch_shapes=[pltpu.SemaphoreType.DMA((4,))],
        compiler_params=pltpu.CompilerParams(vmem_limit_bytes=VMEM_BYTES),
        name="begin",
    )(*map(in_hbm, (source, diagonal, coarse_ids, coarse_inverse)))
    others = []
    for at, phase in enumerate((None, 0, 0, 1, 1)):
        sent = others[0] if at in (2, 4) else mine
        others.append(lax.ppermute(sent, ("grp", "gx", "gy"), pairs(phase)))
    gathered = begin
    bits = [1 << bit for bit in reversed(range(count_y.bit_length() - 1))]
    turns = [("gy", count_y, bit) for bit in bits]
    turns.append(("gx", count_x, 1))
    for axis, count, bit in turns:
        gathered = gathered + lax.ppermute(gathered, axis, [(i, i ^ bit) for i in range(count)])
    prepared = call(
        functools.partial(prepare_kernel, count_y),
        [window, window],
        (mine, others[0], others[1], others[3]),
    )
    field, weight, drive, partial = call(
        functools.partial(first_kernel, counts, scale_factor),
        [padded, window, window, copies],
        (mine, others[2], others[4], ids, inverse, gathered, *prepared),
        scratch=[padded],
        aliases={6: 1, 7: 2},
    )
    gathered = gather(partial, ("gx", "gy"))
    chunk = cells_z // groups
    pieces = call(
        functools.partial(second_kernel, counts, scale_factor, groups),
        [(rows_x, rows_y, chunk)] * groups,
        (field, weight, drive, ids, inverse, gathered),
        scratch=[padded, padded],
    )
    snaps = [pieces[0]] + [
        lax.ppermute(pieces[turn], "grp", [(at, at ^ turn) for at in range(groups)])
        for turn in range(1, groups)
    ]
    early = max(1, groups // 2)
    kept = call(functools.partial(early_kernel, early), (early, LANES), (psi, phi, *snaps[:early]))
    sketched = call(
        functools.partial(late_kernel, groups - early),
        (groups * count_x * count_y, groups, LANES),
        (psi, phi, kept, *snaps[early:]),
    )
    gathered = gather(sketched, ("grp", "gx", "gy"))
    range_new = call(
        functools.partial(range_kernel, groups),
        range_sketch.shape,
        (omega_rows, range_sketch, *snaps),
        specs=[smem] + [vmem] * (1 + groups),
    )
    corange_cols, core_new = call(
        end_kernel, [(groups, psi.shape[0]), core_sketch.shape], (gathered, xi_cols.T, core_sketch)
    )
    return range_new, corange_cols.T, core_new


def with_halo(cells, sides, width):
    for axis, dim in sides:
        count = lax.axis_size(axis)
        ends = count - 1
        head = lax.slice_in_dim(cells, 0, width, axis=dim)
        tail = lax.slice_in_dim(cells, cells.shape[dim] - width, cells.shape[dim], axis=dim)
        cells = jnp.concatenate(
            [
                lax.ppermute(tail, axis, [(i, (i + 1) % count) for i in range(ends)]),
                cells,
                lax.ppermute(head, axis, [((i + 1) % count, i) for i in range(ends)]),
            ],
            axis=dim,
        )
    return cells


def neighbour_image(widened, diagonal):
    center = widened[1:-1, 1:-1]
    beside = widened[2:, 1:-1] + widened[:-2, 1:-1]
    beside = beside + widened[1:-1, 2:] + widened[1:-1, :-2]
    padded = jnp.pad(center, ((0, 0), (0, 0), (1, 1)))
    beside = beside + padded[:, :, 2:] + padded[:, :, :-2]
    return (center, (6.0 + diagonal) * center - beside)


def smooth_once(widened, source, diagonal):
    center, applied = neighbour_image(widened, diagonal)
    return center + jacobi_weight * (source - applied) / (6.0 + diagonal)


def widen_faces(values):
    return with_halo(values, (("gx", 0), ("gy", 1)), 1)


def axis_maps(coarse_ids):
    ranks_x = coarse_ids[:, 0, 0] // (XY_CUTS * Z_CUTS)
    ranks_y = coarse_ids[0, :, 0] // Z_CUTS % XY_CUTS
    ranks_z = coarse_ids[0, 0, :] % Z_CUTS
    cuts_xy = jnp.arange(XY_CUTS, dtype=jnp.int32)
    cuts_z = jnp.arange(Z_CUTS, dtype=jnp.int32)
    map_x = (ranks_x[:, None] == cuts_xy[None, :]).astype(jnp.float32)
    map_y = (ranks_y[:, None] == cuts_xy[None, :]).astype(jnp.float32)
    map_z = (ranks_z[:, None] == cuts_z[None, :]).astype(jnp.float32)
    return (map_x, map_y, map_z)


def restrict_cells(values, maps):
    map_x, map_y, map_z = maps
    rows_x, rows_y, cells_z = values.shape
    along_z = jnp.dot(values.reshape(rows_x * rows_y, cells_z), map_z, precision=highest)
    along_z = along_z.reshape(rows_x, rows_y, Z_CUTS)
    along_y = jnp.einsum("xyc,yb->xbc", along_z, map_y, precision=highest)
    along_x = jnp.einsum("xbc,xa->abc", along_y, map_x, precision=highest)
    return along_x.reshape(-1)


def prolong(correction, maps, extent):
    map_x, map_y, map_z = maps
    boxes = correction.reshape(XY_CUTS, XY_CUTS, Z_CUTS)
    over_x = jnp.einsum("abc,xa->xbc", boxes, map_x, precision=highest)
    over_y = jnp.einsum("xbc,yb->xyc", over_x, map_y, precision=highest)
    spread = jnp.dot(over_y.reshape(extent[0] * extent[1], Z_CUTS), map_z.T, precision=highest)
    return spread.reshape(extent)


def general_body(
    sources,
    diagonal,
    coarse_ids,
    coarse_inverse,
    omega_rows,
    psi,
    phi,
    xi_cols,
    range_sketch,
    core_sketch,
):
    source = sources[0]
    rows_x, rows_y, cells_z = source.shape
    coarse = coarse_inverse.shape[0]
    total_cells = rows_x * lax.axis_size("gx") * rows_y * lax.axis_size("gy") * cells_z
    scale_factor = coarse / total_cells
    maps = axis_maps(coarse_ids)
    stacked = jnp.stack([source, diagonal])
    margin = with_halo(stacked, (("gx", 1), ("gy", 2)), 2)
    place_x = lax.axis_index("gx") * rows_x + jnp.arange(rows_x + 4) - 2
    place_y = lax.axis_index("gy") * rows_y + jnp.arange(rows_y + 4) - 2
    inside_x = ((place_x >= 0) & (place_x < rows_x * lax.axis_size("gx"))).astype(jnp.float32)
    inside_y = ((place_y >= 0) & (place_y < rows_y * lax.axis_size("gy"))).astype(jnp.float32)
    inside = inside_x[:, None, None] * inside_y[None, :, None]
    pressure = jnp.zeros_like(source)
    for outer_step in range(OUTER):
        if outer_step == 0:
            residual = source
        else:
            residual = source - neighbour_image(widen_faces(pressure), diagonal)[1]
        coarse_rhs = lax.psum(restrict_cells(residual, maps), ("gx", "gy"))
        correction = jnp.dot(coarse_inverse, coarse_rhs * scale_factor, precision=highest)
        pressure = pressure + prolong(correction, maps, source.shape)
        for _ in range(SWEEPS // 2):
            widened = with_halo(pressure, (("gx", 0), ("gy", 1)), 2)
            halfway = (
                smooth_once(widened, margin[0, 1:-1, 1:-1], margin[1, 1:-1, 1:-1])
                * inside[1:-1, 1:-1]
            )
            pressure = smooth_once(halfway, source, diagonal)
    snapshot = lax.all_to_all(pressure[None], "grp", split_axis=3, concat_axis=0, tiled=True)
    columns = snapshot.reshape(snapshot.shape[0], -1)
    range_flat = range_sketch.reshape(range_sketch.shape[0], -1)
    range_new = range_flat + jnp.einsum("tk,tc->kc", omega_rows, columns, precision=highest)
    corange_part = jnp.einsum(
        "lc,tc->lt", psi.reshape(psi.shape[0], -1), columns, precision=highest
    )
    core_part = jnp.einsum("sc,tc->st", phi.reshape(phi.shape[0], -1), columns, precision=highest)
    corange_cols, core_images = lax.psum((corange_part, core_part), ("grp", "gx", "gy"))
    core_new = core_sketch + jnp.dot(core_images, xi_cols.T, precision=highest)
    return (range_new.reshape(range_sketch.shape), corange_cols, core_new)


def body(*arrays):
    _, rows_y, cells_z = arrays[1].shape
    coarse, groups = arrays[3].shape[0], lax.axis_size("grp")
    fits = (
        lax.axis_size("gx") == 2
        and lax.axis_size("gy") & (lax.axis_size("gy") - 1) == 0
        and lax.axis_size("gy") > 1
        and rows_y >= OUTER * SWEEPS
        and OUTER == 2
        and rows_y == SUBLANES
        and coarse == XY_CUTS * XY_CUTS * Z_CUTS
        and groups & (groups - 1) == 0
        and 1 < groups <= SUBLANES
        and cells_z % (groups * LANES) == 0
        and cells_z // groups == LANES
        and coarse % LANES == 0
        and arrays[5].shape[0] % SUBLANES == 0
        and arrays[6].shape[0] % SUBLANES == 0
        and arrays[5].shape[0] + arrays[6].shape[0] <= LANES
    )
    if not fits:
        return general_body(*arrays)
    return fast_body(*arrays)


def solution(mesh):
    return jax.shard_map(
        body,
        mesh=mesh,
        in_specs=(
            P("grp", "gx", "gy", None),
            P("gx", "gy", None),
            P("gx", "gy", None),
            P(),
            P(),
            P(None, "gx", "gy", "grp"),
            P(None, "gx", "gy", "grp"),
            P(),
            P(None, "gx", "gy", "grp"),
            P(),
        ),
        out_specs=(P(None, "gx", "gy", "grp"), P(), P()),
        check_vma=False,
    )
```

```python
import functools

import jax
import jax.numpy as jnp
from jax import lax
from jax.experimental import pallas as pl
from jax.experimental.pallas import tpu as pltpu
from jax.sharding import PartitionSpec as P


OUTER = 2
SWEEPS = 4
XY_CUTS = 4
Z_CUTS = 16
XY_BITS = XY_CUTS.bit_length() - 1
Z_BITS = Z_CUTS.bit_length() - 1
LANES = 128
SUBLANES = 8
VMEM_BYTES = 16 * 2**20

jacobi_weight = 2.0 / 3.0
highest = lax.Precision.HIGHEST


def dot_nt(a, b):
    return lax.dot_general(
        a, b, (((1,), (1,)), ((), ())), precision=highest, preferred_element_type=jnp.float32
    )


def dot_tn(a, b):
    return lax.dot_general(
        a, b, (((0,), (0,)), ((), ())), precision=highest, preferred_element_type=jnp.float32
    )


def iota(shape, dim):
    return lax.broadcasted_iota(jnp.int32, shape, dim)


def store_copies(out_ref, rows):
    for copy in range(out_ref.shape[0]):
        for at, row in enumerate(rows):
            out_ref[copy, at : at + 1, :] = row


def box_of(ids_ref, at):
    return lax.shift_right_logical(ids_ref[at, :, :LANES], Z_BITS)


def restrict(values, ids_ref, planes, coarse):
    cells_z = values.shape[1]
    rows_y = ids_ref.shape[1]
    ranks = lax.bitwise_and(ids_ref[0, 0:1, :], Z_CUTS - 1)
    members = lax.bitwise_and(iota((LANES, cells_z), 0), Z_CUTS - 1) == ranks
    sums = dot_nt(values, members.astype(jnp.float32))
    lane_box = lax.shift_right_logical(iota((rows_y, LANES), 1), Z_BITS)
    rows = []
    for part in range(coarse // LANES):
        total = None
        for at, plane in enumerate(planes):
            own = box_of(ids_ref, plane) == lane_box + part * (LANES // Z_CUTS)
            kept = jnp.where(own, sums[at * rows_y : (at + 1) * rows_y], 0.0)
            total = kept if total is None else total + kept
        rows.append(jnp.sum(total, axis=0, keepdims=True))
    return rows


def begin_kernel(
    source_from, diagonal_from, ids_from, inverse_from,
    mine_ref, ids_ref, inverse_ref, out_ref, arrived,
):
    loads = [
        pltpu.make_async_copy(source, target, arrived.at[at])
        for at, (source, target) in enumerate(
            (
                (ids_from, ids_ref),
                (source_from, mine_ref.at[0]),
                (diagonal_from, mine_ref.at[1]),
                (inverse_from, inverse_ref),
            )
        )
    ]
    for load in loads:
        load.start()
    coarse = inverse_ref.shape[0]
    rows_x, rows_y, cells_z = ids_ref.shape
    loads[0].wait()
    lanes = iota((1, LANES), 1)
    boxes = [box_of(ids_ref, at) for at in range(rows_x)]
    below_x = jnp.zeros((1, LANES), jnp.float32)
    for box in boxes:
        below_x = below_x + (lax.shift_right_logical(box[0:1], XY_BITS) <= lanes).astype(jnp.float32)
    ranks_y = lax.bitwise_and(boxes[0], XY_CUTS - 1)
    below_y = jnp.sum((ranks_y <= lanes - XY_CUTS).astype(jnp.float32), axis=0, keepdims=True)
    loads[1].wait()
    rows = restrict(
        mine_ref[0].reshape(rows_x * rows_y, cells_z), ids_ref, range(rows_x), coarse
    ) + [jnp.where(lanes < XY_CUTS, below_x, below_y)]
    for at, part in enumerate(rows):
        out_ref[at : at + 1, :] = part
    loads[2].wait()
    loads[3].wait()


def coarse_planes(rows, inverse_ref, ids_ref, scale_factor, cut_y, place):
    coarse = inverse_ref.shape[0]
    cells_z = ids_ref.shape[2]
    per_part = LANES // Z_CUTS
    row = jnp.broadcast_to(jnp.concatenate(rows, axis=1) * scale_factor, (SUBLANES, coarse))
    solved = dot_nt(row, inverse_ref[...])
    shape = (per_part, LANES)
    own = lax.shift_right_logical(iota(shape, 1), Z_BITS) == iota(shape, 0)
    lines = []
    for part in range(coarse // LANES):
        values = jnp.where(own, solved[:per_part, part * LANES : (part + 1) * LANES], 0.0)
        shift = LANES // 2
        while shift >= Z_CUTS:
            values = values + pltpu.roll(values, shift, 1)
            shift //= 2
        along_z = jnp.concatenate(
            [
                jnp.take_along_axis(
                    values,
                    lax.bitwise_and(ids_ref[0, :per_part, at : at + LANES], Z_CUTS - 1),
                    axis=1,
                )
                for at in range(0, cells_z, LANES)
            ],
            axis=1,
        )
        lines.extend(along_z[at : at + 1] for at in range(per_part))
    place_y, inside = place
    planes = []
    for box_x in range(XY_CUTS):
        first = box_x * XY_CUTS
        plane = jnp.broadcast_to(lines[first], place_y.shape)
        for box_y in range(1, XY_CUTS):
            plane = jnp.where(place_y >= cut_y[box_y - 1], lines[first + box_y], plane)
        planes.append(jnp.where(inside, plane, 0.0))
    return planes


def correction_of(planes, cut_x, place_x):
    value = planes[0]
    for box_x in range(1, XY_CUTS):
        value = jnp.where(cut_x[box_x - 1] <= place_x, planes[box_x], value)
    return value


def cuts_of(row, count_x, count_y):
    cut_x = [row[:, at : at + 1] * (1.0 / count_y) for at in range(XY_CUTS - 1)]
    cut_y = [row[:, XY_CUTS + at : XY_CUTS + at + 1] * (1.0 / count_x) for at in range(XY_CUTS - 1)]
    return cut_x, cut_y


def beside_z(values):
    lanes = iota((values.shape[0], LANES), 1)
    tiles = [values[:, at : at + LANES] for at in range(0, values.shape[1], LANES)]
    empty = jnp.zeros_like(tiles[0])
    ahead = [pltpu.roll(tile, LANES - 1, 1) for tile in tiles] + [empty]
    behind = [empty] + [pltpu.roll(tile, 1, 1) for tile in tiles]
    return jnp.concatenate(
        [
            jnp.where(lanes == LANES - 1, ahead[at + 1], ahead[at])
            + jnp.where(lanes == 0, behind[at], behind[at + 1])
            for at in range(len(tiles))
        ],
        axis=1,
    )


def beside_y(values):
    rows = values.shape[0]
    return pltpu.roll(values, rows - 1, 0) + pltpu.roll(values, 1, 0)


def neighbours(field_ref, at, rows=None):
    center = field_ref[at + 1]
    along_y = beside_y(center)
    if rows is None:
        rows = slice(0, center.shape[0])
    center = center[rows]
    across = field_ref[at, rows, :] + field_ref[at + 2, rows, :]
    return center, across + along_y[rows] + beside_z(center)


def smooth(field_ref, weight_ref, drive_ref, at, rows=None):
    center, beside = neighbours(field_ref, at, rows)
    rows = slice(None) if rows is None else rows
    kept = center * (1.0 - jacobi_weight) + drive_ref[at, rows, :]
    return kept + weight_ref[at, rows, :] * beside


def sweep(from_ref, to_ref, weight_ref, drive_ref, rows_x, reach):
    window_x, window_y, _ = weight_ref.shape
    own_rows = slice(window_y // 3, 2 * window_y // 3)
    for at in range(window_x):
        away = max(0, at - rows_x + 1)
        if away > reach:
            continue
        if away == reach:
            to_ref[at + 1, own_rows, :] = smooth(from_ref, weight_ref, drive_ref, at, own_rows)
        else:
            to_ref[at + 1] = smooth(from_ref, weight_ref, drive_ref, at)


def window_place(count_y, rows_y, shape):
    place_y = iota(shape, 0) + (lax.axis_index("gy") - 1) * rows_y
    inside = (place_y >= 0) & (place_y < rows_y * count_y)
    return place_y.astype(jnp.float32), inside


def mirrored(at, last):
    return jnp.where(lax.axis_index("gx") == 0, at, last - at)


def add_correction(planes, cut_x, window_x, planes_used, from_ref, to_ref):
    for at in range(planes_used):
        place_x = mirrored(at, window_x - 1).astype(jnp.float32)
        value = correction_of(planes, cut_x, place_x)
        to_ref[at + 1] = value if from_ref is None else from_ref[at + 1] + value


def clear_ends(field_ref, window_x):
    empty = jnp.zeros(field_ref.shape[1:], jnp.float32)
    field_ref[0] = empty
    field_ref[window_x + 1] = empty


def fill(blocks, weight_ref, drive_ref):
    for ref, first, row, scale in blocks:
        _, rows_x, rows_y, _ = ref.shape
        for at in range(rows_x):
            plane = mirrored(at, rows_x - 1)
            weight = scale / (6.0 + ref[1, plane])
            weight_ref[first + at, pl.ds(row, rows_y), :] = weight
            drive_ref[first + at, pl.ds(row, rows_y), :] = weight * ref[0, plane]


def pair_places(count_y, rows_y):
    at_y = lax.axis_index("gy")
    parity = lax.rem(at_y, 2)
    even_row = pl.multiple_of((1 - parity) * 2 * rows_y, SUBLANES)
    odd_row = pl.multiple_of(parity * 2 * rows_y, SUBLANES)
    odd_inside = jnp.where((at_y > 0) & (at_y < count_y - 1), jacobi_weight, 0.0)
    return even_row, odd_row, odd_inside


def prepare_kernel(count_y, own_ref, other_ref, even_ref, odd_ref, weight_ref, drive_ref):
    _, rows_x, rows_y, _ = own_ref.shape
    even_row, odd_row, odd_inside = pair_places(count_y, rows_y)
    blocks = (
        (own_ref, 0, rows_y, jacobi_weight),
        (other_ref, rows_x, rows_y, jacobi_weight),
        (even_ref, 0, even_row, jacobi_weight),
        (odd_ref, 0, odd_row, odd_inside),
    )
    fill(blocks, weight_ref, drive_ref)


def first_kernel(
    counts, scale_factor, own_ref, even_other_ref, odd_other_ref, ids_ref, inverse_ref,
    gathered_ref, weight_from, drive_from,
    field_ref, weight_ref, drive_ref, out_ref, spare_ref,
):
    count_x, count_y = counts
    _, rows_x, rows_y, cells_z = own_ref.shape
    window_x, window_y, _ = weight_ref.shape
    even_row, odd_row, odd_inside = pair_places(count_y, rows_y)
    blocks = (
        (even_other_ref, rows_x, even_row, jacobi_weight),
        (odd_other_ref, rows_x, odd_row, odd_inside),
    )
    weight_ref[...] = weight_from[...]
    drive_ref[...] = drive_from[...]
    fill(blocks, weight_ref, drive_ref)

    parts = inverse_ref.shape[0] // LANES
    rows = [gathered_ref[at : at + 1] for at in range(parts + 1)]
    cut_x, cut_y = cuts_of(rows[parts], count_x, count_y)
    place = window_place(count_y, rows_y, (window_y, cells_z))
    planes = coarse_planes(rows[:parts], inverse_ref, ids_ref, scale_factor, cut_y, place)
    clear_ends(field_ref, window_x)
    clear_ends(spare_ref, window_x)
    add_correction(planes, cut_x, window_x, window_x, None, field_ref)
    for step in range(SWEEPS):
        refs = (field_ref, spare_ref) if step % 2 == 0 else (spare_ref, field_ref)
        sweep(*refs, weight_ref, drive_ref, rows_x, 2 * SWEEPS - 1 - step)

    residual, used = [], []
    own_rows = slice(rows_y, 2 * rows_y)
    for at in range(rows_x):
        plane = mirrored(at, rows_x - 1)
        center, beside = neighbours(field_ref, at, own_rows)
        residual.append(own_ref[0, plane] - ((6.0 + own_ref[1, plane]) * center - beside))
        used.append(plane)
    partial = restrict(jnp.concatenate(residual, axis=0), ids_ref, used, inverse_ref.shape[0])
    store_copies(out_ref, partial + rows[parts:])


def second_kernel(
    counts, scale_factor, pieces,
    field_ref, weight_ref, drive_ref, ids_ref, inverse_ref, gathered_ref, *rest,
):
    out_refs, (one_ref, two_ref) = rest[:pieces], rest[pieces:]
    count_x, count_y = counts
    window_x, window_y, cells_z = weight_ref.shape
    rows_x, rows_y, chunk = out_refs[0].shape
    parts = inverse_ref.shape[0] // LANES
    gathered = jnp.sum(gathered_ref[...], axis=0)
    rows = [gathered[at : at + 1] for at in range(parts)]
    cut_x, cut_y = cuts_of(gathered_ref[0, parts : parts + 1], count_x, count_y)
    place = window_place(count_y, rows_y, (window_y, cells_z))
    planes = coarse_planes(rows, inverse_ref, ids_ref, scale_factor, cut_y, place)
    clear_ends(one_ref, window_x)
    clear_ends(two_ref, window_x)
    used = min(window_x, rows_x + SWEEPS)
    add_correction(planes, cut_x, window_x, used, field_ref, one_ref)
    fields = [one_ref, two_ref]
    for step in range(SWEEPS - 1):
        sweep(*fields, weight_ref, drive_ref, rows_x, SWEEPS - 1 - step)
        fields.reverse()
    last_ref, own_ref = fields
    own_rows = slice(rows_y, 2 * rows_y)
    for at in range(rows_x):
        value = smooth(last_ref, weight_ref, drive_ref, at, own_rows)
        own_ref[mirrored(at, rows_x - 1), pl.ds(0, rows_y), :] = value
    me = lax.axis_index("grp")
    for turn in range(pieces):
        first = pl.multiple_of(lax.bitwise_xor(me, turn) * chunk, LANES)
        for at in range(rows_x):
            out_refs[turn][at] = own_ref[at, pl.ds(0, rows_y), pl.ds(first, chunk)]


def range_kernel(pieces, omega_ref, range_ref, *rest):
    snaps, (new_ref,) = rest[:pieces], rest[pieces:]
    rows_x = range_ref.shape[1]
    me = lax.axis_index("grp")
    slots = [lax.bitwise_xor(me, turn) for turn in range(pieces)]
    cells = [[snaps[turn][at] for at in range(rows_x)] for turn in range(pieces)]
    for at_row in range(range_ref.shape[0]):
        scales = [omega_ref[slots[turn], at_row] for turn in range(pieces)]
        for at in range(rows_x):
            value = range_ref[at_row, at]
            for turn in range(pieces):
                value = value + scales[turn] * cells[turn][at]
            new_ref[at_row, at] = value


def sum_rows(values):
    sublanes = iota(values[0].shape, 0)
    shift = SUBLANES // 2
    while shift:
        low = lax.bitwise_and(sublanes, shift) == 0
        half = len(values) // 2
        values = [
            jnp.where(
                low,
                values[at] + pltpu.roll(values[at], SUBLANES - shift, 0),
                values[at + half] + pltpu.roll(values[at + half], shift, 0),
            )
            for at in range(half)
        ]
        shift //= 2
    return values[0]


def products(psi_ref, phi_ref, snaps):
    rows_x = psi_ref.shape[1]
    cells = [[snap[at] for at in range(rows_x)] for snap in snaps]
    kept = [[] for _ in snaps]
    for ref in (psi_ref, phi_ref):
        for first in range(0, ref.shape[0], SUBLANES):
            totals = [[] for _ in snaps]
            for at_row in range(first, first + SUBLANES):
                parts = [ref[at_row, at] for at in range(rows_x)]
                for turn in range(len(snaps)):
                    total = parts[0] * cells[turn][0]
                    for at in range(1, rows_x):
                        total = total + parts[at] * cells[turn][at]
                    totals[turn].append(total)
            for turn in range(len(snaps)):
                kept[turn].append(sum_rows(totals[turn]))
    count = psi_ref.shape[0] + phi_ref.shape[0]
    rest = [jnp.zeros((LANES - count, LANES), jnp.float32)] if count < LANES else []
    ones = jnp.ones((SUBLANES, LANES), jnp.float32)
    return [dot_nt(ones, jnp.concatenate(rows + rest, axis=0))[0:1] for rows in kept]


def early_kernel(pieces, psi_ref, phi_ref, *rest):
    snaps, (out_ref,) = rest[:pieces], rest[pieces:]
    for at, row in enumerate(products(psi_ref, phi_ref, snaps)):
        out_ref[at : at + 1, :] = row


def late_kernel(pieces, psi_ref, phi_ref, early_ref, *rest):
    snaps, (out_ref,) = rest[:pieces], rest[pieces:]
    me = lax.axis_index("grp")
    early = early_ref.shape[0]
    rows = [early_ref[at : at + 1, :] for at in range(early)]
    rows += products(psi_ref, phi_ref, snaps)
    for turn, row in enumerate(rows):
        slot = lax.bitwise_xor(me, turn)
        for copy in range(out_ref.shape[0]):
            out_ref[copy, pl.ds(slot, 1), :] = row


def end_kernel(gathered_ref, xi_ref, core_ref, corange_out_ref, core_out_ref):
    corange = corange_out_ref.shape[1]
    core = core_ref.shape[0]
    total = jnp.sum(gathered_ref[...], axis=0)
    corange_out_ref[...] = total[:, :corange]
    images = total[:, corange : corange + core]
    core_out_ref[...] = core_ref[...] + dot_tn(images, xi_ref[...])


vmem = pl.BlockSpec(memory_space=pltpu.VMEM)
smem = pl.BlockSpec(memory_space=pltpu.SMEM)


def call(kernel, outs, inputs, scratch=(), specs=None):
    many = isinstance(outs, list)
    shapes = [jax.ShapeDtypeStruct(shape, jnp.float32) for shape in (outs if many else [outs])]
    result = pl.pallas_call(
        kernel,
        out_shape=shapes,
        in_specs=specs or [vmem] * len(inputs),
        out_specs=[vmem] * len(shapes),
        scratch_shapes=[pltpu.VMEM(shape, jnp.float32) for shape in scratch],
        compiler_params=pltpu.CompilerParams(vmem_limit_bytes=VMEM_BYTES),
    )(*inputs)
    return result if many else result[0]


def in_hbm(array):
    return pltpu.with_memory_space_constraint(array, pltpu.HBM)


def gather(copies, axes):
    return lax.all_to_all(copies, axes, 0, 0)


def fast_body(
    sources, diagonal, coarse_ids, coarse_inverse, omega_rows, psi, phi, xi_cols, range_sketch,
    core_sketch,
):
    source = sources[0]
    rows_x, rows_y, cells_z = source.shape
    counts = (lax.axis_size("gx"), lax.axis_size("gy"))
    groups = lax.axis_size("grp")
    count_x, count_y = counts
    coarse = coarse_inverse.shape[0]
    scale_factor = coarse / (rows_x * count_x * rows_y * count_y * cells_z)
    window = (rows_x * count_x, 3 * rows_y, cells_z)
    padded = (window[0] + 2,) + window[1:]
    copies = (count_x * count_y, coarse // LANES + 1, LANES)

    def place(group, x, y):
        return (group * count_x + x) * count_y + y

    def partner(group, x, y, phase):
        if phase is None:
            return place(group, x ^ 1, y)
        beyond = y ^ 1 if phase == 0 else ((y + 1) ^ 1) - 1
        return place(group, x, beyond) if 0 <= beyond < count_y else place(group ^ 1, x, y)

    def pairs(phase):
        return [
            (place(group, x, y), partner(group, x, y, phase))
            for group in range(groups)
            for x in range(count_x)
            for y in range(count_y)
        ]

    mine, ids, inverse, begin = pl.pallas_call(
        begin_kernel,
        out_shape=[
            jax.ShapeDtypeStruct((2,) + source.shape, jnp.float32),
            jax.ShapeDtypeStruct(coarse_ids.shape, jnp.int32),
            jax.ShapeDtypeStruct(coarse_inverse.shape, jnp.float32),
            jax.ShapeDtypeStruct(copies[1:], jnp.float32),
        ],
        in_specs=[pl.BlockSpec(memory_space=pltpu.HBM)] * 4,
        out_specs=[vmem] * 4,
        scratch_shapes=[pltpu.SemaphoreType.DMA((4,))],
        compiler_params=pltpu.CompilerParams(vmem_limit_bytes=VMEM_BYTES),
        name="begin",
    )(*map(in_hbm, (source, diagonal, coarse_ids, coarse_inverse)))
    others = []
    for at, phase in enumerate((None, 0, 0, 1, 1)):
        sent = others[0] if at in (2, 4) else mine
        others.append(lax.ppermute(sent, ("grp", "gx", "gy"), pairs(phase)))
    gathered = begin
    bits = [1 << bit for bit in reversed(range(count_y.bit_length() - 1))]
    turns = [("gy", count_y, bit) for bit in bits]
    turns.append(("gx", count_x, 1))
    for axis, count, bit in turns:
        gathered = gathered + lax.ppermute(gathered, axis, [(i, i ^ bit) for i in range(count)])
    prepared = call(
        functools.partial(prepare_kernel, count_y),
        [window, window],
        (mine, others[0], others[1], others[3]),
    )
    field, weight, drive, partial = call(
        functools.partial(first_kernel, counts, scale_factor),
        [padded, window, window, copies],
        (mine, others[2], others[4], ids, inverse, gathered, *prepared),
        scratch=[padded],
    )
    gathered = gather(partial, ("gx", "gy"))
    chunk = cells_z // groups
    pieces = call(
        functools.partial(second_kernel, counts, scale_factor, groups),
        [(rows_x, rows_y, chunk)] * groups,
        (field, weight, drive, ids, inverse, gathered),
        scratch=[padded, padded],
    )
    snaps = [pieces[0]] + [
        lax.ppermute(pieces[turn], "grp", [(at, at ^ turn) for at in range(groups)])
        for turn in range(1, groups)
    ]
    early = max(1, groups // 2)
    kept = call(functools.partial(early_kernel, early), (early, LANES), (psi, phi, *snaps[:early]))
    sketched = call(
        functools.partial(late_kernel, groups - early),
        (groups * count_x * count_y, groups, LANES),
        (psi, phi, kept, *snaps[early:]),
    )
    gathered = gather(sketched, ("grp", "gx", "gy"))
    range_new = call(
        functools.partial(range_kernel, groups),
        range_sketch.shape,
        (omega_rows, range_sketch, *snaps),
        specs=[smem] + [vmem] * (1 + groups),
    )
    corange_cols, core_new = call(
        end_kernel, [(groups, psi.shape[0]), core_sketch.shape], (gathered, xi_cols.T, core_sketch)
    )
    return range_new, corange_cols.T, core_new


def with_halo(cells, sides, width):
    for axis, dim in sides:
        count = lax.axis_size(axis)
        ends = count - 1
        head = lax.slice_in_dim(cells, 0, width, axis=dim)
        tail = lax.slice_in_dim(cells, cells.shape[dim] - width, cells.shape[dim], axis=dim)
        cells = jnp.concatenate(
            [
                lax.ppermute(tail, axis, [(i, (i + 1) % count) for i in range(ends)]),
                cells,
                lax.ppermute(head, axis, [((i + 1) % count, i) for i in range(ends)]),
            ],
            axis=dim,
        )
    return cells


def neighbour_image(widened, diagonal):
    center = widened[1:-1, 1:-1]
    beside = widened[2:, 1:-1] + widened[:-2, 1:-1]
    beside = beside + widened[1:-1, 2:] + widened[1:-1, :-2]
    padded = jnp.pad(center, ((0, 0), (0, 0), (1, 1)))
    beside = beside + padded[:, :, 2:] + padded[:, :, :-2]
    return (center, (6.0 + diagonal) * center - beside)


def smooth_once(widened, source, diagonal):
    center, applied = neighbour_image(widened, diagonal)
    return center + jacobi_weight * (source - applied) / (6.0 + diagonal)


def widen_faces(values):
    return with_halo(values, (("gx", 0), ("gy", 1)), 1)


def axis_maps(coarse_ids):
    ranks_x = coarse_ids[:, 0, 0] // (XY_CUTS * Z_CUTS)
    ranks_y = coarse_ids[0, :, 0] // Z_CUTS % XY_CUTS
    ranks_z = coarse_ids[0, 0, :] % Z_CUTS
    cuts_xy = jnp.arange(XY_CUTS, dtype=jnp.int32)
    cuts_z = jnp.arange(Z_CUTS, dtype=jnp.int32)
    map_x = (ranks_x[:, None] == cuts_xy[None, :]).astype(jnp.float32)
    map_y = (ranks_y[:, None] == cuts_xy[None, :]).astype(jnp.float32)
    map_z = (ranks_z[:, None] == cuts_z[None, :]).astype(jnp.float32)
    return (map_x, map_y, map_z)


def restrict_cells(values, maps):
    map_x, map_y, map_z = maps
    rows_x, rows_y, cells_z = values.shape
    along_z = jnp.dot(values.reshape(rows_x * rows_y, cells_z), map_z, precision=highest)
    along_z = along_z.reshape(rows_x, rows_y, Z_CUTS)
    along_y = jnp.einsum("xyc,yb->xbc", along_z, map_y, precision=highest)
    along_x = jnp.einsum("xbc,xa->abc", along_y, map_x, precision=highest)
    return along_x.reshape(-1)


def prolong(correction, maps, extent):
    map_x, map_y, map_z = maps
    boxes = correction.reshape(XY_CUTS, XY_CUTS, Z_CUTS)
    over_x = jnp.einsum("abc,xa->xbc", boxes, map_x, precision=highest)
    over_y = jnp.einsum("xbc,yb->xyc", over_x, map_y, precision=highest)
    spread = jnp.dot(over_y.reshape(extent[0] * extent[1], Z_CUTS), map_z.T, precision=highest)
    return spread.reshape(extent)


def general_body(
    sources,
    diagonal,
    coarse_ids,
    coarse_inverse,
    omega_rows,
    psi,
    phi,
    xi_cols,
    range_sketch,
    core_sketch,
):
    source = sources[0]
    rows_x, rows_y, cells_z = source.shape
    coarse = coarse_inverse.shape[0]
    total_cells = rows_x * lax.axis_size("gx") * rows_y * lax.axis_size("gy") * cells_z
    scale_factor = coarse / total_cells
    maps = axis_maps(coarse_ids)
    stacked = jnp.stack([source, diagonal])
    margin = with_halo(stacked, (("gx", 1), ("gy", 2)), 2)
    place_x = lax.axis_index("gx") * rows_x + jnp.arange(rows_x + 4) - 2
    place_y = lax.axis_index("gy") * rows_y + jnp.arange(rows_y + 4) - 2
    inside_x = ((place_x >= 0) & (place_x < rows_x * lax.axis_size("gx"))).astype(jnp.float32)
    inside_y = ((place_y >= 0) & (place_y < rows_y * lax.axis_size("gy"))).astype(jnp.float32)
    inside = inside_x[:, None, None] * inside_y[None, :, None]
    pressure = jnp.zeros_like(source)
    for outer_step in range(OUTER):
        if outer_step == 0:
            residual = source
        else:
            residual = source - neighbour_image(widen_faces(pressure), diagonal)[1]
        coarse_rhs = lax.psum(restrict_cells(residual, maps), ("gx", "gy"))
        correction = jnp.dot(coarse_inverse, coarse_rhs * scale_factor, precision=highest)
        pressure = pressure + prolong(correction, maps, source.shape)
        for _ in range(SWEEPS // 2):
            widened = with_halo(pressure, (("gx", 0), ("gy", 1)), 2)
            halfway = (
                smooth_once(widened, margin[0, 1:-1, 1:-1], margin[1, 1:-1, 1:-1])
                * inside[1:-1, 1:-1]
            )
            pressure = smooth_once(halfway, source, diagonal)
    snapshot = lax.all_to_all(pressure[None], "grp", split_axis=3, concat_axis=0, tiled=True)
    columns = snapshot.reshape(snapshot.shape[0], -1)
    range_flat = range_sketch.reshape(range_sketch.shape[0], -1)
    range_new = range_flat + jnp.einsum("tk,tc->kc", omega_rows, columns, precision=highest)
    corange_part = jnp.einsum(
        "lc,tc->lt", psi.reshape(psi.shape[0], -1), columns, precision=highest
    )
    core_part = jnp.einsum("sc,tc->st", phi.reshape(phi.shape[0], -1), columns, precision=highest)
    corange_cols, core_images = lax.psum((corange_part, core_part), ("grp", "gx", "gy"))
    core_new = core_sketch + jnp.dot(core_images, xi_cols.T, precision=highest)
    return (range_new.reshape(range_sketch.shape), corange_cols, core_new)


def body(*arrays):
    _, rows_y, cells_z = arrays[1].shape
    coarse, groups = arrays[3].shape[0], lax.axis_size("grp")
    fits = (
        lax.axis_size("gx") == 2
        and lax.axis_size("gy") & (lax.axis_size("gy") - 1) == 0
        and lax.axis_size("gy") > 1
        and rows_y >= OUTER * SWEEPS
        and OUTER == 2
        and rows_y == SUBLANES
        and coarse == XY_CUTS * XY_CUTS * Z_CUTS
        and groups & (groups - 1) == 0
        and 1 < groups <= SUBLANES
        and cells_z % (groups * LANES) == 0
        and cells_z // groups == LANES
        and coarse % LANES == 0
        and arrays[5].shape[0] % SUBLANES == 0
        and arrays[6].shape[0] % SUBLANES == 0
        and arrays[5].shape[0] + arrays[6].shape[0] <= LANES
    )
    if not fits:
        return general_body(*arrays)
    return fast_body(*arrays)


def solution(mesh):
    return jax.shard_map(
        body,
        mesh=mesh,
        in_specs=(
            P("grp", "gx", "gy", None),
            P("gx", "gy", None),
            P("gx", "gy", None),
            P(),
            P(),
            P(None, "gx", "gy", "grp"),
            P(None, "gx", "gy", "grp"),
            P(),
            P(None, "gx", "gy", "grp"),
            P(),
        ),
        out_specs=(P(None, "gx", "gy", "grp"), P(), P()),
        check_vma=False,
    )
```
